32 devices in a mesh: parts: 2 (over x), limb: 8 (over z, y), rot: 2 (over core).
Axes of the slice: x: 2, y: 2, z: 4, core: 2. Of those that a mesh axis runs over, the one named last changes fastest.
Arguments:
- cipher: float32 [64, 65536], P(('parts', 'limb')), parts along dimension 0, may hold values from -6 to 6
- rotation_keys: float32 [2, 4, 3, 2, 32, 65536], P('rot', None, None, None, 'limb'), may hold values from -3.5 to 3.5
- diagonals: float32 [2, 4, 32, 65536], P('rot', None, 'limb'), may hold values from -2 to 2
- shifts: int32 [2, 4], P('rot'), may hold values from 1 to 65535
- twiddles: int32 [32], replicated, may hold values from 1 to 255, as said below
- moduli: int32 [32], replicated, may hold values from 1048576 to 2097151
- digit_of: int32 [32], replicated, may hold values from 0 to 3, as said below
- conversion: float32 [32, 32], replicated, may hold values from -2 to 2
Outputs:
- product: float32 [2, 64, 65536], P(None, ('parts', 'limb'), 'rot'), parts along dimension 1
The draws below stay inside these ranges and needn't reach their ends.
There are 2 independent parts, one for each index of `parts`. The reference program is written for one: setup_inputs(seed, part) draws one part's arguments, and reference() takes and returns one part's arrays. A program takes and returns all parts, laid end to end along the dimension named above; an argument that names none is the same for every part. Nothing has to cross between parts.
Inputs may be any that keep to these rules, and one draw needn't show every extreme that they name: `digit_of`: each of the 3 digits and the special value 3 is taken by exactly 8 limbs. `twiddles`: odd.
All inputs are finite; a program needn't handle non-finite values.
Results may differ from the reference program's by a relative error of at most 0.0003.
Values sent between devices are 32-bit elements; how exact they have to be, the bound alone decides.
No kernel may reach another device: no remote copies, remote signals or barrier semaphores. Data moves between devices by JAX's collectives and lax.ppermute only.
A program may use at most 256 MiB of HBM per device.

```python
import math
import jax
import jax.numpy as jnp
from jax import lax

RADIX = 256
COEFFS = 65536
DIGITS = 3
DIGIT_LIMBS = 8
EXT = 32
KEYS = 4
GROUPS = 2


def draw_twiddles(key, part):
    return (2 * jax.random.randint(key, (EXT,), 0, RADIX // 2) + 1).astype(jnp.int32)


def draw_digit_of(key, part):
    order = jax.random.permutation(key, EXT)
    groups = jnp.arange(EXT, dtype=jnp.int32) // DIGIT_LIMBS
    return jnp.zeros((EXT,), jnp.int32).at[order].set(groups)


def touch_ends(result, rng, smallest, top_value):
    longest = result.shape.index(max(result.shape))
    spots = []
    for shift in (0, 1):
        where = [jax.random.randint(jax.random.fold_in(rng, axis), (), 0, length) for axis, length in enumerate(result.shape)]
        where[longest] = (where[longest] + shift) % result.shape[longest]
        spots.append(tuple(where))
    return result.at[spots[0]].set(smallest).at[spots[1]].set(top_value)


def levels(stream_key, shape, pieces, smallest, high):
    gain, own = 1.0, jax.random.fold_in(stream_key, 6)
    for dim, blocks in pieces:
        heights = jnp.exp(jax.random.uniform(jax.random.fold_in(own, dim), (blocks,), jnp.float32, smallest / len(pieces), high / len(pieces)))
        gain = gain * jnp.repeat(heights, shape[dim] // blocks).reshape([-1 if axis == dim else 1 for axis in range(len(shape))])
    return gain


def gaussian(stream_key, dims, deviation, bound, split=(), kind=jnp.bfloat16):
    array = deviation * jax.random.normal(stream_key, dims, jnp.float32)
    if split:
        array = array * levels(stream_key, dims, split, -0.22, 0.18)
    return jnp.clip(array, -bound, bound).astype(kind)


def setup_inputs(seed: int = 0, part: int = 0) -> dict:
    streams_of = jax.random.split(jax.random.key(seed), 9)
    own_keys = jax.random.split(jax.random.fold_in(streams_of[8], part), 9)
    return {
        "cipher": gaussian(own_keys[0], (EXT, COEFFS), 1.0, 6.0, ((0, 8),), jnp.float32),
        "rotation_keys": gaussian(streams_of[1], (GROUPS, KEYS, DIGITS, 2, EXT, COEFFS), DIGITS ** -0.5, 3.5, ((0, 2), (4, 8)), jnp.float32),
        "diagonals": gaussian(streams_of[2], (GROUPS, KEYS, EXT, COEFFS), (GROUPS * KEYS) ** -0.5, 2.0, ((0, 2), (2, 8)), jnp.float32),
        "shifts": touch_ends(jax.random.randint(streams_of[3], (GROUPS, KEYS), 1, COEFFS), jax.random.fold_in(streams_of[3], 1), 1, COEFFS - 1).astype(jnp.int32),
        "twiddles": draw_twiddles(jax.random.fold_in(streams_of[8], 71), part),
        "moduli": touch_ends(jax.random.randint(streams_of[5], (EXT,), 1048576, 2097152), jax.random.fold_in(streams_of[5], 1), 1048576, 2097151).astype(jnp.int32),
        "digit_of": draw_digit_of(jax.random.fold_in(streams_of[8], 71), part),
        "conversion": gaussian(streams_of[7], (EXT, EXT), DIGIT_LIMBS ** -0.5, 2.0, (), jnp.float32),
    }


def hartley(twist_exp):
    index_row = jnp.arange(RADIX, dtype=jnp.int32)
    product_idx = twist_exp * index_row[:, None] % RADIX * index_row[None, :] % RADIX
    angle = product_idx.astype(jnp.float32) * (2.0 * math.pi / RADIX)
    return (jnp.cos(angle) + jnp.sin(angle)) / math.sqrt(RADIX)

def transform(block, twist_exp):
    matrix = hartley(twist_exp)
    inner = jnp.dot(matrix, block, precision=lax.Precision.HIGHEST)
    return jnp.dot(inner, matrix, precision=lax.Precision.HIGHEST)

def reference(cipher, rotation_keys, diagonals, shifts, twiddles, moduli, digit_of, conversion):
    spin = jax.vmap(transform)
    spin_many = jax.vmap(spin, in_axes=(0, None))
    special = digit_of == DIGITS
    digit_ids = jnp.arange(DIGITS, dtype=jnp.int32)
    member = (digit_of[None, :] == digit_ids[:, None]).astype(jnp.float32)
    identity_mat = jnp.eye(EXT, dtype=jnp.float32)
    raise_mat = jnp.where(member[:, :, None] > 0, identity_mat[None], conversion[None]) * member[:, None, :]
    coef = spin(cipher.reshape(EXT, RADIX, RADIX), twiddles)
    raised = jnp.einsum('dml,lxy->dmxy', raise_mat, coef, precision=lax.Precision.HIGHEST)
    raised_e = spin_many(raised, twiddles).reshape(DIGITS, EXT, COEFFS)
    spec_idx = jnp.nonzero(special, size=DIGIT_LIMBS)[0].astype(jnp.int32)
    spec_twist = twiddles[spec_idx]
    lower_mat = conversion[:, spec_idx]
    moduli_f = moduli.astype(jnp.float32)
    scale_all = lax.optimization_barrier(jnp.sum(moduli_f[:, None] / moduli_f[spec_idx][None, :], axis=1)) / DIGIT_LIMBS
    carried = cipher * special[:, None].astype(jnp.float32)

    def one_rotation(total, inputs):
        amount, key_block, diag_block = inputs
        rolled = jnp.roll(raised_e, amount, axis=2)
        accum = lax.optimization_barrier(jnp.sum(rolled[:, None] * key_block, axis=0)) + jnp.roll(carried, amount, axis=1)[None]
        accum_special = accum[:, spec_idx].reshape(2, DIGIT_LIMBS, RADIX, RADIX)
        coef_special = spin_many(accum_special, spec_twist)
        mixed = jnp.einsum('qp,cpxy->cqxy', lower_mat, coef_special, precision=lax.Precision.HIGHEST)
        lowered = spin_many(mixed, twiddles).reshape(2, EXT, COEFFS)
        down = jnp.where(special[None, :, None], accum, (accum - lowered) * scale_all[None, :, None])
        return (total + diag_block[None] * down, None)
    total, _ = lax.scan(one_rotation, jnp.zeros((2, EXT, COEFFS), jnp.float32), (shifts.reshape(-1), rotation_keys.reshape(-1, DIGITS, 2, EXT, COEFFS), diagonals.reshape(-1, EXT, COEFFS)))
    return total
```

```python
import functools
import math

import jax
import jax.numpy as jnp
import numpy as np
from jax import lax
from jax.experimental import pallas as pl
from jax.experimental.pallas import tpu as pltpu
from jax.sharding import PartitionSpec as P

RADIX = 256
DIGITS = 3
LANES = 128
F32 = jnp.float32
BF16 = jnp.bfloat16


VMEM_LIMIT = 60 * 1024 * 1024
ANY = pl.BlockSpec(memory_space=pl.ANY)
SMEM = pl.BlockSpec(memory_space=pltpu.SMEM)


def ring_order(mesh):
    n = mesh.shape["limb"]
    line = np.moveaxis(mesh.devices, list(mesh.axis_names).index("limb"), 0).reshape(n, -1)[:, 0]
    at = [getattr(d, "coords", None) for d in line]
    if any(c is None for c in at):
        return list(range(n))
    near = [
        [j for j in range(n) if sum(abs(x - y) for x, y in zip(at[i], at[j])) == 1] for i in range(n)
    ]

    def walk(path):
        if len(path) == n:
            return path if 0 in near[path[-1]] else None
        for j in near[path[-1]]:
            if j not in path:
                found = walk(path + [j])
                if found:
                    return found
        return None

    return walk([0]) or list(range(n))


def split(x):
    hi = x.astype(BF16)
    return hi, (x - hi.astype(F32)).astype(BF16)


def mm(a, b):
    dot = functools.partial(jnp.dot, preferred_element_type=F32)
    return dot(a[0], b[0]) + dot(a[1], b[0]) + dot(a[0], b[1])


def spin(x, h):
    return mm(h, split(mm(split(x), h)))


def grid_of(ref, m, limbs):
    left = ref[pl.ds(m, RADIX, stride=2 * limbs), :]
    right = ref[pl.ds(limbs + m, RADIX, stride=2 * limbs), :]
    return jnp.concatenate([left, right], axis=1)


def params(**kw):
    return pltpu.CompilerParams(vmem_limit_bytes=VMEM_LIMIT, **kw)


def coef_kernel(tw, where, base_hi, base_lo, cipher, coef, mats):
    m = pl.program_id(0)
    limbs = pl.num_programs(0)
    g = tw[where[0] * limbs + m]
    row = lax.broadcasted_iota(jnp.int32, (RADIX, RADIX), 0)
    col = lax.broadcasted_iota(jnp.int32, (RADIX, RADIX), 1)
    pick = jnp.where(((row * g) & (RADIX - 1)) == col, 1.0, 0.0).astype(BF16)
    hi = jnp.dot(pick, base_hi[...], preferred_element_type=F32).astype(BF16)
    lo = jnp.dot(pick, base_lo[...], preferred_element_type=F32).astype(BF16)
    mats[0, 0] = hi
    mats[0, 1] = lo
    x = grid_of(cipher, m, limbs)
    u = split(mm((hi, lo), split(x)))
    first = where[1] == 0
    half = tuple(jnp.where(first, h[:, :LANES].astype(F32), h[:, LANES:].astype(F32)).astype(BF16) for h in (hi, lo))
    coef[0] = mm(u, half)


def coef_call(tw, where, base_hi, base_lo, cipher, limbs):
    whole = lambda a: pl.BlockSpec(a.shape, lambda m, *_: (0,) * a.ndim)
    return pl.pallas_call(
        coef_kernel,
        grid_spec=pltpu.PrefetchScalarGridSpec(
            num_scalar_prefetch=2,
            grid=(limbs,),
            in_specs=[whole(base_hi), whole(base_lo), whole(cipher)],
            out_specs=[
                pl.BlockSpec((1, RADIX, LANES), lambda m, *_: (m, 0, 0)),
                pl.BlockSpec((1, 2, RADIX, RADIX), lambda m, *_: (m, 0, 0, 0)),
            ],
        ),
        out_shape=[
            jax.ShapeDtypeStruct((limbs, RADIX, LANES), F32),
            jax.ShapeDtypeStruct((limbs, 2, RADIX, RADIX), BF16),
        ],
        compiler_params=params(),
        name="coef",
    )(tw, where, base_hi, base_lo, cipher)


def mix_kernel(n, limbs, lens, order, digit, where, srcs, conv, *refs):
    blocks, out, got, table, sem = refs[: len(lens)], refs[-4], refs[-3], refs[-2], refs[-1]
    size = got.shape[0] * limbs // (DIGITS + 1)
    copies = []
    for i, (start, stop) in enumerate(lens):
        c = pltpu.make_async_copy(blocks[i], got.at[srcs[i], pl.ds(start, stop - start)], sem.at[i])
        c.start()
        copies.append(c)
    first = where[0] * limbs
    for j in range(DIGITS * size):
        l = order[j]
        for m in range(limbs):
            same = digit[l] == digit[first + m]
            one = jnp.where(first + m == l, 1.0, 0.0)
            table[m, j] = jnp.where(same, one, conv[first + m, l])
    for c in copies:
        c.wait()
    step = 64

    def rows(r, carry):
        r0 = pl.multiple_of(r * step, step)
        for d in range(DIGITS):
            acc = [jnp.zeros((step, LANES), F32) for _ in range(limbs)]
            for j in range(size):
                l = order[d * size + j]
                x = got[l // limbs, l % limbs, pl.ds(r0, step), :]
                for m in range(limbs):
                    acc[m] = acc[m] + table[m, d * size + j] * x
            for m in range(limbs):
                out[d, m, pl.ds(r0, step), :] = acc[m]
        return carry

    lax.fori_loop(0, RADIX // step, rows, 0)


def mix_call(n, limbs, lens, order, digit, where, srcs, conv, blocks):
    vmem = pl.BlockSpec(memory_space=pltpu.VMEM)
    return pl.pallas_call(
        functools.partial(mix_kernel, n, limbs, lens),
        in_specs=[SMEM] * 5 + [ANY] * len(blocks),
        out_specs=vmem,
        out_shape=jax.ShapeDtypeStruct((DIGITS, limbs, RADIX, LANES), F32),
        scratch_shapes=[
            pltpu.VMEM((n, limbs, RADIX, LANES), F32),
            pltpu.SMEM((limbs, n * limbs), F32),
            pltpu.SemaphoreType.DMA((len(blocks),)),
        ],
        compiler_params=params(),
        name="mix",
    )(order, digit, where, srcs, conv, *blocks)


def raise_kernel(digit, where, own, other, mats, cipher, out):
    d, m = pl.program_id(0), pl.program_id(1)
    limbs = pl.num_programs(1)
    same = digit[where[0] * limbs + m] == d

    @pl.when(same)
    def _():
        for h in range(2):
            at = pl.ds(h * limbs + m, RADIX, stride=2 * limbs)
            out[0, at, :] = cipher[at, :]

    @pl.when(jnp.logical_not(same))
    def _():
        first = where[1] == 0
        a, b = own[0, 0], other[0, 0]
        x = jnp.concatenate([jnp.where(first, a, b), jnp.where(first, b, a)], axis=1)
        y = spin(x, (mats[0, 0], mats[0, 1]))
        for h in range(2):
            out[0, pl.ds(h * limbs + m, RADIX, stride=2 * limbs), :] = y[:, h * LANES : (h + 1) * LANES]


def raise_call(digit, where, own, other, mats, cipher):
    limbs = mats.shape[0]
    rows = cipher.shape[0]
    piece = pl.BlockSpec((1, 1, RADIX, LANES), lambda d, m, *_: (d, m, 0, 0))
    return pl.pallas_call(
        raise_kernel,
        grid_spec=pltpu.PrefetchScalarGridSpec(
            num_scalar_prefetch=2,
            grid=(DIGITS, limbs),
            in_specs=[
                piece,
                piece,
                pl.BlockSpec((1, 2, RADIX, RADIX), lambda d, m, *_: (m, 0, 0, 0)),
                pl.BlockSpec((rows, LANES), lambda d, m, *_: (0, 0)),
            ],
            out_specs=pl.BlockSpec((1, rows, LANES), lambda d, m, *_: (d, 0, 0)),
        ),
        out_shape=jax.ShapeDtypeStruct((DIGITS, rows, LANES), F32),
        compiler_params=params(),
        name="raise",
    )(digit, where, own, other, mats, cipher)


def accum_kernel(shifts, slot, raised, cipher, keys, diag, mats, gain, mask, part, out0, out1, rolled, acc):
    k, m = pl.program_id(0), pl.program_id(1)
    limbs = pl.num_programs(1)
    rows = cipher.shape[0]

    @pl.when(m == 0)
    def _():
        s = shifts[k]
        tiles, lane = s // LANES, s % LANES
        step = 256
        keep = jnp.concatenate([mask[...]] * (step // 8), axis=0)

        def turn(r, carry):
            r0 = pl.multiple_of(r * step, step)
            for g in range(DIGITS + 1):
                x = raised[g, pl.ds(r0, step), :] if g < DIGITS else cipher[pl.ds(r0, step), :] * keep
                y = pltpu.roll(x, lane, axis=1)
                rolled[g, pl.ds(r0, step), :] = y
                rolled[g, pl.ds(rows + r0, step), :] = y
            return carry

        lax.fori_loop(0, rows // step, turn, 0)
        part_step = 64
        here = lax.broadcasted_iota(jnp.int32, (part_step, LANES), 1) >= lane
        g8 = jnp.concatenate([gain[...]] * (part_step // 8), axis=0)
        base = rows - limbs * tiles

        def add(r, carry):
            r0 = pl.multiple_of(r * part_step, part_step)
            turned = []
            for g in range(DIGITS + 1):
                u = rolled[g, pl.ds(pl.multiple_of(base + r0, limbs), part_step), :]
                v = rolled[g, pl.ds(pl.multiple_of(base - limbs + r0, limbs), part_step), :]
                turned.append(jnp.where(here, u, v))
            w = diag[0, pl.ds(r0, part_step), :] * g8
            for c in range(2):
                a = turned[DIGITS]
                for d in range(DIGITS):
                    a = a + turned[d] * keys[0, 2 * d + c, pl.ds(r0, part_step), :]
                acc[c, pl.ds(r0, part_step), :] = a
                before = jnp.where(k == 0, 0.0, part[c, pl.ds(r0, part_step), :])
                part[c, pl.ds(r0, part_step), :] = before + w * a
            return carry

        lax.fori_loop(0, rows // part_step, add, 0)

    @pl.when(slot[m] >= 0)
    def _():
        h = (mats[0, 0], mats[0, 1])
        for c, out in ((0, out0), (1, out1)):
            y = spin(grid_of(acc.at[c], m, limbs), h)
            out[0, 0:RADIX, :] = y[:, :LANES]
            out[0, RADIX:, :] = y[:, LANES:]


def accum_call(shifts, slot, raised, cipher, keys, diag, mats, gain, mask, specials):
    limbs = mats.shape[0]
    rows = cipher.shape[0]
    count = keys.shape[0]
    items = count * specials
    whole = lambda a: pl.BlockSpec(a.shape, lambda k, m, *_: (0,) * a.ndim)
    at = lambda k, m, shifts, slot: (jnp.where(slot[m] >= 0, k * specials + slot[m], items), 0, 0)
    item = pl.BlockSpec((1, 2 * RADIX, LANES), at)
    return pl.pallas_call(
        accum_kernel,
        grid_spec=pltpu.PrefetchScalarGridSpec(
            num_scalar_prefetch=2,
            grid=(count, limbs),
            in_specs=[
                whole(raised),
                whole(cipher),
                pl.BlockSpec((1,) + keys.shape[1:], lambda k, m, *_: (k, 0, 0, 0)),
                pl.BlockSpec((1, rows, LANES), lambda k, m, *_: (k, 0, 0)),
                pl.BlockSpec((1, 2, RADIX, RADIX), lambda k, m, *_: (m, 0, 0, 0)),
                whole(gain),
                whole(mask),
            ],
            out_specs=[pl.BlockSpec((2, rows, LANES), lambda k, m, *_: (0, 0, 0)), item, item],
            scratch_shapes=[
                pltpu.VMEM((DIGITS + 1, 2 * rows, LANES), F32),
                pltpu.VMEM((2, rows, LANES), F32),
            ],
        ),
        out_shape=[jax.ShapeDtypeStruct((2, rows, LANES), F32)]
        + [jax.ShapeDtypeStruct((items + 1, 2 * RADIX, LANES), F32)] * 2,
        compiler_params=params(),
        name="accum",
    )(shifts, slot, raised, cipher, keys, diag, mats, gain, mask)


def table_kernel(n, items, specials, limbs, order, pos, table, rounds, a_ref, b_ref):
    shape = (items, LANES)
    row_i = lax.broadcasted_iota(jnp.int32, shape, 0)
    row = row_i.astype(F32)
    lane = lax.broadcasted_iota(jnp.int32, shape, 1).astype(F32)
    kind = lax.rem(row_i, specials)
    org = jnp.zeros(shape, F32)
    for s in range(specials):
        owner = pos[lax.div(order[DIGITS * specials + s], limbs)]
        org = jnp.where(kind == s, owner.astype(F32), org)
    a_ref[...] = jnp.zeros(shape, F32)
    b_ref[...] = jnp.zeros(shape, F32)
    big = float(items * 2 * n + items)

    def choose(front, spread):
        cand = jnp.logical_and(spread < n - 1, front == lane)
        key = jnp.where(cand, spread * items + row, big)
        best = jnp.min(key, axis=0, keepdims=True)
        hit = jnp.where(jnp.logical_and(cand, key == best), 1.0, 0.0)
        item = jnp.sum(hit * (row - items), axis=0, keepdims=True) + items
        return item.astype(jnp.int32), jnp.sum(hit, axis=1, keepdims=True)

    def cond(c):
        return c[1] > 0

    def body(c):
        t, _ = c
        a, b = a_ref[...], b_ref[...]
        front = org + a
        item, grown = choose(jnp.where(front >= n, front - n, front), a + b)
        table[pl.ds(2 * t, 1), :] = item
        a = a + grown
        front = org - b
        item, grown = choose(jnp.where(front < 0, front + n, front), a + b)
        table[pl.ds(2 * t + 1, 1), :] = item
        b = b + grown
        a_ref[...] = a
        b_ref[...] = b
        left = jnp.sum(n - 1 - a - b).astype(jnp.int32)
        return t + 1, left

    t, _ = lax.while_loop(cond, body, (jnp.int32(0), jnp.int32(1)))
    rounds[0] = t


def table_call(n, items, specials, limbs, order, pos):
    most = items * (n - 1)
    return pl.pallas_call(
        functools.partial(table_kernel, n, items, specials, limbs),
        in_specs=[SMEM, SMEM],
        out_specs=[pl.BlockSpec(memory_space=pltpu.VMEM), SMEM],
        out_shape=[
            jax.ShapeDtypeStruct((2 * most, LANES), jnp.int32),
            jax.ShapeDtypeStruct((1,), jnp.int32),
        ],
        scratch_shapes=[pltpu.VMEM((items, LANES), F32)] * 2,
        compiler_params=params(),
        name="table",
    )(order, pos)


def pack_kernel(n, items, first, last, table, at, *refs):
    if first:
        store, outs, rest = refs[0], refs[2:4], refs[4:]
        ins = ()
    elif last:
        store, ins, rest = refs[3], refs[1:3], refs[4:]
        outs = ()
    else:
        store, ins, outs, rest = refs[3], refs[1:3], refs[4:6], refs[6:]
    buf, sem = rest
    t, p = at[0], at[1]
    came = [items, items]
    if not first:
        back = 2 * (t - 1) * n
        came = [table[back + lax.rem(p + n - 1, n)], table[back + n + lax.rem(p + 1, n)]]
    go = [items, items]
    if not last:
        go = [table[2 * t * n + p], table[2 * t * n + n + p]]

    if not first:
        for i in range(2):
            @pl.when(came[i] < items)
            def _():
                pltpu.make_async_copy(ins[i], buf.at[i], sem.at[i]).start()

    if not last:
        fresh = [jnp.logical_and(go[i] != came[0], go[i] != came[1]) for i in range(2)]
        old = [jnp.logical_and(go[i] < items, fresh[i]) for i in range(2)]
        new = [jnp.logical_and(go[i] < items, jnp.logical_not(fresh[i])) for i in range(2)]
        for i in range(2):
            @pl.when(old[i])
            def _():
                pltpu.make_async_copy(store.at[go[i]], buf.at[2 + i], sem.at[2 + i]).start()

    if not first:
        for i in range(2):
            @pl.when(came[i] < items)
            def _():
                pltpu.make_async_copy(ins[i], buf.at[i], sem.at[i]).wait()
                pltpu.make_async_copy(buf.at[i], store.at[came[i]], sem.at[i]).start()

    if not last:
        for i in range(2):
            @pl.when(old[i])
            def _():
                pltpu.make_async_copy(store.at[go[i]], buf.at[2 + i], sem.at[2 + i]).wait()
                pltpu.make_async_copy(buf.at[2 + i], outs[i], sem.at[2 + i]).start()

            if not first:
                @pl.when(new[i])
                def _():
                    which = jnp.where(go[i] == came[0], 0, 1)
                    pltpu.make_async_copy(buf.at[which], outs[i], sem.at[2 + i]).start()

        for i in range(2):
            @pl.when(go[i] < items)
            def _():
                pltpu.make_async_copy(buf.at[2 + i], outs[i], sem.at[2 + i]).wait()

    if not first:
        for i in range(2):
            @pl.when(came[i] < items)
            def _():
                pltpu.make_async_copy(buf.at[i], store.at[came[i]], sem.at[i]).wait()


def pack_call(n, items, table, at, store, ins=None, last=False):
    first = ins is None
    item = jax.ShapeDtypeStruct(store.shape[1:], store.dtype)
    args = (table, at, store) + (() if first else tuple(ins))
    outs = [jax.ShapeDtypeStruct(store.shape, store.dtype)] + ([] if last else [item, item])
    size = math.prod(item.shape) * 4
    res = pl.pallas_call(
        functools.partial(pack_kernel, n, items, first, last),
        in_specs=[SMEM, SMEM] + [ANY] * (len(args) - 2),
        out_specs=[ANY] * len(outs),
        out_shape=outs,
        input_output_aliases={2: 0},
        scratch_shapes=[
            pltpu.VMEM((4,) + item.shape, F32),
            pltpu.SemaphoreType.DMA((4,)),
        ],
        compiler_params=params(),
        cost_estimate=pl.CostEstimate(flops=0, bytes_accessed=8 * size, transcendentals=0),
        name="pack",
    )(*args)
    return res[0], list(res[1:])


def lower_kernel(order, digit, where, scale, conv, in0, in1, diag, mats, part, keep, send, total):
    k, m = pl.program_id(0), pl.program_id(1)
    limbs = pl.num_programs(1)
    specials = in0.shape[0]
    q = where[0] * limbs + m

    @pl.when(jnp.logical_and(k == 0, m == 0))
    def _():
        total[...] = part[...]

    @pl.when(digit[q] != DIGITS)
    def _():
        h = (mats[0, 0], mats[0, 1])
        w = [conv[q, order[DIGITS * specials + s]] for s in range(specials)]
        size = scale[q]
        for c, src in ((0, in0), (1, in1)):
            x = w[0] * src[0]
            for s in range(1, specials):
                x = x + w[s] * src[s]
            y = spin(jnp.concatenate([x[:RADIX], x[RADIX:]], axis=1), h)
            for i in range(2):
                at = pl.ds(i * limbs + m, RADIX, stride=2 * limbs)
                dg = diag[0, at, :] * size
                total[c, at, :] = total[c, at, :] - dg * y[:, i * LANES : (i + 1) * LANES]

    @pl.when(jnp.logical_and(k == pl.num_programs(0) - 1, m == limbs - 1))
    def _():
        half = total.shape[1] // 2
        mine = where[1]
        keep[...] = total[:, pl.ds(pl.multiple_of(mine * half, half), half), :]
        send[...] = total[:, pl.ds(pl.multiple_of((1 - mine) * half, half), half), :]


def lower_call(order, digit, where, scale, conv, store0, store1, diag, mats, part, specials):
    limbs = mats.shape[0]
    rows = part.shape[1]
    count = diag.shape[0]
    half = (2, rows // 2, LANES)
    item = pl.BlockSpec((specials, 2 * RADIX, LANES), lambda k, m: (k, 0, 0))
    out = pl.BlockSpec(half, lambda k, m: (0, 0, 0))
    return pl.pallas_call(
        lower_kernel,
        grid=(count, limbs),
        in_specs=[SMEM] * 5
        + [
            item,
            item,
            pl.BlockSpec((1, rows, LANES), lambda k, m: (k, 0, 0)),
            pl.BlockSpec((1, 2, RADIX, RADIX), lambda k, m: (m, 0, 0, 0)),
            pl.BlockSpec(part.shape, lambda k, m: (0, 0, 0)),
        ],
        out_specs=[out, out],
        out_shape=[jax.ShapeDtypeStruct(half, F32)] * 2,
        scratch_shapes=[pltpu.VMEM((2, rows, LANES), F32)],
        compiler_params=params(),
        name="lower",
    )(order, digit, where, scale, conv, store0, store1, diag, mats, part)


def interleave(x):
    *lead, limbs, coeffs = x.shape
    x = x.reshape(*lead, limbs, coeffs // LANES, LANES)
    return jnp.swapaxes(x, -3, -2).reshape(*lead, coeffs // LANES * limbs, LANES)


def per_device(order_of, cipher, rotation_keys, diagonals, shifts, twiddles, moduli, digit_of, conversion):
    n = len(order_of)
    limbs = cipher.shape[0]
    ext = digit_of.shape[0]
    specials = ext // (DIGITS + 1)
    count = rotation_keys.shape[1]
    items = count * specials
    pos_of = np.argsort(np.array(order_of)).astype(np.int32)
    cw = [(order_of[i], order_of[(i + 1) % n]) for i in range(n)]
    ccw = [(b, a) for a, b in cw]
    me, rot = lax.axis_index("limb"), lax.axis_index("rot")
    where = jnp.stack([me, rot]).astype(jnp.int32)
    pos = jnp.asarray(pos_of)
    my_pos = pos[me]
    swap = lambda x: lax.ppermute(x, "rot", [(0, 1), (1, 0)])

    grid = np.arange(RADIX)
    angle = (grid[:, None] * grid[None, :] % RADIX) * (2.0 * math.pi / RADIX)
    base = ((np.cos(angle) + np.sin(angle)) / math.sqrt(RADIX)).astype(np.float32)
    base_hi = base.astype(BF16)
    base_lo = (base - base_hi.astype(np.float32)).astype(BF16)

    rows_c = interleave(cipher)
    keys = interleave(rotation_keys).reshape(count, DIGITS * 2, -1, LANES)
    diag = interleave(diagonals).reshape(count, -1, LANES)

    coef, mats = coef_call(twiddles, where, jnp.asarray(base_hi), jnp.asarray(base_lo), rows_c, limbs)

    ids = jnp.arange(ext, dtype=jnp.int32)
    before = (digit_of[None, :] < digit_of[:, None]) | (
        (digit_of[None, :] == digit_of[:, None]) & (ids[None, :] < ids[:, None])
    )
    place = jnp.sum(before.astype(jnp.int32), axis=1)
    order = jnp.sum(jnp.where(place[None, :] == ids[:, None], ids[None, :], 0), axis=1)
    slot = lax.dynamic_slice_in_dim(jnp.maximum(place - DIGITS * specials, -1), me * limbs, limbs, 0)
    special = digit_of == DIGITS
    mod = moduli.astype(F32)
    scale = jnp.sum(jnp.where(special[None, :], mod[:, None] / mod[None, :], 0.0), axis=1) / specials
    my_special = lax.dynamic_slice_in_dim(special, me * limbs, limbs, 0)
    my_gain = jnp.where(my_special, 1.0, lax.dynamic_slice_in_dim(scale, me * limbs, limbs, 0))
    rows8 = lambda v: jnp.broadcast_to(jnp.tile(v, 8 // limbs)[:, None], (8, LANES))
    gain, mask = rows8(my_gain), rows8(my_special.astype(F32))

    blocks, lens, steps = [coef], [(0, limbs)], [0]
    right, left = coef, coef
    both = (n - 1) // 2
    for r in range(1, both + 1):
        right, left = lax.ppermute(right, "limb", cw), lax.ppermute(left, "limb", ccw)
        blocks += [right, left]
        lens += [(0, limbs)] * 2
        steps += [-r, r]
    if n % 2 == 0:
        cut = limbs // 2
        blocks += [lax.ppermute(right[:cut], "limb", cw), lax.ppermute(left[cut:], "limb", ccw)]
        lens += [(0, cut), (cut, limbs)]
        steps += [n // 2, n // 2]
    srcs = jnp.asarray(
        np.array([[order_of[(pos_of[d] + s) % n] for s in steps] for d in range(n)], np.int32)
    )[me]

    table, rounds = table_call(n, items, specials, limbs, order, pos)
    table = table[:, :n].reshape(-1)

    mixed = mix_call(n, limbs, tuple(lens), order, digit_of, where, srcs, conversion, blocks)
    raised = raise_call(digit_of, where, mixed, swap(mixed), mats, rows_c)
    part, *stores = accum_call(
        shifts.reshape(-1), slot, raised, rows_c, keys, diag, mats, gain, mask, specials
    )

    spot = lambda t: jnp.stack([jnp.asarray(t, jnp.int32), my_pos])

    def travel(sends):
        return [lax.ppermute(sends[0], "limb", cw), lax.ppermute(sends[1], "limb", ccw)]

    fixed = items * (n - 1) // (2 * n)
    streams = [(s, None) for s in stores]
    for t in range(fixed):
        for i, (store, ins) in enumerate(streams):
            store, sends = pack_call(n, items, table, spot(t), store, ins)
            streams[i] = (store, travel(sends))

    def more(state):
        return state[0] < rounds[0]

    def one(state):
        t, streams = state
        nxt = []
        for store, ins in streams:
            store, sends = pack_call(n, items, table, spot(t), store, ins)
            nxt.append((store, travel(sends)))
        return t + 1, nxt

    t, streams = lax.while_loop(more, one, (jnp.int32(fixed), streams))
    stores = [pack_call(n, items, table, spot(t), store, ins, last=True)[0] for store, ins in streams]

    keep, send = lower_call(
        order, digit_of, where, scale, conversion, stores[0], stores[1], diag, mats, part, specials
    )
    total = keep + swap(send)
    total = jnp.swapaxes(total.reshape(2, -1, limbs, LANES), 1, 2)
    return total.reshape(2, limbs, -1)


def solution(mesh):
    in_specs = (
        P(("parts", "limb"), None),
        P("rot", None, None, None, "limb", None),
        P("rot", None, "limb", None),
        P("rot", None),
        P(),
        P(),
        P(),
        P(),
    )
    out_specs = P(None, ("parts", "limb"), "rot")
    return jax.shard_map(
        functools.partial(per_device, ring_order(mesh)),
        mesh=mesh,
        in_specs=in_specs,
        out_specs=out_specs,
        check_vma=False,
    )
```

```python
import functools
import math

import jax
import jax.numpy as jnp
import numpy as np
from jax import lax
from jax.experimental import pallas as pl
from jax.experimental.pallas import tpu as pltpu
from jax.sharding import PartitionSpec as P

RADIX = 256
DIGITS = 3
LANES = 128
F32 = jnp.float32
BF16 = jnp.bfloat16


ANY = pl.BlockSpec(memory_space=pl.ANY)
VMEM = pl.BlockSpec(memory_space=pltpu.VMEM)
SMEM = pl.BlockSpec(memory_space=pltpu.SMEM)


def ring_order(mesh):
    n = mesh.shape["limb"]
    line = np.moveaxis(mesh.devices, list(mesh.axis_names).index("limb"), 0).reshape(n, -1)[:, 0]
    at = [getattr(d, "coords", None) for d in line]
    if any(c is None for c in at):
        return list(range(n))
    near = [
        [j for j in range(n) if sum(abs(x - y) for x, y in zip(at[i], at[j])) == 1] for i in range(n)
    ]

    def walk(path):
        if len(path) == n:
            return path if 0 in near[path[-1]] else None
        for j in near[path[-1]]:
            if j not in path:
                found = walk(path + [j])
                if found:
                    return found
        return None

    return walk([0]) or list(range(n))


def split(x):
    hi = x.astype(BF16)
    return hi, (x - hi.astype(F32)).astype(BF16)


def mm(a, b):
    dot = functools.partial(jnp.dot, preferred_element_type=F32)
    return dot(a[0], b[0]) + dot(a[1], b[0]) + dot(a[0], b[1])


def spin(x, h):
    return mm(h, split(mm(split(x), h)))


def grid_of(ref, m, limbs):
    left = ref[pl.ds(m, RADIX, stride=2 * limbs), :]
    right = ref[pl.ds(limbs + m, RADIX, stride=2 * limbs), :]
    return jnp.concatenate([left, right], axis=1)


def params(mib):
    return pltpu.CompilerParams(vmem_limit_bytes=mib * 2**20)


def coef_kernel(tw, where, base_hi, base_lo, cipher, coef, mats):
    m = pl.program_id(0)
    limbs = pl.num_programs(0)
    g = tw[where[0] * limbs + m]
    row = lax.broadcasted_iota(jnp.int32, (RADIX, RADIX), 0)
    col = lax.broadcasted_iota(jnp.int32, (RADIX, RADIX), 1)
    pick = jnp.where(((row * g) & (RADIX - 1)) == col, 1.0, 0.0).astype(BF16)
    hi = jnp.dot(pick, base_hi[...], preferred_element_type=F32).astype(BF16)
    lo = jnp.dot(pick, base_lo[...], preferred_element_type=F32).astype(BF16)
    mats[0, 0] = hi
    mats[0, 1] = lo
    x = grid_of(cipher, m, limbs)
    u = split(mm((hi, lo), split(x)))
    first = where[1] == 0
    half = tuple(jnp.where(first, h[:, :LANES].astype(F32), h[:, LANES:].astype(F32)).astype(BF16) for h in (hi, lo))
    coef[0] = mm(u, half)


def coef_call(tw, where, base_hi, base_lo, cipher, limbs):
    whole = lambda a: pl.BlockSpec(a.shape, lambda m, *_: (0,) * a.ndim)
    return pl.pallas_call(
        coef_kernel,
        grid_spec=pltpu.PrefetchScalarGridSpec(
            num_scalar_prefetch=2,
            grid=(limbs,),
            in_specs=[whole(base_hi), whole(base_lo), whole(cipher)],
            out_specs=[
                pl.BlockSpec((1, RADIX, LANES), lambda m, *_: (m, 0, 0)),
                pl.BlockSpec((1, 2, RADIX, RADIX), lambda m, *_: (m, 0, 0, 0)),
            ],
        ),
        out_shape=[
            jax.ShapeDtypeStruct((limbs, RADIX, LANES), F32),
            jax.ShapeDtypeStruct((limbs, 2, RADIX, RADIX), BF16),
        ],
        compiler_params=params(16),
        name="coef",
    )(tw, where, base_hi, base_lo, cipher)


def mix_kernel(n, limbs, lens, order, digit, where, srcs, conv, *refs):
    blocks, out, got, table, sem = refs[: len(lens)], refs[-4], refs[-3], refs[-2], refs[-1]
    size = got.shape[0] * limbs // (DIGITS + 1)
    copies = []
    for i, (start, stop) in enumerate(lens):
        c = pltpu.make_async_copy(blocks[i], got.at[srcs[i], pl.ds(start, stop - start)], sem.at[i])
        c.start()
        copies.append(c)
    first = where[0] * limbs
    for j in range(DIGITS * size):
        l = order[j]
        for m in range(limbs):
            same = digit[l] == digit[first + m]
            one = jnp.where(first + m == l, 1.0, 0.0)
            table[m, j] = jnp.where(same, one, conv[first + m, l])
    for c in copies:
        c.wait()
    step = 64

    def rows(r, carry):
        r0 = pl.multiple_of(r * step, step)
        for d in range(DIGITS):
            acc = [jnp.zeros((step, LANES), F32) for _ in range(limbs)]
            for j in range(size):
                l = order[d * size + j]
                x = got[l // limbs, l % limbs, pl.ds(r0, step), :]
                for m in range(limbs):
                    acc[m] = acc[m] + table[m, d * size + j] * x
            for m in range(limbs):
                out[d, m, pl.ds(r0, step), :] = acc[m]
        return carry

    lax.fori_loop(0, RADIX // step, rows, 0)


def mix_call(n, limbs, lens, order, digit, where, srcs, conv, blocks):
    vmem = pl.BlockSpec(memory_space=pltpu.VMEM)
    return pl.pallas_call(
        functools.partial(mix_kernel, n, limbs, lens),
        in_specs=[SMEM] * 5 + [ANY] * len(blocks),
        out_specs=vmem,
        out_shape=jax.ShapeDtypeStruct((DIGITS, limbs, RADIX, LANES), F32),
        scratch_shapes=[
            pltpu.VMEM((n, limbs, RADIX, LANES), F32),
            pltpu.SMEM((limbs, n * limbs), F32),
            pltpu.SemaphoreType.DMA((len(blocks),)),
        ],
        compiler_params=params(16),
        name="mix",
    )(order, digit, where, srcs, conv, *blocks)


def raise_kernel(digit, where, own, other, mats, cipher, out):
    d, m = pl.program_id(0), pl.program_id(1)
    limbs = pl.num_programs(1)
    same = digit[where[0] * limbs + m] == d

    @pl.when(same)
    def _():
        for h in range(2):
            at = pl.ds(h * limbs + m, RADIX, stride=2 * limbs)
            out[0, at, :] = cipher[at, :]

    @pl.when(jnp.logical_not(same))
    def _():
        first = where[1] == 0
        a, b = own[0, 0], other[0, 0]
        x = jnp.concatenate([jnp.where(first, a, b), jnp.where(first, b, a)], axis=1)
        y = spin(x, (mats[0, 0], mats[0, 1]))
        for h in range(2):
            out[0, pl.ds(h * limbs + m, RADIX, stride=2 * limbs), :] = y[:, h * LANES : (h + 1) * LANES]


def raise_call(digit, where, own, other, mats, cipher):
    limbs = mats.shape[0]
    rows = cipher.shape[0]
    piece = pl.BlockSpec((1, 1, RADIX, LANES), lambda d, m, *_: (d, m, 0, 0))
    return pl.pallas_call(
        raise_kernel,
        grid_spec=pltpu.PrefetchScalarGridSpec(
            num_scalar_prefetch=2,
            grid=(DIGITS, limbs),
            in_specs=[
                piece,
                piece,
                pl.BlockSpec((1, 2, RADIX, RADIX), lambda d, m, *_: (m, 0, 0, 0)),
                pl.BlockSpec((rows, LANES), lambda d, m, *_: (0, 0)),
            ],
            out_specs=pl.BlockSpec((1, rows, LANES), lambda d, m, *_: (d, 0, 0)),
        ),
        out_shape=jax.ShapeDtypeStruct((DIGITS, rows, LANES), F32),
        compiler_params=params(16),
        name="raise",
    )(digit, where, own, other, mats, cipher)


def accum_kernel(k, limbs, specials, shifts, slot, raised, cipher, keys, diag, mats, gain, mask, *refs):
    part, store, (rolled, acc, stage, sem) = refs[-7], refs[-6:-4], refs[-4:]
    rb = pl.program_id(0)
    rows, block = cipher.shape[0], acc.shape[1] // pl.num_programs(0)
    pad = rolled.shape[1] - rows
    s = shifts[k]
    tiles, lane = s // LANES, s % LANES

    @pl.when(rb == 0)
    def _():
        step = 256
        keep = jnp.concatenate([mask[...]] * (step // 8), axis=0)

        def turn(r, carry):
            r0 = pl.multiple_of(r * step, step)
            for g in range(DIGITS + 1):
                x = raised[g, pl.ds(r0, step), :] if g < DIGITS else cipher[pl.ds(r0, step), :] * keep
                rolled[g, pl.ds(r0, step), :] = pltpu.roll(x, lane, axis=1)
            return carry

        lax.fori_loop(0, rows // step, turn, 0)
        for g in range(DIGITS + 1):
            rolled[g, pl.ds(rows, pad), :] = rolled[g, pl.ds(0, pad), :]

    here = lax.broadcasted_iota(jnp.int32, (pad, LANES), 1) >= lane
    g8 = jnp.concatenate([gain[...]] * (pad // 8), axis=0)

    def add(r, carry):
        r0 = pl.multiple_of(r * pad, pad)
        at = rb * block + r0
        u0 = lax.rem(at - limbs * tiles + rows, rows)
        v0 = lax.rem(at - limbs * tiles - limbs + 2 * rows, rows)
        turned = []
        for g in range(DIGITS + 1):
            u = rolled[g, pl.ds(pl.multiple_of(u0, limbs), pad), :]
            v = rolled[g, pl.ds(pl.multiple_of(v0, limbs), pad), :]
            turned.append(jnp.where(here, u, v))
        w = diag[0, pl.ds(r0, pad), :] * g8
        for c in range(2):
            a = turned[DIGITS]
            for d in range(DIGITS):
                a = a + turned[d] * keys[0, 2 * d + c, pl.ds(r0, pad), :]
            acc[c, pl.ds(pl.multiple_of(at, pad), pad), :] = a
            w_a = w * a
            part[c, pl.ds(r0, pad), :] = w_a if k == 0 else refs[0][c, pl.ds(r0, pad), :] + w_a
        return carry

    lax.fori_loop(0, block // pad, add, 0)

    @pl.when(rb == pl.num_programs(0) - 1)
    def _():
        def emit(m, carry):
            @pl.when(slot[m] >= 0)
            def _():
                h = (mats[m, 0], mats[m, 1])
                copies = []
                for c in range(2):
                    y = spin(grid_of(acc.at[c], m, limbs), h)
                    stage[c, 0:RADIX, :] = y[:, :LANES]
                    stage[c, RADIX:, :] = y[:, LANES:]
                    copies.append(
                        pltpu.make_async_copy(stage.at[c], store[c].at[k * specials + slot[m]], sem.at[c])
                    )
                    copies[-1].start()
                for copy in copies:
                    copy.wait()

            return carry

        lax.fori_loop(0, limbs, emit, 0)


def accum_call(k, shifts, slot, raised, cipher, keys, diag, mats, gain, mask, specials, carried=None):
    limbs = mats.shape[0]
    rows = cipher.shape[0]
    items = keys.shape[0] * specials
    block, pad = rows // 8, 64
    once = lambda a: pl.BlockSpec(a.shape, lambda r: (0,) * a.ndim, pipeline_mode=pl.Buffered(1))
    piece = pl.BlockSpec((2, block, LANES), lambda r: (0, r, 0))
    store = jax.ShapeDtypeStruct((items, 2 * RADIX, LANES), F32)
    args = (shifts, slot, raised, cipher, keys, diag, mats, gain, mask)
    specs = [
        SMEM,
        SMEM,
        once(raised),
        once(cipher),
        pl.BlockSpec((1, keys.shape[1], block, LANES), lambda r: (k, 0, r, 0)),
        pl.BlockSpec((1, block, LANES), lambda r: (k, r, 0)),
        once(mats),
        once(gain),
        once(mask),
    ]
    alias = {}
    if carried is not None:
        alias = {len(args) + i: i for i in range(3)}
        args += tuple(carried)
        specs += [piece, ANY, ANY]
    return pl.pallas_call(
        functools.partial(accum_kernel, k, limbs, specials),
        grid=(rows // block,),
        in_specs=specs,
        out_specs=[piece, ANY, ANY],
        out_shape=[jax.ShapeDtypeStruct((2, rows, LANES), F32), store, store],
        input_output_aliases=alias,
        scratch_shapes=[
            pltpu.VMEM((DIGITS + 1, rows + pad, LANES), F32),
            pltpu.VMEM((2, rows, LANES), F32),
            pltpu.VMEM((2, 2 * RADIX, LANES), F32),
            pltpu.SemaphoreType.DMA((2,)),
        ],
        compiler_params=params(24),
        cost_estimate=pl.CostEstimate(flops=10**9, bytes_accessed=16 * 2**20, transcendentals=0),
        name="accum",
    )(*args)


def table_kernel(n, count, specials, limbs, least, order, pos, spot, plan, rounds, comp, a_ref, b_ref, end_ref):
    items = count * specials
    shape = (items, LANES)
    row_i = lax.broadcasted_iota(jnp.int32, shape, 0)
    row = row_i.astype(F32)
    lane = lax.broadcasted_iota(jnp.int32, shape, 1).astype(F32)
    kind, turn = lax.rem(row_i, specials), lax.div(row_i, specials)
    ready = jnp.maximum(2 * turn - 1, 0)
    weight = 3.0 * turn.astype(F32)
    p = spot[0]
    before, after = lax.rem(p + n - 1, n), lax.rem(p + 1, n)
    line = lax.broadcasted_iota(jnp.int32, (1, LANES), 1)
    org = jnp.zeros(shape, F32)
    for s in range(specials):
        owner = pos[lax.div(order[DIGITS * specials + s], limbs)]
        org = jnp.where(kind == s, owner.astype(F32), org)
    a_ref[...] = jnp.zeros(shape, F32)
    b_ref[...] = jnp.zeros(shape, F32)
    end_ref[...] = jnp.zeros(shape, F32)
    big = float(items * (2 * n + 3 * count))

    def choose(front, spread, t):
        open_ = jnp.logical_and(spread < n - 1, ready <= t)
        cand = jnp.logical_and(open_, front == lane)
        key = jnp.where(cand, (2.0 * spread + weight) * items + row, big)
        best = jnp.min(key, axis=0, keepdims=True)
        hit = jnp.where(jnp.logical_and(cand, key == best), 1.0, 0.0)
        item = jnp.sum(hit * (row - items), axis=0, keepdims=True) + items
        return item, jnp.sum(hit, axis=1, keepdims=True)

    def note(t, r, item, where):
        mine = jnp.sum(jnp.where(line == where, item, 0.0), axis=1, keepdims=True)
        plan[t, pl.ds(r, 1), :] = jnp.broadcast_to(mine, (1, LANES)).astype(jnp.int32)

    none = jnp.full((1, LANES), float(items), F32)
    note(0, 2, none, p)
    note(0, 3, none, p)

    def cond(c):
        return jnp.logical_or(c[1] > 0, c[0] < least)

    def body(c):
        t, _ = c
        a, b = a_ref[...], b_ref[...]
        front = org + a
        item, right = choose(jnp.where(front >= n, front - n, front), a + b, t)
        note(t, 0, item, p)
        note(t + 1, 2, item, before)
        a = a + right
        front = org - b
        item, left = choose(jnp.where(front < 0, front + n, front), a + b, t)
        note(t, 1, item, p)
        note(t + 1, 3, item, after)
        b = b + left
        a_ref[...] = a
        b_ref[...] = b
        end_ref[...] = jnp.where(right + left > 0, (t + 1).astype(F32), end_ref[...])
        return t + 1, jnp.sum(n - 1 - a - b).astype(jnp.int32)

    t, _ = lax.while_loop(cond, body, (jnp.int32(0), jnp.int32(1)))
    rounds[0] = t
    note(t, 0, none, p)
    note(t, 1, none, p)
    for k in range(count):
        comp[k] = jnp.max(end_ref[pl.ds(k * specials, specials), :]).astype(jnp.int32)


def table_call(n, count, specials, limbs, least, order, pos, spot):
    items = count * specials
    most = items * (n - 1) + 2 * count
    return pl.pallas_call(
        functools.partial(table_kernel, n, count, specials, limbs, least),
        in_specs=[SMEM] * 3,
        out_specs=[pl.BlockSpec(memory_space=pltpu.VMEM), SMEM, SMEM],
        out_shape=[
            jax.ShapeDtypeStruct((most + 1, 8, LANES), jnp.int32),
            jax.ShapeDtypeStruct((1,), jnp.int32),
            jax.ShapeDtypeStruct((count,), jnp.int32),
        ],
        scratch_shapes=[pltpu.VMEM((items, LANES), F32)] * 3,
        compiler_params=params(8),
        name="table",
    )(order, pos, spot)


def pack_kernel(items, t, first, last, *refs):
    refs = list(refs)
    if t is None:
        t = refs.pop(0)[0]
    table, store = refs.pop(0), refs.pop(0)
    ins = () if first else (refs.pop(0), refs.pop(0))
    refs.pop(0)
    outs = () if last else (refs.pop(0), refs.pop(0))
    tile, keep, send, tsem = refs
    plan = pltpu.make_async_copy(table.at[t], tile, tsem)
    plan.start()
    plan.wait()
    go = [tile[0, 0], tile[1, 0]]
    came = [tile[2, 0], tile[3, 0]]
    for i in range(len(ins)):
        @pl.when(came[i] < items)
        def _():
            pltpu.make_async_copy(ins[i], store.at[came[i]], keep.at[i]).start()

    old = []
    for j in range(len(outs)):
        fresh = [jnp.logical_and(go[j] == came[i], came[i] < items) for i in range(len(ins))]
        held = go[j] < items
        for f in fresh:
            held = jnp.logical_and(held, jnp.logical_not(f))
        old.append(held)

        @pl.when(held)
        def _():
            pltpu.make_async_copy(store.at[go[j]], outs[j], send.at[j]).start()

        for i in range(len(ins)):
            @pl.when(fresh[i])
            def _():
                outs[j][...] = ins[i][...]

    for i in range(len(ins)):
        @pl.when(came[i] < items)
        def _():
            pltpu.make_async_copy(ins[i], store.at[came[i]], keep.at[i]).wait()
    for j in range(len(outs)):
        @pl.when(old[j])
        def _():
            pltpu.make_async_copy(store.at[go[j]], outs[j], send.at[j]).wait()


def pack_call(table, t, store, ins=None, last=False):
    first = ins is None
    items = store.shape[0]
    item = jax.ShapeDtypeStruct(store.shape[1:], store.dtype)
    static = isinstance(t, int)
    args = (() if static else (t.reshape(1),)) + (table, store) + (() if first else tuple(ins))
    at = 1 if static else 2
    outs = [jax.ShapeDtypeStruct(store.shape, store.dtype)] + ([] if last else [item, item])
    size = math.prod(item.shape) * 4
    res = pl.pallas_call(
        functools.partial(pack_kernel, items, t if static else None, first, last),
        in_specs=([] if static else [SMEM]) + [ANY, ANY] + [VMEM] * (0 if first else 2),
        out_specs=[ANY] + [VMEM] * (len(outs) - 1),
        out_shape=outs,
        input_output_aliases={at: 0},
        scratch_shapes=[
            pltpu.SMEM(table.shape[1:], jnp.int32),
            pltpu.SemaphoreType.DMA((2,)),
            pltpu.SemaphoreType.DMA((2,)),
            pltpu.SemaphoreType.DMA,
        ],
        compiler_params=params(2),
        cost_estimate=pl.CostEstimate(flops=0, bytes_accessed=8 * size, transcendentals=0),
        name="pack",
    )(*args)
    return res[0], list(res[1:])


def lower_kernel(low, high, specials, limbs, *refs):
    order, digit, where, scale, conv, comp, diag, mats, part, *refs = refs
    store = refs[:2]
    total, got, dg, xs, sem = refs[-5:]
    count = diag.shape[0]
    first = where[0] * limbs
    total[...] = part[...]

    def turn(k, carry):
        ripe = comp[k] > low
        if high is not None:
            ripe = jnp.logical_and(ripe, comp[k] <= high)

        @pl.when(ripe)
        def _():
            copies = [
                pltpu.make_async_copy(store[c].at[pl.ds(k * specials, specials)], got.at[c], sem.at[c])
                for c in range(2)
            ] + [pltpu.make_async_copy(diag.at[k], dg, sem.at[2])]
            for copy in copies:
                copy.start()
            for copy in copies:
                copy.wait()

            def limb(m, carry):
                q = first + m

                @pl.when(digit[q] != DIGITS)
                def _():
                    h = (mats[m, 0], mats[m, 1])
                    w = [conv[q, order[DIGITS * specials + s]] for s in range(specials)]
                    size = scale[q]
                    step = 64
                    for c in range(2):
                        for i in range(2):
                            for r in range(0, RADIX, step):
                                x = w[0] * got[c, 0, pl.ds(i * RADIX + r, step), :]
                                for s in range(1, specials):
                                    x = x + w[s] * got[c, s, pl.ds(i * RADIX + r, step), :]
                                hi, lo = split(x)
                                xs[c, 0, pl.ds(r, step), pl.ds(i * LANES, LANES)] = hi
                                xs[c, 1, pl.ds(r, step), pl.ds(i * LANES, LANES)] = lo
                    for c in range(2):
                        y = mm(h, split(mm((xs[c, 0], xs[c, 1]), h)))
                        for i in range(2):
                            at = pl.ds(i * limbs + m, RADIX, stride=2 * limbs)
                            total[c, at, :] = total[c, at, :] - dg[at, :] * size * y[:, i * LANES : (i + 1) * LANES]

                return carry

            lax.fori_loop(0, limbs, limb, 0)

        return carry

    lax.fori_loop(0, count, turn, 0)
    if high is None:
        keep, send = refs[2:4]
        half = total.shape[1] // 2
        mine = where[1]
        keep[...] = total[:, pl.ds(pl.multiple_of(mine * half, half), half), :]
        send[...] = total[:, pl.ds(pl.multiple_of((1 - mine) * half, half), half), :]
    else:
        refs[2][...] = total[...]


def lower_call(low, high, order, digit, where, scale, conv, comp, diag, mats, part, stores, specials):
    limbs = mats.shape[0]
    rows = part.shape[1]
    half = jax.ShapeDtypeStruct((2, rows // 2, LANES), F32)
    last = high is None
    shape = lambda a: jax.ShapeDtypeStruct(a.shape, a.dtype)
    return pl.pallas_call(
        functools.partial(lower_kernel, low, high, specials, limbs),
        in_specs=[SMEM] * 6 + [ANY, VMEM, VMEM, ANY, ANY],
        out_specs=[VMEM] * 2 if last else [VMEM, ANY, ANY],
        out_shape=[half] * 2 if last else [shape(part)] + [shape(s) for s in stores],
        input_output_aliases={} if last else {9: 1, 10: 2},
        scratch_shapes=[
            pltpu.VMEM((2, rows, LANES), F32),
            pltpu.VMEM((2, specials, 2 * RADIX, LANES), F32),
            pltpu.VMEM((rows, LANES), F32),
            pltpu.VMEM((2, 2, RADIX, RADIX), BF16),
            pltpu.SemaphoreType.DMA((3,)),
        ],
        compiler_params=params(24),
        cost_estimate=pl.CostEstimate(flops=10**9, bytes_accessed=12 * 2**20, transcendentals=0),
        name="lower",
    )(order, digit, where, scale, conv, comp, diag, mats, part, *stores)


def interleave(x):
    *lead, limbs, coeffs = x.shape
    x = x.reshape(*lead, limbs, coeffs // LANES, LANES)
    return jnp.swapaxes(x, -3, -2).reshape(*lead, coeffs // LANES * limbs, LANES)


def per_device(order_of, cipher, rotation_keys, diagonals, shifts, twiddles, moduli, digit_of, conversion):
    n = len(order_of)
    limbs = cipher.shape[0]
    ext = digit_of.shape[0]
    specials = ext // (DIGITS + 1)
    count = rotation_keys.shape[1]
    items = count * specials
    pos_of = np.argsort(np.array(order_of)).astype(np.int32)
    cw = [(order_of[i], order_of[(i + 1) % n]) for i in range(n)]
    ccw = [(b, a) for a, b in cw]
    me, rot = lax.axis_index("limb"), lax.axis_index("rot")
    where = jnp.stack([me, rot]).astype(jnp.int32)
    pos = jnp.asarray(pos_of)
    my_pos = pos[me]
    swap = lambda x: lax.ppermute(x, "rot", [(0, 1), (1, 0)])

    grid = np.arange(RADIX)
    angle = (grid[:, None] * grid[None, :] % RADIX) * (2.0 * math.pi / RADIX)
    base = ((np.cos(angle) + np.sin(angle)) / math.sqrt(RADIX)).astype(np.float32)
    base_hi = base.astype(BF16)
    base_lo = (base - base_hi.astype(np.float32)).astype(BF16)

    rows_c = interleave(cipher)
    keys = interleave(rotation_keys).reshape(count, DIGITS * 2, -1, LANES)
    diag = interleave(diagonals).reshape(count, -1, LANES)

    coef, mats = coef_call(twiddles, where, jnp.asarray(base_hi), jnp.asarray(base_lo), rows_c, limbs)

    ids = jnp.arange(ext, dtype=jnp.int32)
    before = (digit_of[None, :] < digit_of[:, None]) | (
        (digit_of[None, :] == digit_of[:, None]) & (ids[None, :] < ids[:, None])
    )
    place = jnp.sum(before.astype(jnp.int32), axis=1)
    order = jnp.sum(jnp.where(place[None, :] == ids[:, None], ids[None, :], 0), axis=1)
    slot = lax.dynamic_slice_in_dim(jnp.maximum(place - DIGITS * specials, -1), me * limbs, limbs, 0)
    special = digit_of == DIGITS
    mod = moduli.astype(F32)
    scale = jnp.sum(jnp.where(special[None, :], mod[:, None] / mod[None, :], 0.0), axis=1) / specials
    my_special = lax.dynamic_slice_in_dim(special, me * limbs, limbs, 0)
    my_gain = jnp.where(my_special, 1.0, lax.dynamic_slice_in_dim(scale, me * limbs, limbs, 0))
    rows8 = lambda v: jnp.broadcast_to(jnp.tile(v, 8 // limbs)[:, None], (8, LANES))
    gain, mask = rows8(my_gain), rows8(my_special.astype(F32))

    blocks, lens, steps = [coef], [(0, limbs)], [0]
    right, left = coef, coef
    both = (n - 1) // 2
    for r in range(1, both + 1):
        right, left = lax.ppermute(right, "limb", cw), lax.ppermute(left, "limb", ccw)
        blocks += [right, left]
        lens += [(0, limbs)] * 2
        steps += [-r, r]
    if n % 2 == 0:
        cut = limbs // 2
        blocks += [lax.ppermute(right[:cut], "limb", cw), lax.ppermute(left[cut:], "limb", ccw)]
        lens += [(0, cut), (cut, limbs)]
        steps += [n // 2, n // 2]
    srcs = jnp.asarray(
        np.array([[order_of[(pos_of[d] + s) % n] for s in steps] for d in range(n)], np.int32)
    )[me]

    fixed = items * n // (2 * n)
    plan, rounds, comp = table_call(n, count, specials, limbs, fixed, order, pos, my_pos.reshape(1))
    blocks[-1], order, slot, gain, mask, scale, plan, rounds, comp = lax.optimization_barrier(
        (blocks[-1], order, slot, gain, mask, scale, plan, rounds, comp)
    )

    mixed = mix_call(n, limbs, tuple(lens), order, digit_of, where, srcs, conversion, blocks)
    raised = raise_call(digit_of, where, mixed, swap(mixed), mats, rows_c)

    def accumulate(k, carried=None):
        return accum_call(
            k, shifts.reshape(-1), slot, raised, rows_c, keys, diag, mats, gain, mask, specials, carried
        )

    def lower(low, high, part, stores):
        return lower_call(
            low, high, order, digit_of, where, scale, conversion, comp, diag, mats, part, stores, specials
        )

    def travel(sends):
        return [lax.ppermute(sends[0], "limb", cw), lax.ppermute(sends[1], "limb", ccw)]

    ready = {max(2 * k - 1, 0): k for k in range(1, count)}
    gates = [fixed - 5, fixed - 3, fixed - 1]
    part, *stores = accumulate(0)
    ins = [None, None]
    low = -1
    for t in range(fixed):
        if t in ready:
            part, *stores = accumulate(ready[t], (part, *stores))
        for c in range(2):
            stores[c], sends = pack_call(plan, t, stores[c], ins[c])
            ins[c] = travel(sends)
        if t in gates:
            part, *stores = lower(low, t, part, stores)
            low = t

    def more(state):
        return state[0] < rounds[0]

    def one(state):
        t, stores, ins = state
        stores, ins = list(stores), list(ins)
        for c in range(2):
            stores[c], sends = pack_call(plan, t, stores[c], ins[c])
            ins[c] = travel(sends)
        return t + 1, stores, ins

    t, stores, ins = lax.while_loop(more, one, (jnp.int32(fixed), stores, ins))
    stores = [pack_call(plan, t, stores[c], ins[c], last=True)[0] for c in range(2)]
    keep, send = lower(low, None, part, stores)
    total = keep + swap(send)
    total = jnp.swapaxes(total.reshape(2, -1, limbs, LANES), 1, 2)
    return total.reshape(2, limbs, -1)


def solution(mesh):
    in_specs = (
        P(("parts", "limb"), None),
        P("rot", None, None, None, "limb", None),
        P("rot", None, "limb", None),
        P("rot", None),
        P(),
        P(),
        P(),
        P(),
    )
    out_specs = P(None, ("parts", "limb"), "rot")
    return jax.shard_map(
        functools.partial(per_device, ring_order(mesh)),
        mesh=mesh,
        in_specs=in_specs,
        out_specs=out_specs,
        check_vma=False,
    )
```

```python
import functools
import math

import jax
import jax.numpy as jnp
import numpy as np
from jax import lax
from jax.experimental import pallas as pl
from jax.experimental.pallas import tpu as pltpu
from jax.sharding import PartitionSpec as P

RADIX = 256
DIGITS = 3
LANES = 128
F32 = jnp.float32
BF16 = jnp.bfloat16


ANY = pl.BlockSpec(memory_space=pl.ANY)
VMEM = pl.BlockSpec(memory_space=pltpu.VMEM)
HBM = pl.BlockSpec(memory_space=pltpu.HBM)
SMEM = pl.BlockSpec(memory_space=pltpu.SMEM)


def ring_order(mesh):
    n = mesh.shape["limb"]
    line = np.moveaxis(mesh.devices, list(mesh.axis_names).index("limb"), 0).reshape(n, -1)[:, 0]
    at = [getattr(d, "coords", None) for d in line]
    if any(c is None for c in at):
        return list(range(n))
    near = [
        [j for j in range(n) if sum(abs(x - y) for x, y in zip(at[i], at[j])) == 1] for i in range(n)
    ]

    def walk(path):
        if len(path) == n:
            return path if 0 in near[path[-1]] else None
        for j in near[path[-1]]:
            if j not in path:
                found = walk(path + [j])
                if found:
                    return found
        return None

    return walk([0]) or list(range(n))


def split(x):
    hi = x.astype(BF16)
    return hi, (x - hi.astype(F32)).astype(BF16)


def mm(a, b):
    dot = functools.partial(jnp.dot, preferred_element_type=F32)
    return dot(a[0], b[0]) + dot(a[1], b[0]) + dot(a[0], b[1])


def spin(x, h):
    return mm(h, split(mm(split(x), h)))


def grid_of(ref, m, limbs):
    left = ref[pl.ds(m, RADIX, stride=2 * limbs), :]
    right = ref[pl.ds(limbs + m, RADIX, stride=2 * limbs), :]
    return jnp.concatenate([left, right], axis=1)


def in_hbm(x):
    return pltpu.with_memory_space_constraint(x, pltpu.HBM)


def params(mib):
    return pltpu.CompilerParams(vmem_limit_bytes=mib * 2**20)


def coef_kernel(tw, where, base_hi, base_lo, cipher, coef, mats, grid, bases, sem):
    limbs = coef.shape[0]
    copies = [
        pltpu.make_async_copy(base_hi, bases.at[0], sem.at[0]),
        pltpu.make_async_copy(base_lo, bases.at[1], sem.at[1]),
        pltpu.make_async_copy(cipher, grid, sem.at[2]),
    ]
    for copy in copies:
        copy.start()
    row = lax.broadcasted_iota(jnp.int32, (RADIX, RADIX), 0)
    col = lax.broadcasted_iota(jnp.int32, (RADIX, RADIX), 1)
    first = where[1] == 0
    for copy in copies:
        copy.wait()

    def limb(m, carry):
        g = tw[where[0] * limbs + m]
        pick = jnp.where(((row * g) & (RADIX - 1)) == col, 1.0, 0.0).astype(BF16)
        hi = jnp.dot(pick, bases[0], preferred_element_type=F32).astype(BF16)
        lo = jnp.dot(pick, bases[1], preferred_element_type=F32).astype(BF16)
        mats[m, 0] = hi
        mats[m, 1] = lo
        u = split(mm((hi, lo), split(grid_of(grid, m, limbs))))
        half = tuple(
            jnp.where(first, h[:, :LANES].astype(F32), h[:, LANES:].astype(F32)).astype(BF16) for h in (hi, lo)
        )
        coef[m] = mm(u, half)
        return carry

    lax.fori_loop(0, limbs, limb, 0)


def coef_call(tw, where, base_hi, base_lo, cipher, limbs):
    return pl.pallas_call(
        coef_kernel,
        in_specs=[SMEM, SMEM, HBM, HBM, HBM],
        out_specs=[VMEM, VMEM],
        out_shape=[
            jax.ShapeDtypeStruct((limbs, RADIX, LANES), F32),
            jax.ShapeDtypeStruct((limbs, 2, RADIX, RADIX), BF16),
        ],
        scratch_shapes=[
            pltpu.VMEM(cipher.shape, F32),
            pltpu.VMEM((2, RADIX, RADIX), BF16),
            pltpu.SemaphoreType.DMA((3,)),
        ],
        compiler_params=params(12),
        name="coef",
    )(in_hbm(tw), where, in_hbm(base_hi), in_hbm(base_lo), in_hbm(cipher))


def mix_kernel(n, limbs, lens, order, digit, where, srcs, conv, *refs):
    blocks, out, got, table, sem = refs[: len(lens)], refs[-4], refs[-3], refs[-2], refs[-1]
    size = got.shape[0] * limbs // (DIGITS + 1)
    copies = []
    for i, (start, stop) in enumerate(lens):
        c = pltpu.make_async_copy(blocks[i], got.at[srcs[i], pl.ds(start, stop - start)], sem.at[i])
        c.start()
        copies.append(c)
    first = where[0] * limbs
    for j in range(DIGITS * size):
        l = order[j]
        for m in range(limbs):
            same = digit[l] == digit[first + m]
            one = jnp.where(first + m == l, 1.0, 0.0)
            table[m, j] = jnp.where(same, one, conv[first + m, l])
    for c in copies:
        c.wait()
    step = 64

    def rows(r, carry):
        r0 = pl.multiple_of(r * step, step)
        for d in range(DIGITS):
            acc = [jnp.zeros((step, LANES), F32) for _ in range(limbs)]
            for j in range(size):
                l = order[d * size + j]
                x = got[l // limbs, l % limbs, pl.ds(r0, step), :]
                for m in range(limbs):
                    acc[m] = acc[m] + table[m, d * size + j] * x
            for m in range(limbs):
                out[d, m, pl.ds(r0, step), :] = acc[m]
        return carry

    lax.fori_loop(0, RADIX // step, rows, 0)


def mix_call(n, limbs, lens, order, digit, where, srcs, conv, blocks):
    vmem = pl.BlockSpec(memory_space=pltpu.VMEM)
    return pl.pallas_call(
        functools.partial(mix_kernel, n, limbs, lens),
        in_specs=[SMEM] * 5 + [HBM] * len(blocks),
        out_specs=vmem,
        out_shape=jax.ShapeDtypeStruct((DIGITS, limbs, RADIX, LANES), F32),
        scratch_shapes=[
            pltpu.VMEM((n, limbs, RADIX, LANES), F32),
            pltpu.SMEM((limbs, n * limbs), F32),
            pltpu.SemaphoreType.DMA((len(blocks),)),
        ],
        compiler_params=params(16),
        name="mix",
    )(order, in_hbm(digit), where, srcs, in_hbm(conv), *blocks)


def raise_kernel(pad, digit, where, own, other, mats, cipher, out):
    d, m = pl.program_id(0), pl.program_id(1)
    limbs = pl.num_programs(1)
    same = digit[where[0] * limbs + m] == d
    at = [pl.ds(h * limbs + m, RADIX, stride=2 * limbs) for h in range(2)]

    @pl.when(same)
    def _():
        for h in range(2):
            out[0, at[h], :] = cipher[at[h], :]

    @pl.when(jnp.logical_and(jnp.logical_not(same), d < DIGITS))
    def _():
        first = where[1] == 0
        a, b = own[0, 0], other[0, 0]
        x = jnp.concatenate([jnp.where(first, a, b), jnp.where(first, b, a)], axis=1)
        y = spin(x, (mats[0, 0], mats[0, 1]))
        for h in range(2):
            out[0, at[h], :] = y[:, h * LANES : (h + 1) * LANES]

    @pl.when(jnp.logical_and(jnp.logical_not(same), d == DIGITS))
    def _():
        for h in range(2):
            out[0, at[h], :] = jnp.zeros((RADIX, LANES), F32)

    @pl.when(m == limbs - 1)
    def _():
        out[0, pl.ds(out.shape[1] - pad, pad), :] = out[0, pl.ds(0, pad), :]


def raise_call(digit, where, own, other, mats, cipher, pad):
    limbs = mats.shape[0]
    rows = cipher.shape[0]
    piece = pl.BlockSpec((1, 1, RADIX, LANES), lambda d, m, *_: (jnp.minimum(d, DIGITS - 1), m, 0, 0))
    return pl.pallas_call(
        functools.partial(raise_kernel, pad),
        grid_spec=pltpu.PrefetchScalarGridSpec(
            num_scalar_prefetch=2,
            grid=(DIGITS + 1, limbs),
            in_specs=[
                piece,
                piece,
                pl.BlockSpec((1, 2, RADIX, RADIX), lambda d, m, *_: (m, 0, 0, 0)),
                pl.BlockSpec((rows, LANES), lambda d, m, *_: (0, 0)),
            ],
            out_specs=pl.BlockSpec((1, rows + pad, LANES), lambda d, m, *_: (d, 0, 0)),
        ),
        out_shape=jax.ShapeDtypeStruct((DIGITS + 1, rows + pad, LANES), F32),
        compiler_params=params(16),
        name="raise",
    )(digit, where, own, other, mats, cipher)


def accum_kernel(k, limbs, specials, pad, shifts, slot, raised, keys, diag, mats, gain, *refs):
    part, store, (acc, stage, sem) = refs[-7:-5], refs[-5:-3], refs[-3:]
    rb = pl.program_id(0)
    rows = acc.shape[1]
    block = rows // pl.num_programs(0)
    s = shifts[k]
    tiles, lane = s // LANES, s % LANES
    here = lax.broadcasted_iota(jnp.int32, (pad, LANES), 1) < LANES - lane
    g8 = jnp.concatenate([gain[...]] * (pad // 8), axis=0)

    def add(r, carry):
        r0 = pl.multiple_of(r * pad, pad)
        at = rb * block + r0
        u0 = lax.rem(at - limbs * tiles + rows, rows)
        v0 = lax.rem(at - limbs * tiles - limbs + 2 * rows, rows)
        turned = []
        for g in range(DIGITS + 1):
            u = raised[g, pl.ds(pl.multiple_of(u0, limbs), pad), :]
            v = raised[g, pl.ds(pl.multiple_of(v0, limbs), pad), :]
            turned.append(pltpu.roll(jnp.where(here, u, v), lane, axis=1))
        w = diag[0, pl.ds(r0, pad), :] * g8
        for c in range(2):
            a = turned[DIGITS]
            for d in range(DIGITS):
                a = a + turned[d] * keys[0, 2 * d + c, pl.ds(r0, pad), :]
            acc[c, pl.ds(pl.multiple_of(at, pad), pad), :] = a
            w_a = w * a
            part[c][pl.ds(r0, pad), :] = w_a if k == 0 else refs[c][pl.ds(r0, pad), :] + w_a
        return carry

    lax.fori_loop(0, block // pad, add, 0)

    @pl.when(rb == pl.num_programs(0) - 1)
    def _():
        def emit(m, carry):
            @pl.when(slot[m] >= 0)
            def _():
                h = (mats[m, 0], mats[m, 1])
                copies = []
                for c in range(2):
                    y = spin(grid_of(acc.at[c], m, limbs), h)
                    stage[c, 0:RADIX, :] = y[:, :LANES]
                    stage[c, RADIX:, :] = y[:, LANES:]
                    copies.append(
                        pltpu.make_async_copy(stage.at[c], store[c].at[k * specials + slot[m]], sem.at[c])
                    )
                    copies[-1].start()
                for copy in copies:
                    copy.wait()

            return carry

        lax.fori_loop(0, limbs, emit, 0)


def accum_call(k, shifts, slot, raised, keys, diag, mats, gain, specials, pad, carried=None):
    limbs = mats.shape[0]
    rows = raised.shape[1] - pad
    items = keys.shape[0] * specials
    block = rows // 8
    piece = pl.BlockSpec((block, LANES), lambda r: (r, 0))
    part = jax.ShapeDtypeStruct((rows, LANES), F32)
    store = jax.ShapeDtypeStruct((items, 2 * RADIX, LANES), F32)
    args = (in_hbm(shifts), slot, raised, in_hbm(keys), in_hbm(diag), mats, gain)
    specs = [
        SMEM,
        SMEM,
        VMEM,
        pl.BlockSpec((1, keys.shape[1], block, LANES), lambda r: (k, 0, r, 0)),
        pl.BlockSpec((1, block, LANES), lambda r: (k, r, 0)),
        VMEM,
        VMEM,
    ]
    alias = {}
    if carried is not None:
        carried = (*carried[:2], *map(in_hbm, carried[2:]))
        alias = {len(args) + i: i for i in range(4)}
        args += tuple(carried)
        specs += [piece, piece, HBM, HBM]
    return pl.pallas_call(
        functools.partial(accum_kernel, k, limbs, specials, pad),
        grid=(rows // block,),
        in_specs=specs,
        out_specs=[piece, piece, HBM, HBM],
        out_shape=[part, part, store, store],
        input_output_aliases=alias,
        scratch_shapes=[
            pltpu.VMEM((2, rows, LANES), F32),
            pltpu.VMEM((2, 2 * RADIX, LANES), F32),
            pltpu.SemaphoreType.DMA((2,)),
        ],
        compiler_params=params(16),
        cost_estimate=pl.CostEstimate(flops=10**9, bytes_accessed=12 * 2**20, transcendentals=0),
        name="accum",
    )(*args)


def table_kernel(n, count, specials, limbs, least, order, pos, spot, plan, rounds, comp, a_ref, b_ref, end_ref):
    items = count * specials
    shape = (items, LANES)
    row_i = lax.broadcasted_iota(jnp.int32, shape, 0)
    row = row_i.astype(F32)
    lane = lax.broadcasted_iota(jnp.int32, shape, 1).astype(F32)
    kind, turn = lax.rem(row_i, specials), lax.div(row_i, specials)
    ready = jnp.maximum(2 * turn - 1, 0)
    weight = 3.0 * turn.astype(F32)
    p = spot[0]
    before, after = lax.rem(p + n - 1, n), lax.rem(p + 1, n)
    line = lax.broadcasted_iota(jnp.int32, (1, LANES), 1)
    org = jnp.zeros(shape, F32)
    for s in range(specials):
        owner = pos[lax.div(order[DIGITS * specials + s], limbs)]
        org = jnp.where(kind == s, owner.astype(F32), org)
    a_ref[...] = jnp.zeros(shape, F32)
    b_ref[...] = jnp.zeros(shape, F32)
    end_ref[...] = jnp.zeros(shape, F32)
    big = float(items * (2 * n + 3 * count))

    def choose(front, spread, t):
        open_ = jnp.logical_and(spread < n - 1, ready <= t)
        cand = jnp.logical_and(open_, front == lane)
        key = jnp.where(cand, (2.0 * spread + weight) * items + row, big)
        best = jnp.min(key, axis=0, keepdims=True)
        hit = jnp.where(jnp.logical_and(cand, key == best), 1.0, 0.0)
        item = jnp.sum(hit * (row - items), axis=0, keepdims=True) + items
        return item, jnp.sum(hit, axis=1, keepdims=True)

    def note(t, r, item, where):
        mine = jnp.sum(jnp.where(line == where, item, 0.0), axis=1, keepdims=True)
        plan[t, pl.ds(r, 1), :] = jnp.broadcast_to(mine, (1, LANES)).astype(jnp.int32)

    none = jnp.full((1, LANES), float(items), F32)
    note(0, 2, none, p)
    note(0, 3, none, p)

    def cond(c):
        return jnp.logical_or(c[1] > 0, c[0] < least)

    def body(c):
        t, _ = c
        a, b = a_ref[...], b_ref[...]
        front = org + a
        item, right = choose(jnp.where(front >= n, front - n, front), a + b, t)
        note(t, 0, item, p)
        note(t + 1, 2, item, before)
        a = a + right
        front = org - b
        item, left = choose(jnp.where(front < 0, front + n, front), a + b, t)
        note(t, 1, item, p)
        note(t + 1, 3, item, after)
        b = b + left
        a_ref[...] = a
        b_ref[...] = b
        end_ref[...] = jnp.where(right + left > 0, (t + 1).astype(F32), end_ref[...])
        return t + 1, jnp.sum(n - 1 - a - b).astype(jnp.int32)

    t, _ = lax.while_loop(cond, body, (jnp.int32(0), jnp.int32(1)))
    rounds[0] = t
    note(t, 0, none, p)
    note(t, 1, none, p)
    for k in range(count):
        comp[k] = jnp.max(end_ref[pl.ds(k * specials, specials), :]).astype(jnp.int32)


def table_call(n, count, specials, limbs, least, order, pos, spot):
    items = count * specials
    most = items * (n - 1) + 2 * count
    return pl.pallas_call(
        functools.partial(table_kernel, n, count, specials, limbs, least),
        in_specs=[SMEM] * 3,
        out_specs=[pl.BlockSpec(memory_space=pltpu.VMEM), SMEM, SMEM],
        out_shape=[
            jax.ShapeDtypeStruct((most + 1, 8, LANES), jnp.int32),
            jax.ShapeDtypeStruct((1,), jnp.int32),
            jax.ShapeDtypeStruct((count,), jnp.int32),
        ],
        scratch_shapes=[pltpu.VMEM((items, LANES), F32)] * 3,
        compiler_params=params(8),
        name="table",
    )(order, in_hbm(pos), spot)


def pack_kernel(items, t, first, last, *refs):
    refs = list(refs)
    if t is None:
        t = refs.pop(0)[0]
    table, store = refs.pop(0), refs.pop(0)
    ins = () if first else (refs.pop(0), refs.pop(0))
    refs.pop(0)
    outs = () if last else (refs.pop(0), refs.pop(0))
    tile, keep, send, tsem = refs
    plan = pltpu.make_async_copy(table.at[t], tile, tsem)
    plan.start()
    plan.wait()
    go = [tile[0, 0], tile[1, 0]]
    came = [tile[2, 0], tile[3, 0]]
    for i in range(len(ins)):
        @pl.when(came[i] < items)
        def _():
            pltpu.make_async_copy(ins[i], store.at[came[i]], keep.at[i]).start()

    old = []
    for j in range(len(outs)):
        fresh = [jnp.logical_and(go[j] == came[i], came[i] < items) for i in range(len(ins))]
        held = go[j] < items
        for f in fresh:
            held = jnp.logical_and(held, jnp.logical_not(f))
        old.append(held)

        @pl.when(held)
        def _():
            pltpu.make_async_copy(store.at[go[j]], outs[j], send.at[j]).start()

        for i in range(len(ins)):
            @pl.when(fresh[i])
            def _():
                outs[j][...] = ins[i][...]

    for i in range(len(ins)):
        @pl.when(came[i] < items)
        def _():
            pltpu.make_async_copy(ins[i], store.at[came[i]], keep.at[i]).wait()
    for j in range(len(outs)):
        @pl.when(old[j])
        def _():
            pltpu.make_async_copy(store.at[go[j]], outs[j], send.at[j]).wait()


def pack_call(table, t, store, ins=None, last=False):
    first = ins is None
    store = in_hbm(store)
    items = store.shape[0]
    item = jax.ShapeDtypeStruct(store.shape[1:], store.dtype)
    static = isinstance(t, int)
    args = (() if static else (t.reshape(1),)) + (table, store) + (() if first else tuple(ins))
    at = 1 if static else 2
    outs = [jax.ShapeDtypeStruct(store.shape, store.dtype)] + ([] if last else [item, item])
    size = math.prod(item.shape) * 4
    res = pl.pallas_call(
        functools.partial(pack_kernel, items, t if static else None, first, last),
        in_specs=([] if static else [SMEM]) + [ANY, HBM] + [VMEM] * (0 if first else 2),
        out_specs=[HBM] + [VMEM] * (len(outs) - 1),
        out_shape=outs,
        input_output_aliases={at: 0},
        scratch_shapes=[
            pltpu.SMEM(table.shape[1:], jnp.int32),
            pltpu.SemaphoreType.DMA((2,)),
            pltpu.SemaphoreType.DMA((2,)),
            pltpu.SemaphoreType.DMA,
        ],
        compiler_params=params(2),
        cost_estimate=pl.CostEstimate(flops=0, bytes_accessed=8 * size, transcendentals=0),
        name="pack",
    )(*args)
    return res[0], list(res[1:])


def lower_kernel(low, high, specials, limbs, *refs):
    order, digit, where, scale, conv, comp, diag, mats, part, store, *refs = refs
    last = high is None
    if last:
        t, plan, in0, in1, store, keep, send, total, got, dg, xs, sem, tile = refs
        copy = pltpu.make_async_copy(plan.at[t[0]], tile, sem.at[2])
        copy.start()
        copy.wait()
        came = [tile[2, 0], tile[3, 0]]
        for i, ref in enumerate((in0, in1)):
            @pl.when(came[i] < store.shape[0])
            def _():
                pltpu.make_async_copy(ref, store.at[came[i]], sem.at[i]).start()
        for i, ref in enumerate((in0, in1)):
            @pl.when(came[i] < store.shape[0])
            def _():
                pltpu.make_async_copy(ref, store.at[came[i]], sem.at[i]).wait()
    else:
        total, _, got, dg, xs, sem = refs
    count = diag.shape[0]
    first = where[0] * limbs
    total[...] = part[...]

    def turn(k, carry):
        ripe = comp[k] > low
        if not last:
            ripe = jnp.logical_and(ripe, comp[k] <= high)

        @pl.when(ripe)
        def _():
            copies = [
                pltpu.make_async_copy(store.at[pl.ds(k * specials, specials)], got, sem.at[0]),
                pltpu.make_async_copy(diag.at[k], dg, sem.at[1]),
            ]
            for copy in copies:
                copy.start()
            for copy in copies:
                copy.wait()

            def limb(m, carry):
                q = first + m

                @pl.when(digit[q] != DIGITS)
                def _():
                    h = (mats[m, 0], mats[m, 1])
                    w = [conv[q, order[DIGITS * specials + s]] for s in range(specials)]
                    size = scale[q]
                    step = 64
                    for i in range(2):
                        for r in range(0, RADIX, step):
                            x = w[0] * got[0, pl.ds(i * RADIX + r, step), :]
                            for s in range(1, specials):
                                x = x + w[s] * got[s, pl.ds(i * RADIX + r, step), :]
                            hi, lo = split(x)
                            xs[0, pl.ds(r, step), pl.ds(i * LANES, LANES)] = hi
                            xs[1, pl.ds(r, step), pl.ds(i * LANES, LANES)] = lo
                    y = mm(h, split(mm((xs[0], xs[1]), h)))
                    for i in range(2):
                        at = pl.ds(i * limbs + m, RADIX, stride=2 * limbs)
                        total[at, :] = total[at, :] - dg[at, :] * size * y[:, i * LANES : (i + 1) * LANES]

                return carry

            lax.fori_loop(0, limbs, limb, 0)

        return carry

    lax.fori_loop(0, count, turn, 0)
    if last:
        half = total.shape[0] // 2
        mine = where[1]
        keep[...] = total[pl.ds(pl.multiple_of(mine * half, half), half), :]
        send[...] = total[pl.ds(pl.multiple_of((1 - mine) * half, half), half), :]


def lower_call(low, high, order, digit, where, scale, conv, comp, diag, mats, specials, part, store, end=()):
    limbs = mats.shape[0]
    store = in_hbm(store)
    rows = part.shape[0]
    half = jax.ShapeDtypeStruct((rows // 2, LANES), F32)
    last = high is None
    shape = lambda a: jax.ShapeDtypeStruct(a.shape, a.dtype)
    scratch = [
        pltpu.VMEM((specials, 2 * RADIX, LANES), F32),
        pltpu.VMEM((rows, LANES), F32),
        pltpu.VMEM((2, RADIX, RADIX), BF16),
        pltpu.SemaphoreType.DMA((3,)),
    ]
    if last:
        scratch = [pltpu.VMEM((rows, LANES), F32)] + scratch + [pltpu.SMEM(end[1].shape[1:], jnp.int32)]
    return pl.pallas_call(
        functools.partial(lower_kernel, low, high, specials, limbs),
        in_specs=[SMEM] * 6 + [ANY, VMEM, VMEM, HBM] + ([SMEM] + [ANY] * 3 if last else []),
        out_specs=[HBM, VMEM, VMEM] if last else [VMEM, HBM],
        out_shape=[shape(store), half, half] if last else [shape(part), shape(store)],
        input_output_aliases={9: 0} if last else {9: 1},
        scratch_shapes=scratch,
        compiler_params=params(16),
        cost_estimate=pl.CostEstimate(flops=5 * 10**8, bytes_accessed=6 * 2**20, transcendentals=0),
        name="lower",
    )(order, in_hbm(digit), where, scale, in_hbm(conv), comp, in_hbm(diag), mats, part, store, *end)


def interleave(x):
    *lead, limbs, coeffs = x.shape
    x = x.reshape(*lead, limbs, coeffs // LANES, LANES)
    return jnp.swapaxes(x, -3, -2).reshape(*lead, coeffs // LANES * limbs, LANES)


def per_device(order_of, cipher, rotation_keys, diagonals, shifts, twiddles, moduli, digit_of, conversion):
    n = len(order_of)
    limbs = cipher.shape[0]
    ext = digit_of.shape[0]
    specials = ext // (DIGITS + 1)
    count = rotation_keys.shape[1]
    items = count * specials
    pos_of = np.argsort(np.array(order_of)).astype(np.int32)
    cw = [(order_of[i], order_of[(i + 1) % n]) for i in range(n)]
    ccw = [(b, a) for a, b in cw]
    me, rot = lax.axis_index("limb"), lax.axis_index("rot")
    where = jnp.stack([me, rot]).astype(jnp.int32)
    pos = jnp.asarray(pos_of)
    my_pos = pos[me]
    swap = lambda x: lax.ppermute(x, "rot", [(0, 1), (1, 0)])

    grid = np.arange(RADIX)
    angle = (grid[:, None] * grid[None, :] % RADIX) * (2.0 * math.pi / RADIX)
    base = ((np.cos(angle) + np.sin(angle)) / math.sqrt(RADIX)).astype(np.float32)
    base_hi = base.astype(BF16)
    base_lo = (base - base_hi.astype(np.float32)).astype(BF16)

    rows_c = interleave(cipher)
    keys = interleave(rotation_keys).reshape(count, DIGITS * 2, -1, LANES)
    diag = interleave(diagonals).reshape(count, -1, LANES)

    coef, mats = coef_call(twiddles, where, jnp.asarray(base_hi), jnp.asarray(base_lo), rows_c, limbs)

    ids = jnp.arange(ext, dtype=jnp.int32)
    before = (digit_of[None, :] < digit_of[:, None]) | (
        (digit_of[None, :] == digit_of[:, None]) & (ids[None, :] < ids[:, None])
    )
    place = jnp.sum(before.astype(jnp.int32), axis=1)
    order = jnp.sum(jnp.where(place[None, :] == ids[:, None], ids[None, :], 0), axis=1)
    slot = lax.dynamic_slice_in_dim(jnp.maximum(place - DIGITS * specials, -1), me * limbs, limbs, 0)
    special = digit_of == DIGITS
    mod = moduli.astype(F32)
    scale = jnp.sum(jnp.where(special[None, :], mod[:, None] / mod[None, :], 0.0), axis=1) / specials
    my_special = lax.dynamic_slice_in_dim(special, me * limbs, limbs, 0)
    my_gain = jnp.where(my_special, 1.0, lax.dynamic_slice_in_dim(scale, me * limbs, limbs, 0))
    rows8 = lambda v: jnp.broadcast_to(jnp.tile(v, 8 // limbs)[:, None], (8, LANES))
    gain = rows8(my_gain)
    fixed = items * n // (2 * n)
    plan, rounds, comp = table_call(n, count, specials, limbs, fixed, order, pos, my_pos.reshape(1))

    blocks, lens, steps = [coef], [(0, limbs)], [0]
    right, left = coef, coef
    both = (n - 1) // 2
    for r in range(1, both + 1):
        right, left = lax.ppermute(right, "limb", cw), lax.ppermute(left, "limb", ccw)
        blocks += [right, left]
        lens += [(0, limbs)] * 2
        steps += [-r, r]
        if r == 2:
            right, left, order, slot, gain, scale, plan, rounds, comp = lax.optimization_barrier(
                (right, left, order, slot, gain, scale, plan, rounds, comp)
            )
    if n % 2 == 0:
        cut = limbs // 2
        blocks += [lax.ppermute(right[:cut], "limb", cw), lax.ppermute(left[cut:], "limb", ccw)]
        lens += [(0, cut), (cut, limbs)]
        steps += [n // 2, n // 2]
    srcs = jnp.asarray(
        np.array([[order_of[(pos_of[d] + s) % n] for s in steps] for d in range(n)], np.int32)
    )[me]

    pad = 64
    mixed = mix_call(n, limbs, tuple(lens), order, digit_of, where, srcs, conversion, blocks)
    raised = raise_call(digit_of, where, mixed, swap(mixed), mats, rows_c, pad)

    def accumulate(k, carried=None):
        return accum_call(k, shifts.reshape(-1), slot, raised, keys, diag, mats, gain, specials, pad, carried)

    def lower(low, high, c, end=()):
        return lower_call(
            low, high, order, digit_of, where, scale, conversion, comp, diag, mats, specials, part[c], stores[c], end
        )

    def travel(sends):
        return [lax.ppermute(sends[0], "limb", cw), lax.ppermute(sends[1], "limb", ccw)]

    ready = {max(2 * k - 1, 0): k for k in range(1, count)}
    gates = [fixed - 5, fixed - 3, fixed - 1]
    part, stores = [None, None], [None, None]
    *part, stores[0], stores[1] = accumulate(0)
    ins = [None, None]
    low = -1
    for t in range(fixed):
        if t in ready:
            *part, stores[0], stores[1] = accumulate(ready[t], (*part, *stores))
        for c in range(2):
            stores[c], sends = pack_call(plan, t, stores[c], ins[c])
            ins[c] = travel(sends)
            if t in gates:
                part[c], stores[c] = lower(low, t, c)
        if t in gates:
            low = t

    def more(state):
        return state[0] < rounds[0]

    def one(state):
        t, stores, ins = state
        stores, ins = list(stores), list(ins)
        for c in range(2):
            stores[c], sends = pack_call(plan, t, stores[c], ins[c])
            ins[c] = travel(sends)
        return t + 1, stores, ins

    t, stores, ins = lax.while_loop(more, one, (jnp.int32(fixed), stores, ins))
    sums = []
    for c in range(2):
        _, keep, send = lower(low, None, c, (t.reshape(1), plan, *ins[c]))
        sums.append(keep + swap(send))
    total = jnp.stack(sums)
    total = jnp.swapaxes(total.reshape(2, -1, limbs, LANES), 1, 2)
    return total.reshape(2, limbs, -1)


def solution(mesh):
    in_specs = (
        P(("parts", "limb"), None),
        P("rot", None, None, None, "limb", None),
        P("rot", None, "limb", None),
        P("rot", None),
        P(),
        P(),
        P(),
        P(),
    )
    out_specs = P(None, ("parts", "limb"), "rot")
    return jax.shard_map(
        functools.partial(per_device, ring_order(mesh)),
        mesh=mesh,
        in_specs=in_specs,
        out_specs=out_specs,
        check_vma=False,
    )
```

```python
import functools
import math

import jax
import jax.numpy as jnp
import numpy as np
from jax import lax
from jax.experimental import pallas as pl
from jax.experimental.pallas import tpu as pltpu
from jax.sharding import PartitionSpec as P

RADIX = 256
DIGITS = 3
LANES = 128
PLAN = 4
F32 = jnp.float32
BF16 = jnp.bfloat16


ANY = pl.BlockSpec(memory_space=pl.ANY)
VMEM = pl.BlockSpec(memory_space=pltpu.VMEM)
HBM = pl.BlockSpec(memory_space=pltpu.HBM)
SMEM = pl.BlockSpec(memory_space=pltpu.SMEM)


def ring_order(mesh):
    n = mesh.shape["limb"]
    line = np.moveaxis(mesh.devices, list(mesh.axis_names).index("limb"), 0).reshape(n, -1)[:, 0]
    at = [getattr(d, "coords", None) for d in line]
    if any(c is None for c in at):
        return list(range(n))
    near = [
        [j for j in range(n) if sum(abs(x - y) for x, y in zip(at[i], at[j])) == 1] for i in range(n)
    ]

    def walk(path):
        if len(path) == n:
            return path if 0 in near[path[-1]] else None
        for j in near[path[-1]]:
            if j not in path:
                found = walk(path + [j])
                if found:
                    return found
        return None

    return walk([0]) or list(range(n))


def split(x):
    hi = x.astype(BF16)
    return hi, (x - hi.astype(F32)).astype(BF16)


def mm(a, b):
    dot = functools.partial(jnp.dot, preferred_element_type=F32)
    return dot(a[0], b[0]) + dot(a[1], b[0]) + dot(a[0], b[1])


def spin(x, h):
    return mm(h, split(mm(split(x), h)))


def grid_of(ref, m, limbs):
    left = ref[pl.ds(m, RADIX, stride=2 * limbs), :]
    right = ref[pl.ds(limbs + m, RADIX, stride=2 * limbs), :]
    return jnp.concatenate([left, right], axis=1)


def in_hbm(x):
    return pltpu.with_memory_space_constraint(x, pltpu.HBM)


def params(mib):
    return pltpu.CompilerParams(vmem_limit_bytes=mib * 2**20)


def coef_kernel(tw, where, base_hi, base_lo, cipher, coef, mats, grid, bases, sem):
    limbs = coef.shape[0]
    copies = [
        pltpu.make_async_copy(base_hi, bases.at[0], sem.at[0]),
        pltpu.make_async_copy(base_lo, bases.at[1], sem.at[1]),
        pltpu.make_async_copy(cipher, grid, sem.at[2]),
    ]
    for copy in copies:
        copy.start()
    row = lax.broadcasted_iota(jnp.int32, (RADIX, RADIX), 0)
    col = lax.broadcasted_iota(jnp.int32, (RADIX, RADIX), 1)
    first = where[1] == 0
    for copy in copies:
        copy.wait()

    def limb(m, carry):
        g = tw[where[0] * limbs + m]
        pick = jnp.where(((row * g) & (RADIX - 1)) == col, 1.0, 0.0).astype(BF16)
        hi = jnp.dot(pick, bases[0], preferred_element_type=F32).astype(BF16)
        lo = jnp.dot(pick, bases[1], preferred_element_type=F32).astype(BF16)
        mats[m, 0] = hi
        mats[m, 1] = lo
        u = split(mm((hi, lo), split(grid_of(grid, m, limbs))))
        half = tuple(
            jnp.where(first, h[:, :LANES].astype(F32), h[:, LANES:].astype(F32)).astype(BF16) for h in (hi, lo)
        )
        coef[m] = mm(u, half)
        return carry

    lax.fori_loop(0, limbs, limb, 0)


def coef_call(tw, where, base_hi, base_lo, cipher, limbs):
    return pl.pallas_call(
        coef_kernel,
        in_specs=[SMEM, SMEM, HBM, HBM, HBM],
        out_specs=[VMEM, VMEM],
        out_shape=[
            jax.ShapeDtypeStruct((limbs, RADIX, LANES), F32),
            jax.ShapeDtypeStruct((limbs, 2, RADIX, RADIX), BF16),
        ],
        scratch_shapes=[
            pltpu.VMEM(cipher.shape, F32),
            pltpu.VMEM((2, RADIX, RADIX), BF16),
            pltpu.SemaphoreType.DMA((3,)),
        ],
        compiler_params=params(12),
        name="coef",
    )(in_hbm(tw), where, in_hbm(base_hi), in_hbm(base_lo), in_hbm(cipher))


def mix_kernel(n, limbs, lens, order, digit, where, srcs, conv, *refs):
    blocks, out, got, table, sem = refs[: len(lens)], refs[-4], refs[-3], refs[-2], refs[-1]
    size = got.shape[0] * limbs // (DIGITS + 1)
    copies = []
    for i, (start, stop) in enumerate(lens):
        c = pltpu.make_async_copy(blocks[i], got.at[srcs[i], pl.ds(start, stop - start)], sem.at[i])
        c.start()
        copies.append(c)
    first = where[0] * limbs
    for j in range(DIGITS * size):
        l = order[j]
        for m in range(limbs):
            same = digit[l] == digit[first + m]
            one = jnp.where(first + m == l, 1.0, 0.0)
            table[m, j] = jnp.where(same, one, conv[first + m, l])
    for c in copies:
        c.wait()
    step = 64

    def rows(r, carry):
        r0 = pl.multiple_of(r * step, step)
        for d in range(DIGITS):
            acc = [jnp.zeros((step, LANES), F32) for _ in range(limbs)]
            for j in range(size):
                l = order[d * size + j]
                x = got[l // limbs, l % limbs, pl.ds(r0, step), :]
                for m in range(limbs):
                    acc[m] = acc[m] + table[m, d * size + j] * x
            for m in range(limbs):
                out[d, m, pl.ds(r0, step), :] = acc[m]
        return carry

    lax.fori_loop(0, RADIX // step, rows, 0)


def mix_call(n, limbs, lens, order, digit, where, srcs, conv, blocks):
    vmem = pl.BlockSpec(memory_space=pltpu.VMEM)
    return pl.pallas_call(
        functools.partial(mix_kernel, n, limbs, lens),
        in_specs=[SMEM] * 5 + [HBM] * len(blocks),
        out_specs=vmem,
        out_shape=jax.ShapeDtypeStruct((DIGITS, limbs, RADIX, LANES), F32),
        scratch_shapes=[
            pltpu.VMEM((n, limbs, RADIX, LANES), F32),
            pltpu.SMEM((limbs, n * limbs), F32),
            pltpu.SemaphoreType.DMA((len(blocks),)),
        ],
        compiler_params=params(16),
        name="mix",
    )(order, in_hbm(digit), where, srcs, in_hbm(conv), *blocks)


def raise_kernel(pad, digit, where, own, other, mats, cipher, out):
    d, m = pl.program_id(0), pl.program_id(1)
    limbs = pl.num_programs(1)
    same = digit[where[0] * limbs + m] == d
    at = [pl.ds(h * limbs + m, RADIX, stride=2 * limbs) for h in range(2)]

    @pl.when(same)
    def _():
        for h in range(2):
            out[0, at[h], :] = cipher[at[h], :]

    @pl.when(jnp.logical_and(jnp.logical_not(same), d < DIGITS))
    def _():
        first = where[1] == 0
        a, b = own[0, 0], other[0, 0]
        x = jnp.concatenate([jnp.where(first, a, b), jnp.where(first, b, a)], axis=1)
        y = spin(x, (mats[0, 0], mats[0, 1]))
        for h in range(2):
            out[0, at[h], :] = y[:, h * LANES : (h + 1) * LANES]

    @pl.when(jnp.logical_and(jnp.logical_not(same), d == DIGITS))
    def _():
        for h in range(2):
            out[0, at[h], :] = jnp.zeros((RADIX, LANES), F32)

    @pl.when(m == limbs - 1)
    def _():
        out[0, pl.ds(out.shape[1] - pad, pad), :] = out[0, pl.ds(0, pad), :]


def raise_call(digit, where, own, other, mats, cipher, pad):
    limbs = mats.shape[0]
    rows = cipher.shape[0]
    piece = pl.BlockSpec((1, 1, RADIX, LANES), lambda d, m, *_: (jnp.minimum(d, DIGITS - 1), m, 0, 0))
    return pl.pallas_call(
        functools.partial(raise_kernel, pad),
        grid_spec=pltpu.PrefetchScalarGridSpec(
            num_scalar_prefetch=2,
            grid=(DIGITS + 1, limbs),
            in_specs=[
                piece,
                piece,
                pl.BlockSpec((1, 2, RADIX, RADIX), lambda d, m, *_: (m, 0, 0, 0)),
                pl.BlockSpec((rows, LANES), lambda d, m, *_: (0, 0)),
            ],
            out_specs=pl.BlockSpec((1, rows + pad, LANES), lambda d, m, *_: (d, 0, 0)),
        ),
        out_shape=jax.ShapeDtypeStruct((DIGITS + 1, rows + pad, LANES), F32),
        compiler_params=params(16),
        name="raise",
    )(digit, where, own, other, mats, cipher)


def accum_kernel(k, limbs, specials, pad, shifts, slot, raised, keys, diag, mats, gain, *refs):
    part, store, (acc, stage, kbuf, dbuf, sem, ksem) = refs[-10:-8], refs[-8:-6], refs[-6:]
    rows = acc.shape[1]
    pieces = ksem.shape[0]
    block = rows // pieces

    def fetch(i):
        at = pl.ds(pl.multiple_of(i * block, block), block)
        return [
            pltpu.make_async_copy(keys.at[k, :, at], kbuf.at[:, at], ksem.at[i, 0]),
            pltpu.make_async_copy(diag.at[k, at], dbuf.at[at], ksem.at[i, 1]),
        ]

    for i in range(pieces):
        for copy in fetch(i):
            copy.start()
    s = shifts[k]
    tiles, lane = s // LANES, s % LANES
    here = lax.broadcasted_iota(jnp.int32, (pad, LANES), 1) < LANES - lane
    g8 = jnp.concatenate([gain[...]] * (pad // 8), axis=0)

    def piece(i, carry):
        for copy in fetch(i):
            copy.wait()

        def add(r, carry):
            at = pl.multiple_of(i * block + r * pad, pad)
            u0 = lax.rem(at - limbs * tiles + rows, rows)
            v0 = lax.rem(at - limbs * tiles - limbs + 2 * rows, rows)
            turned = []
            for g in range(DIGITS + 1):
                u = raised[g, pl.ds(pl.multiple_of(u0, limbs), pad), :]
                v = raised[g, pl.ds(pl.multiple_of(v0, limbs), pad), :]
                turned.append(pltpu.roll(jnp.where(here, u, v), lane, axis=1))
            w = dbuf[pl.ds(at, pad), :] * g8
            for c in range(2):
                a = turned[DIGITS]
                for d in range(DIGITS):
                    a = a + turned[d] * kbuf[2 * d + c, pl.ds(at, pad), :]
                acc[c, pl.ds(at, pad), :] = a
                w_a = w * a
                part[c][pl.ds(at, pad), :] = w_a if k == 0 else refs[c][pl.ds(at, pad), :] + w_a
            return carry

        return lax.fori_loop(0, block // pad, add, carry)

    lax.fori_loop(0, pieces, piece, 0)

    def emit(m, carry):
        @pl.when(slot[m] >= 0)
        def _():
            h = (mats[m, 0], mats[m, 1])
            copies = []
            for c in range(2):
                y = spin(grid_of(acc.at[c], m, limbs), h)
                stage[c, 0:RADIX, :] = y[:, :LANES]
                stage[c, RADIX:, :] = y[:, LANES:]
                copies.append(pltpu.make_async_copy(stage.at[c], store[c].at[k * specials + slot[m]], sem.at[c]))
                copies[-1].start()
            for copy in copies:
                copy.wait()

        return carry

    lax.fori_loop(0, limbs, emit, 0)


def accum_call(k, shifts, slot, raised, keys, diag, mats, gain, specials, pad, carried=None):
    limbs = mats.shape[0]
    rows = raised.shape[1] - pad
    items = keys.shape[0] * specials
    part = jax.ShapeDtypeStruct((rows, LANES), F32)
    store = jax.ShapeDtypeStruct((items, 2 * RADIX, LANES), F32)
    args = (in_hbm(shifts), slot, raised, in_hbm(keys), in_hbm(diag), mats, gain)
    specs = [SMEM, SMEM, VMEM, HBM, HBM, VMEM, VMEM]
    alias = {}
    if carried is not None:
        carried = (*carried[:2], *map(in_hbm, carried[2:]))
        alias = {len(args) + i: i for i in range(4)}
        args += tuple(carried)
        specs += [VMEM, VMEM, HBM, HBM]
    return pl.pallas_call(
        functools.partial(accum_kernel, k, limbs, specials, pad),
        in_specs=specs,
        out_specs=[VMEM, VMEM, HBM, HBM],
        out_shape=[part, part, store, store],
        input_output_aliases=alias,
        scratch_shapes=[
            pltpu.VMEM((2, rows, LANES), F32),
            pltpu.VMEM((2, 2 * RADIX, LANES), F32),
            pltpu.VMEM(keys.shape[1:], F32),
            pltpu.VMEM((rows, LANES), F32),
            pltpu.SemaphoreType.DMA((2,)),
            pltpu.SemaphoreType.DMA((4, 2)),
        ],
        compiler_params=params(24),
        cost_estimate=pl.CostEstimate(flops=10**9, bytes_accessed=8 * 2**20, transcendentals=0),
        name="accum",
    )(*args)


def table_kernel(n, count, specials, limbs, least, order, pos, spot, plan, rounds, comp, a_ref, b_ref, end_ref):
    items = count * specials
    shape = (items, LANES)
    row_i = lax.broadcasted_iota(jnp.int32, shape, 0)
    row = row_i.astype(F32)
    lane = lax.broadcasted_iota(jnp.int32, shape, 1).astype(F32)
    kind, turn = lax.rem(row_i, specials), lax.div(row_i, specials)
    ready = jnp.maximum(2 * turn - 1, 0)
    weight = 3.0 * turn.astype(F32)
    p = spot[0]
    before, after = lax.rem(p + n - 1, n), lax.rem(p + 1, n)
    line = lax.broadcasted_iota(jnp.int32, (1, LANES), 1)
    org = jnp.zeros(shape, F32)
    for s in range(specials):
        owner = pos[lax.div(order[DIGITS * specials + s], limbs)]
        org = jnp.where(kind == s, owner.astype(F32), org)
    a_ref[...] = jnp.zeros(shape, F32)
    b_ref[...] = jnp.zeros(shape, F32)
    end_ref[...] = jnp.zeros(shape, F32)
    big = float(items * (2 * n + 3 * count))

    def choose(front, spread, t):
        open_ = jnp.logical_and(spread < n - 1, ready <= t)
        cand = jnp.logical_and(open_, front == lane)
        key = jnp.where(cand, (2.0 * spread + weight) * items + row, big)
        best = jnp.min(key, axis=0, keepdims=True)
        hit = jnp.where(jnp.logical_and(cand, key == best), 1.0, 0.0)
        item = jnp.sum(hit * (row - items), axis=0, keepdims=True) + items
        return item, jnp.sum(hit, axis=1, keepdims=True)

    def note(t, r, item, where):
        t = jnp.asarray(t, jnp.int32)
        mine = jnp.sum(jnp.where(line == where, item, 0.0), axis=1, keepdims=True)
        at = pl.ds(lax.div(PLAN * t + r, LANES), 1)
        here = line == lax.rem(PLAN * t + r, LANES)
        plan[at, :] = jnp.where(here, jnp.broadcast_to(mine, (1, LANES)).astype(jnp.int32), plan[at, :])

    none = jnp.full((1, LANES), float(items), F32)
    plan[...] = jnp.full(plan.shape, items, jnp.int32)
    note(0, 2, none, p)
    note(0, 3, none, p)

    def cond(c):
        return jnp.logical_or(c[1] > 0, c[0] < least)

    def body(c):
        t, _ = c
        a, b = a_ref[...], b_ref[...]
        front = org + a
        item, right = choose(jnp.where(front >= n, front - n, front), a + b, t)
        note(t, 0, item, p)
        note(t + 1, 2, item, before)
        a = a + right
        front = org - b
        item, left = choose(jnp.where(front < 0, front + n, front), a + b, t)
        note(t, 1, item, p)
        note(t + 1, 3, item, after)
        b = b + left
        a_ref[...] = a
        b_ref[...] = b
        end_ref[...] = jnp.where(right + left > 0, (t + 1).astype(F32), end_ref[...])
        return t + 1, jnp.sum(n - 1 - a - b).astype(jnp.int32)

    t, _ = lax.while_loop(cond, body, (jnp.int32(0), jnp.int32(1)))
    rounds[0] = t
    note(t, 0, none, p)
    note(t, 1, none, p)
    for k in range(count):
        comp[k] = jnp.max(end_ref[pl.ds(k * specials, specials), :]).astype(jnp.int32)


def table_call(n, count, specials, limbs, least, order, pos, spot):
    items = count * specials
    most = items * (n - 1) + 2 * count
    return pl.pallas_call(
        functools.partial(table_kernel, n, count, specials, limbs, least),
        in_specs=[SMEM] * 3,
        out_specs=[pl.BlockSpec(memory_space=pltpu.VMEM), SMEM, SMEM],
        out_shape=[
            jax.ShapeDtypeStruct((-(-PLAN * (most + 1) // (8 * LANES)) * 8, LANES), jnp.int32),
            jax.ShapeDtypeStruct((1,), jnp.int32),
            jax.ShapeDtypeStruct((count,), jnp.int32),
        ],
        scratch_shapes=[pltpu.VMEM((items, LANES), F32)] * 3,
        compiler_params=params(8),
        name="table",
    )(order, in_hbm(pos), spot)


def round_of(tile, t):
    got = [tile[lax.div(f, LANES), lax.rem(f, LANES)] for f in (jnp.asarray(PLAN * t + r, jnp.int32) for r in range(PLAN))]
    return got[:2], got[2:]


def pack_kernel(items, t, first, last, *refs):
    refs = list(refs)
    if t is None:
        t = refs.pop(0)[0]
    table, store = refs.pop(0), refs.pop(0)
    ins = () if first else (refs.pop(0), refs.pop(0))
    refs.pop(0)
    outs = () if last else (refs.pop(0), refs.pop(0))
    tile, keep, send, tsem = refs
    plan = pltpu.make_async_copy(table, tile, tsem)
    plan.start()
    plan.wait()
    go, came = round_of(tile, t)
    for i in range(len(ins)):
        @pl.when(came[i] < items)
        def _():
            pltpu.make_async_copy(ins[i], store.at[came[i]], keep.at[i]).start()

    old = []
    for j in range(len(outs)):
        fresh = [jnp.logical_and(go[j] == came[i], came[i] < items) for i in range(len(ins))]
        held = go[j] < items
        for f in fresh:
            held = jnp.logical_and(held, jnp.logical_not(f))
        old.append(held)

        @pl.when(held)
        def _():
            pltpu.make_async_copy(store.at[go[j]], outs[j], send.at[j]).start()

        for i in range(len(ins)):
            @pl.when(fresh[i])
            def _():
                outs[j][...] = ins[i][...]

    for i in range(len(ins)):
        @pl.when(came[i] < items)
        def _():
            pltpu.make_async_copy(ins[i], store.at[came[i]], keep.at[i]).wait()
    for j in range(len(outs)):
        @pl.when(old[j])
        def _():
            pltpu.make_async_copy(store.at[go[j]], outs[j], send.at[j]).wait()


def pack_call(table, t, store, ins=None, last=False):
    first = ins is None
    store = in_hbm(store)
    items = store.shape[0]
    item = jax.ShapeDtypeStruct(store.shape[1:], store.dtype)
    static = isinstance(t, int)
    args = (() if static else (t.reshape(1),)) + (table, store) + (() if first else tuple(ins))
    at = 1 if static else 2
    outs = [jax.ShapeDtypeStruct(store.shape, store.dtype)] + ([] if last else [item, item])
    size = math.prod(item.shape) * 4
    res = pl.pallas_call(
        functools.partial(pack_kernel, items, t if static else None, first, last),
        in_specs=([] if static else [SMEM]) + [ANY, HBM] + [VMEM] * (0 if first else 2),
        out_specs=[HBM] + [VMEM] * (len(outs) - 1),
        out_shape=outs,
        input_output_aliases={at: 0},
        scratch_shapes=[
            pltpu.SMEM(table.shape, jnp.int32),
            pltpu.SemaphoreType.DMA((2,)),
            pltpu.SemaphoreType.DMA((2,)),
            pltpu.SemaphoreType.DMA,
        ],
        compiler_params=params(2),
        cost_estimate=pl.CostEstimate(flops=0, bytes_accessed=8 * size, transcendentals=0),
        name="pack",
    )(*args)
    return res[0], list(res[1:])


def lower_kernel(low, high, specials, limbs, *refs):
    order, digit, where, scale, conv, comp, diag, mats, *refs = refs
    part, store, refs = refs[:2], refs[2:4], refs[4:]
    last = high is None
    if last:
        t, plan, *refs = refs
        ins, store, keep, send, refs = (refs[0:2], refs[2:4]), refs[4:6], refs[6:8], refs[8:10], refs[10:]
        total, got, dg, xs, sem, tile = refs
        total = [total.at[0], total.at[1]]
        copy = pltpu.make_async_copy(plan, tile, sem.at[0])
        copy.start()
        copy.wait()
        _, came = round_of(tile, t[0])

        def arrive(act):
            for c in range(2):
                for i in range(2):
                    @pl.when(came[i] < store[c].shape[0])
                    def _():
                        act(pltpu.make_async_copy(ins[c][i], store[c].at[came[i]], sem.at[2 * c + i]))

        arrive(lambda copy: copy.start())
        arrive(lambda copy: copy.wait())
    else:
        total, (got, dg, xs, sem) = refs[:2], refs[4:]
    count = diag.shape[0]
    first = where[0] * limbs
    for c in range(2):
        total[c][...] = part[c][...]

    def turn(k, carry):
        ripe = comp[k] > low
        if not last:
            ripe = jnp.logical_and(ripe, comp[k] <= high)

        @pl.when(ripe)
        def _():
            items = [
                pltpu.make_async_copy(store[c].at[pl.ds(k * specials, specials)], got.at[c], sem.at[c])
                for c in range(2)
            ]
            weigh = pltpu.make_async_copy(diag.at[k], dg, sem.at[2])
            items[0].start()
            weigh.start()
            items[1].start()
            items[0].wait()
            weigh.wait()
            for c in range(2):
                if c:
                    items[c].wait()

                def limb(m, carry):
                    q = first + m

                    @pl.when(digit[q] != DIGITS)
                    def _():
                        h = (mats[m, 0], mats[m, 1])
                        w = [conv[q, order[DIGITS * specials + s]] for s in range(specials)]
                        size = scale[q]
                        step = 64
                        for i in range(2):
                            for r in range(0, RADIX, step):
                                x = w[0] * got[c, 0, pl.ds(i * RADIX + r, step), :]
                                for s in range(1, specials):
                                    x = x + w[s] * got[c, s, pl.ds(i * RADIX + r, step), :]
                                hi, lo = split(x)
                                xs[0, pl.ds(r, step), pl.ds(i * LANES, LANES)] = hi
                                xs[1, pl.ds(r, step), pl.ds(i * LANES, LANES)] = lo
                        y = mm(h, split(mm((xs[0], xs[1]), h)))
                        for i in range(2):
                            at = pl.ds(i * limbs + m, RADIX, stride=2 * limbs)
                            total[c][at, :] = total[c][at, :] - dg[at, :] * size * y[:, i * LANES : (i + 1) * LANES]

                    return carry

                lax.fori_loop(0, limbs, limb, 0)

        return carry

    lax.fori_loop(0, count, turn, 0)
    if last:
        half = total[0].shape[0] // 2
        mine = where[1]
        for c in range(2):
            keep[c][...] = total[c][pl.ds(pl.multiple_of(mine * half, half), half), :]
            send[c][...] = total[c][pl.ds(pl.multiple_of((1 - mine) * half, half), half), :]


def lower_call(low, high, order, digit, where, scale, conv, comp, diag, mats, specials, part, store, end=()):
    limbs = mats.shape[0]
    store = [in_hbm(s) for s in store]
    rows = part[0].shape[0]
    half = jax.ShapeDtypeStruct((rows // 2, LANES), F32)
    last = high is None
    shape = lambda a: jax.ShapeDtypeStruct(a.shape, a.dtype)
    scratch = [
        pltpu.VMEM((2, specials, 2 * RADIX, LANES), F32),
        pltpu.VMEM((rows, LANES), F32),
        pltpu.VMEM((2, RADIX, RADIX), BF16),
        pltpu.SemaphoreType.DMA((4,)),
    ]
    if last:
        scratch = [pltpu.VMEM((2, rows, LANES), F32)] + scratch + [pltpu.SMEM(end[1].shape, jnp.int32)]
    return pl.pallas_call(
        functools.partial(lower_kernel, low, high, specials, limbs),
        in_specs=[SMEM] * 6 + [HBM, VMEM, VMEM, VMEM, HBM, HBM] + ([SMEM, ANY] + [VMEM] * 4 if last else []),
        out_specs=[HBM, HBM] + [VMEM] * 4 if last else [VMEM, VMEM, HBM, HBM],
        out_shape=[shape(s) for s in store] + [half] * 4 if last else [shape(p) for p in (*part, *store)],
        input_output_aliases={10: 0, 11: 1} if last else {10: 2, 11: 3},
        scratch_shapes=scratch,
        compiler_params=params(24),
        cost_estimate=pl.CostEstimate(flops=10**9, bytes_accessed=8 * 2**20, transcendentals=0),
        name="lower",
    )(order, in_hbm(digit), where, scale, in_hbm(conv), comp, in_hbm(diag), mats, *part, *store, *end)


def interleave(x):
    *lead, limbs, coeffs = x.shape
    x = x.reshape(*lead, limbs, coeffs // LANES, LANES)
    return jnp.swapaxes(x, -3, -2).reshape(*lead, coeffs // LANES * limbs, LANES)


def per_device(order_of, cipher, rotation_keys, diagonals, shifts, twiddles, moduli, digit_of, conversion):
    n = len(order_of)
    limbs = cipher.shape[0]
    ext = digit_of.shape[0]
    specials = ext // (DIGITS + 1)
    count = rotation_keys.shape[1]
    items = count * specials
    pos_of = np.argsort(np.array(order_of)).astype(np.int32)
    cw = [(order_of[i], order_of[(i + 1) % n]) for i in range(n)]
    ccw = [(b, a) for a, b in cw]
    me, rot = lax.axis_index("limb"), lax.axis_index("rot")
    where = jnp.stack([me, rot]).astype(jnp.int32)
    pos = jnp.asarray(pos_of)
    my_pos = pos[me]
    swap = lambda x: lax.ppermute(x, "rot", [(0, 1), (1, 0)])

    grid = np.arange(RADIX)
    angle = (grid[:, None] * grid[None, :] % RADIX) * (2.0 * math.pi / RADIX)
    base = ((np.cos(angle) + np.sin(angle)) / math.sqrt(RADIX)).astype(np.float32)
    base_hi = base.astype(BF16)
    base_lo = (base - base_hi.astype(np.float32)).astype(BF16)

    rows_c = interleave(cipher)
    keys = interleave(rotation_keys).reshape(count, DIGITS * 2, -1, LANES)
    diag = interleave(diagonals).reshape(count, -1, LANES)

    coef, mats = coef_call(twiddles, where, jnp.asarray(base_hi), jnp.asarray(base_lo), rows_c, limbs)

    ids = jnp.arange(ext, dtype=jnp.int32)
    before = (digit_of[None, :] < digit_of[:, None]) | (
        (digit_of[None, :] == digit_of[:, None]) & (ids[None, :] < ids[:, None])
    )
    place = jnp.sum(before.astype(jnp.int32), axis=1)
    order = jnp.sum(jnp.where(place[None, :] == ids[:, None], ids[None, :], 0), axis=1)
    slot = lax.dynamic_slice_in_dim(jnp.maximum(place - DIGITS * specials, -1), me * limbs, limbs, 0)
    special = digit_of == DIGITS
    mod = moduli.astype(F32)
    scale = jnp.sum(jnp.where(special[None, :], mod[:, None] / mod[None, :], 0.0), axis=1) / specials
    my_special = lax.dynamic_slice_in_dim(special, me * limbs, limbs, 0)
    my_gain = jnp.where(my_special, 1.0, lax.dynamic_slice_in_dim(scale, me * limbs, limbs, 0))
    rows8 = lambda v: jnp.broadcast_to(jnp.tile(v, 8 // limbs)[:, None], (8, LANES))
    gain = rows8(my_gain)
    fixed = items * n // (2 * n)
    plan, rounds, comp = table_call(n, count, specials, limbs, fixed, order, pos, my_pos.reshape(1))

    blocks, lens, steps = [coef], [(0, limbs)], [0]
    right, left = coef, coef
    both = (n - 1) // 2
    for r in range(1, both + 1):
        right, left = lax.ppermute(right, "limb", cw), lax.ppermute(left, "limb", ccw)
        blocks += [right, left]
        lens += [(0, limbs)] * 2
        steps += [-r, r]
        if r == 2:
            right, left, order, slot, gain, scale, plan, rounds, comp = lax.optimization_barrier(
                (right, left, order, slot, gain, scale, plan, rounds, comp)
            )
    if n % 2 == 0:
        cut = limbs // 2
        blocks += [lax.ppermute(right[:cut], "limb", cw), lax.ppermute(left[cut:], "limb", ccw)]
        lens += [(0, cut), (cut, limbs)]
        steps += [n // 2, n // 2]
    srcs = jnp.asarray(
        np.array([[order_of[(pos_of[d] + s) % n] for s in steps] for d in range(n)], np.int32)
    )[me]

    pad = 64
    mixed = mix_call(n, limbs, tuple(lens), order, digit_of, where, srcs, conversion, blocks)
    raised = raise_call(digit_of, where, mixed, swap(mixed), mats, rows_c, pad)

    def accumulate(k, carried=None):
        return accum_call(k, shifts.reshape(-1), slot, raised, keys, diag, mats, gain, specials, pad, carried)

    def lower(low, high, end=()):
        return lower_call(
            low, high, order, digit_of, where, scale, conversion, comp, diag, mats, specials, part, stores, end
        )

    def travel(sends):
        return [lax.ppermute(sends[0], "limb", cw), lax.ppermute(sends[1], "limb", ccw)]

    ready = {max(2 * k - 1, 0): k for k in range(1, count)}
    gates = [fixed - 5, fixed - 3, fixed - 1]
    part, stores = [None, None], [None, None]
    *part, stores[0], stores[1] = accumulate(0)
    ins = [None, None]
    low = -1
    for t in range(fixed):
        if t in ready:
            *part, stores[0], stores[1] = accumulate(ready[t], (*part, *stores))
        for c in range(2):
            stores[c], sends = pack_call(plan, t, stores[c], ins[c])
            ins[c] = travel(sends)
        if t in gates:
            *part, stores[0], stores[1] = lower(low, t)
            low = t

    def more(state):
        return state[0] < rounds[0]

    def one(state):
        t, stores, ins = state
        stores, ins = list(stores), list(ins)
        for c in range(2):
            stores[c], sends = pack_call(plan, t, stores[c], ins[c])
            ins[c] = travel(sends)
        return t + 1, stores, ins

    t, stores, ins = lax.while_loop(more, one, (jnp.int32(fixed), stores, ins))
    _, _, *halves = lower(low, None, (t.reshape(1), plan, *ins[0], *ins[1]))
    total = jnp.stack([keep + swap(send) for keep, send in zip(halves[:2], halves[2:])])
    total = jnp.swapaxes(total.reshape(2, -1, limbs, LANES), 1, 2)
    return total.reshape(2, limbs, -1)


def solution(mesh):
    in_specs = (
        P(("parts", "limb"), None),
        P("rot", None, None, None, "limb", None),
        P("rot", None, "limb", None),
        P("rot", None),
        P(),
        P(),
        P(),
        P(),
    )
    out_specs = P(None, ("parts", "limb"), "rot")
    return jax.shard_map(
        functools.partial(per_device, ring_order(mesh)),
        mesh=mesh,
        in_specs=in_specs,
        out_specs=out_specs,
        check_vma=False,
    )
```

```python
import functools
import math

import jax
import jax.numpy as jnp
import numpy as np
from jax import lax
from jax.experimental import pallas as pl
from jax.experimental.pallas import tpu as pltpu
from jax.sharding import PartitionSpec as P

RADIX = 256
DIGITS = 3
LANES = 128
PLAN = 4
F32 = jnp.float32
BF16 = jnp.bfloat16


ANY = pl.BlockSpec(memory_space=pl.ANY)
VMEM = pl.BlockSpec(memory_space=pltpu.VMEM)
HBM = pl.BlockSpec(memory_space=pltpu.HBM)
SMEM = pl.BlockSpec(memory_space=pltpu.SMEM)


def ring_order(mesh):
    n = mesh.shape["limb"]
    line = np.moveaxis(mesh.devices, list(mesh.axis_names).index("limb"), 0).reshape(n, -1)[:, 0]
    at = [getattr(d, "coords", None) for d in line]
    if any(c is None for c in at):
        return list(range(n))
    near = [
        [j for j in range(n) if sum(abs(x - y) for x, y in zip(at[i], at[j])) == 1] for i in range(n)
    ]

    def walk(path):
        if len(path) == n:
            return path if 0 in near[path[-1]] else None
        for j in near[path[-1]]:
            if j not in path:
                found = walk(path + [j])
                if found:
                    return found
        return None

    return walk([0]) or list(range(n))


def split(x):
    hi = x.astype(BF16)
    return hi, (x - hi.astype(F32)).astype(BF16)


def mm(a, b):
    dot = functools.partial(jnp.dot, preferred_element_type=F32)
    return dot(a[0], b[0]) + dot(a[1], b[0]) + dot(a[0], b[1])


def spin(x, h):
    return mm(h, split(mm(split(x), h)))


def grid_of(ref, m, limbs):
    left = ref[pl.ds(m, RADIX, stride=2 * limbs), :]
    right = ref[pl.ds(limbs + m, RADIX, stride=2 * limbs), :]
    return jnp.concatenate([left, right], axis=1)


def in_hbm(x):
    return pltpu.with_memory_space_constraint(x, pltpu.HBM)


def params(mib):
    return pltpu.CompilerParams(vmem_limit_bytes=mib * 2**20)


def coef_kernel(tw, where, base_hi, base_lo, cipher, coef0, coef1, mats, grid, bases, sem):
    limbs = mats.shape[0]
    cut = coef0.shape[0]
    copies = [
        pltpu.make_async_copy(base_hi, bases.at[0], sem.at[0]),
        pltpu.make_async_copy(base_lo, bases.at[1], sem.at[1]),
        pltpu.make_async_copy(cipher, grid, sem.at[2]),
    ]
    for copy in copies:
        copy.start()
    row = lax.broadcasted_iota(jnp.int32, (RADIX, RADIX), 0)
    col = lax.broadcasted_iota(jnp.int32, (RADIX, RADIX), 1)
    first = where[1] == 0
    for copy in copies:
        copy.wait()

    def limb(coef, start, m, carry):
        g = tw[where[0] * limbs + m]
        pick = jnp.where(((row * g) & (RADIX - 1)) == col, 1.0, 0.0).astype(BF16)
        hi = jnp.dot(pick, bases[0], preferred_element_type=F32).astype(BF16)
        lo = jnp.dot(pick, bases[1], preferred_element_type=F32).astype(BF16)
        mats[m, 0] = hi
        mats[m, 1] = lo
        u = split(mm((hi, lo), split(grid_of(grid, m, limbs))))
        half = tuple(
            jnp.where(first, h[:, :LANES].astype(F32), h[:, LANES:].astype(F32)).astype(BF16) for h in (hi, lo)
        )
        coef[m - start] = mm(u, half)
        return carry

    lax.fori_loop(0, cut, functools.partial(limb, coef0, 0), 0)
    lax.fori_loop(cut, limbs, functools.partial(limb, coef1, cut), 0)


def coef_call(tw, where, base_hi, base_lo, cipher, limbs):
    return pl.pallas_call(
        coef_kernel,
        in_specs=[SMEM, SMEM, HBM, HBM, HBM],
        out_specs=[VMEM, VMEM, VMEM],
        out_shape=[
            jax.ShapeDtypeStruct((limbs // 2, RADIX, LANES), F32),
            jax.ShapeDtypeStruct((limbs - limbs // 2, RADIX, LANES), F32),
            jax.ShapeDtypeStruct((limbs, 2, RADIX, RADIX), BF16),
        ],
        scratch_shapes=[
            pltpu.VMEM(cipher.shape, F32),
            pltpu.VMEM((2, RADIX, RADIX), BF16),
            pltpu.SemaphoreType.DMA((3,)),
        ],
        compiler_params=params(12),
        name="coef",
    )(in_hbm(tw), where, in_hbm(base_hi), in_hbm(base_lo), in_hbm(cipher))


def mix_kernel(n, limbs, lens, order, digit, where, srcs, conv, *refs):
    blocks, out, got, table, sem = refs[: len(lens)], refs[-4], refs[-3], refs[-2], refs[-1]
    size = got.shape[0] * limbs // (DIGITS + 1)
    copies = []
    for i, (start, stop) in enumerate(lens):
        c = pltpu.make_async_copy(blocks[i], got.at[srcs[i], pl.ds(start, stop - start)], sem.at[i])
        c.start()
        copies.append(c)
    first = where[0] * limbs
    for j in range(DIGITS * size):
        l = order[j]
        for m in range(limbs):
            same = digit[l] == digit[first + m]
            one = jnp.where(first + m == l, 1.0, 0.0)
            table[m, j] = jnp.where(same, one, conv[first + m, l])
    for c in copies:
        c.wait()
    step = 64

    def rows(r, carry):
        r0 = pl.multiple_of(r * step, step)
        for d in range(DIGITS):
            acc = [jnp.zeros((step, LANES), F32) for _ in range(limbs)]
            for j in range(size):
                l = order[d * size + j]
                x = got[l // limbs, l % limbs, pl.ds(r0, step), :]
                for m in range(limbs):
                    acc[m] = acc[m] + table[m, d * size + j] * x
            for m in range(limbs):
                out[d, m, pl.ds(r0, step), :] = acc[m]
        return carry

    lax.fori_loop(0, RADIX // step, rows, 0)


def mix_call(n, limbs, lens, order, digit, where, srcs, conv, blocks):
    vmem = pl.BlockSpec(memory_space=pltpu.VMEM)
    return pl.pallas_call(
        functools.partial(mix_kernel, n, limbs, lens),
        in_specs=[SMEM] * 5 + [HBM] * len(blocks),
        out_specs=vmem,
        out_shape=jax.ShapeDtypeStruct((DIGITS, limbs, RADIX, LANES), F32),
        scratch_shapes=[
            pltpu.VMEM((n, limbs, RADIX, LANES), F32),
            pltpu.SMEM((limbs, n * limbs), F32),
            pltpu.SemaphoreType.DMA((len(blocks),)),
        ],
        compiler_params=params(16),
        name="mix",
    )(order, in_hbm(digit), where, srcs, in_hbm(conv), *blocks)


def raise_kernel(pad, digit, where, own, other, mats, cipher, out, rows_in, sem):
    limbs = mats.shape[0]
    rows = cipher.shape[0]
    swapped = where[1] != 0
    fetch = pltpu.make_async_copy(cipher, rows_in, sem)
    fetch.start()

    def known(d, m):
        return digit[where[0] * limbs + m] == d

    def at(m, h):
        return pl.ds(h * limbs + m, RADIX, stride=2 * limbs)

    def convert(i, carry):
        d, m = lax.div(i, limbs), lax.rem(i, limbs)

        @pl.when(jnp.logical_not(known(d, m)))
        def _():
            a, b = own[d, m], other[d, m]
            x = jnp.concatenate([jnp.where(swapped, b, a), jnp.where(swapped, a, b)], axis=1)
            y = spin(x, (mats[m, 0], mats[m, 1]))
            for h in range(2):
                out[d, at(m, h), :] = y[:, h * LANES : (h + 1) * LANES]

        return carry

    lax.fori_loop(0, DIGITS * limbs, convert, 0)
    fetch.wait()

    def place(m, carry):
        d = digit[where[0] * limbs + m]
        for h in range(2):
            out[d, at(m, h), :] = rows_in[at(m, h), :]

        @pl.when(d != DIGITS)
        def _():
            for h in range(2):
                out[DIGITS, at(m, h), :] = jnp.zeros((RADIX, LANES), F32)

        return carry

    lax.fori_loop(0, limbs, place, 0)
    for d in range(DIGITS + 1):
        out[d, pl.ds(rows, pad), :] = out[d, pl.ds(0, pad), :]


def raise_call(digit, where, own, other, mats, cipher, pad):
    rows = cipher.shape[0]
    return pl.pallas_call(
        functools.partial(raise_kernel, pad),
        in_specs=[SMEM, SMEM] + [VMEM] * 3 + [HBM],
        out_specs=VMEM,
        out_shape=jax.ShapeDtypeStruct((DIGITS + 1, rows + pad, LANES), F32),
        scratch_shapes=[pltpu.VMEM(cipher.shape, F32), pltpu.SemaphoreType.DMA],
        compiler_params=params(16),
        name="raise",
    )(in_hbm(digit), where, own, other, mats, in_hbm(cipher))


def accum_kernel(k, c, limbs, specials, pad, shifts, slot, raised, keys, diag, mats, gain, *refs):
    part, store, acc, stage, kbuf, dbuf, sem, ksem = refs[-8:]
    rows = acc.shape[0]
    pieces = ksem.shape[0]
    block = rows // pieces

    def fetch(i):
        at = pl.ds(pl.multiple_of(i * block, block), block)
        return [
            pltpu.make_async_copy(keys.at[k, :, c, at], kbuf.at[:, at], ksem.at[i, 0]),
            pltpu.make_async_copy(diag.at[k, at], dbuf.at[at], ksem.at[i, 1]),
        ]

    for i in range(pieces):
        for copy in fetch(i):
            copy.start()
    s = shifts[k]
    tiles, lane = s // LANES, s % LANES
    here = lax.broadcasted_iota(jnp.int32, (pad, LANES), 1) < LANES - lane
    g8 = jnp.concatenate([gain[...]] * (pad // 8), axis=0)

    def piece(i, carry):
        for copy in fetch(i):
            copy.wait()

        def add(r, carry):
            at = pl.multiple_of(i * block + r * pad, pad)
            u0 = lax.rem(at - limbs * tiles + rows, rows)
            v0 = lax.rem(at - limbs * tiles - limbs + 2 * rows, rows)
            a = None
            for g in range(DIGITS, -1, -1):
                u = raised[g, pl.ds(pl.multiple_of(u0, limbs), pad), :]
                v = raised[g, pl.ds(pl.multiple_of(v0, limbs), pad), :]
                x = pltpu.roll(jnp.where(here, u, v), lane, axis=1)
                a = x if g == DIGITS else a + x * kbuf[g, pl.ds(at, pad), :]
            acc[pl.ds(at, pad), :] = a
            w_a = dbuf[pl.ds(at, pad), :] * g8 * a
            part[pl.ds(at, pad), :] = w_a if k == 0 else refs[0][pl.ds(at, pad), :] + w_a
            return carry

        return lax.fori_loop(0, block // pad, add, carry)

    lax.fori_loop(0, pieces, piece, 0)

    def emit(m, carry):
        @pl.when(slot[m] >= 0)
        def _():
            y = spin(grid_of(acc, m, limbs), (mats[m, 0], mats[m, 1]))
            stage[0:RADIX, :] = y[:, :LANES]
            stage[RADIX:, :] = y[:, LANES:]
            copy = pltpu.make_async_copy(stage, store.at[k * specials + slot[m]], sem)
            copy.start()
            copy.wait()

        return carry

    lax.fori_loop(0, limbs, emit, 0)


def accum_call(k, c, shifts, slot, raised, keys, diag, mats, gain, specials, pad, part, store):
    limbs = mats.shape[0]
    rows = raised.shape[1] - pad
    items = keys.shape[0] * specials
    args = (in_hbm(shifts), slot, raised, in_hbm(keys), in_hbm(diag), mats, gain)
    specs = [SMEM, SMEM, VMEM, HBM, HBM, VMEM, VMEM]
    alias = {}
    if part is not None:
        alias = {len(args): 0, len(args) + 1: 1}
        args += (part, in_hbm(store))
        specs += [VMEM, HBM]
    return pl.pallas_call(
        functools.partial(accum_kernel, k, c, limbs, specials, pad),
        in_specs=specs,
        out_specs=[VMEM, HBM],
        out_shape=[
            jax.ShapeDtypeStruct((rows, LANES), F32),
            jax.ShapeDtypeStruct((items, 2 * RADIX, LANES), F32),
        ],
        input_output_aliases=alias,
        scratch_shapes=[
            pltpu.VMEM((rows, LANES), F32),
            pltpu.VMEM((2 * RADIX, LANES), F32),
            pltpu.VMEM((DIGITS, rows, LANES), F32),
            pltpu.VMEM((rows, LANES), F32),
            pltpu.SemaphoreType.DMA,
            pltpu.SemaphoreType.DMA((4, 2)),
        ],
        compiler_params=params(16),
        cost_estimate=pl.CostEstimate(flops=5 * 10**8, bytes_accessed=4 * 2**20, transcendentals=0),
        name="accum",
    )(*args)


def table_kernel(n, count, specials, limbs, least, order, pos, spot, plan, rounds, comp, a_ref, b_ref, end_ref):
    items = count * specials
    shape = (items, LANES)
    row_i = lax.broadcasted_iota(jnp.int32, shape, 0)
    row = row_i.astype(F32)
    lane = lax.broadcasted_iota(jnp.int32, shape, 1).astype(F32)
    kind, turn = lax.rem(row_i, specials), lax.div(row_i, specials)
    ready = jnp.maximum(2 * turn - 1, 0)
    weight = 3.0 * turn.astype(F32)
    p = spot[0]
    before, after = lax.rem(p + n - 1, n), lax.rem(p + 1, n)
    line = lax.broadcasted_iota(jnp.int32, (1, LANES), 1)
    org = jnp.zeros(shape, F32)
    for s in range(specials):
        owner = pos[lax.div(order[DIGITS * specials + s], limbs)]
        org = jnp.where(kind == s, owner.astype(F32), org)
    a_ref[...] = jnp.zeros(shape, F32)
    b_ref[...] = jnp.zeros(shape, F32)
    end_ref[...] = jnp.zeros(shape, F32)
    big = float(items * (2 * n + 3 * count))

    def choose(front, spread, t):
        open_ = jnp.logical_and(spread < n - 1, ready <= t)
        cand = jnp.logical_and(open_, front == lane)
        key = jnp.where(cand, (2.0 * spread + weight) * items + row, big)
        best = jnp.min(key, axis=0, keepdims=True)
        hit = jnp.where(jnp.logical_and(cand, key == best), 1.0, 0.0)
        item = jnp.sum(hit * (row - items), axis=0, keepdims=True) + items
        return item, jnp.sum(hit, axis=1, keepdims=True)

    def note(t, r, item, where):
        t = jnp.asarray(t, jnp.int32)
        mine = jnp.sum(jnp.where(line == where, item, 0.0), axis=1, keepdims=True)
        at = pl.ds(lax.div(PLAN * t + r, LANES), 1)
        here = line == lax.rem(PLAN * t + r, LANES)
        plan[at, :] = jnp.where(here, jnp.broadcast_to(mine, (1, LANES)).astype(jnp.int32), plan[at, :])

    none = jnp.full((1, LANES), float(items), F32)
    plan[...] = jnp.full(plan.shape, items, jnp.int32)
    note(0, 2, none, p)
    note(0, 3, none, p)

    def cond(c):
        return jnp.logical_or(c[1] > 0, c[0] < least)

    def body(c):
        t, _ = c
        a, b = a_ref[...], b_ref[...]
        front = org + a
        item, right = choose(jnp.where(front >= n, front - n, front), a + b, t)
        note(t, 0, item, p)
        note(t + 1, 2, item, before)
        a = a + right
        front = org - b
        item, left = choose(jnp.where(front < 0, front + n, front), a + b, t)
        note(t, 1, item, p)
        note(t + 1, 3, item, after)
        b = b + left
        a_ref[...] = a
        b_ref[...] = b
        end_ref[...] = jnp.where(right + left > 0, (t + 1).astype(F32), end_ref[...])
        return t + 1, jnp.sum(n - 1 - a - b).astype(jnp.int32)

    t, _ = lax.while_loop(cond, body, (jnp.int32(0), jnp.int32(1)))
    rounds[0] = t
    note(t, 0, none, p)
    note(t, 1, none, p)
    for k in range(count):
        comp[k] = jnp.max(end_ref[pl.ds(k * specials, specials), :]).astype(jnp.int32)


def table_call(n, count, specials, limbs, least, order, pos, spot):
    items = count * specials
    most = items * (n - 1) + 2 * count
    return pl.pallas_call(
        functools.partial(table_kernel, n, count, specials, limbs, least),
        in_specs=[SMEM] * 3,
        out_specs=[pl.BlockSpec(memory_space=pltpu.VMEM), SMEM, SMEM],
        out_shape=[
            jax.ShapeDtypeStruct((-(-PLAN * (most + 1) // (8 * LANES)) * 8, LANES), jnp.int32),
            jax.ShapeDtypeStruct((1,), jnp.int32),
            jax.ShapeDtypeStruct((count,), jnp.int32),
        ],
        scratch_shapes=[pltpu.VMEM((items, LANES), F32)] * 3,
        compiler_params=params(8),
        name="table",
    )(order, in_hbm(pos), spot)


def round_of(tile, t):
    got = [tile[lax.div(f, LANES), lax.rem(f, LANES)] for f in (jnp.asarray(PLAN * t + r, jnp.int32) for r in range(PLAN))]
    return got[:2], got[2:]


def pack_kernel(items, t, first, last, *refs):
    refs = list(refs)
    if t is None:
        t = refs.pop(0)[0]
    table, store = refs.pop(0), refs.pop(0)
    ins = () if first else (refs.pop(0), refs.pop(0))
    refs.pop(0)
    outs = () if last else (refs.pop(0), refs.pop(0))
    tile, keep, send, tsem = refs
    plan = pltpu.make_async_copy(table, tile, tsem)
    plan.start()
    plan.wait()
    go, came = round_of(tile, t)
    for i in range(len(ins)):
        @pl.when(came[i] < items)
        def _():
            pltpu.make_async_copy(ins[i], store.at[came[i]], keep.at[i]).start()

    old = []
    for j in range(len(outs)):
        fresh = [jnp.logical_and(go[j] == came[i], came[i] < items) for i in range(len(ins))]
        held = go[j] < items
        for f in fresh:
            held = jnp.logical_and(held, jnp.logical_not(f))
        old.append(held)

        @pl.when(held)
        def _():
            pltpu.make_async_copy(store.at[go[j]], outs[j], send.at[j]).start()

        for i in range(len(ins)):
            @pl.when(fresh[i])
            def _():
                outs[j][...] = ins[i][...]

    for i in range(len(ins)):
        @pl.when(came[i] < items)
        def _():
            pltpu.make_async_copy(ins[i], store.at[came[i]], keep.at[i]).wait()
    for j in range(len(outs)):
        @pl.when(old[j])
        def _():
            pltpu.make_async_copy(store.at[go[j]], outs[j], send.at[j]).wait()


def pack_call(table, t, store, ins=None, last=False):
    first = ins is None
    store = in_hbm(store)
    items = store.shape[0]
    item = jax.ShapeDtypeStruct(store.shape[1:], store.dtype)
    static = isinstance(t, int)
    args = (() if static else (t.reshape(1),)) + (table, store) + (() if first else tuple(ins))
    at = 1 if static else 2
    outs = [jax.ShapeDtypeStruct(store.shape, store.dtype)] + ([] if last else [item, item])
    size = math.prod(item.shape) * 4
    res = pl.pallas_call(
        functools.partial(pack_kernel, items, t if static else None, first, last),
        in_specs=([] if static else [SMEM]) + [ANY, HBM] + [VMEM] * (0 if first else 2),
        out_specs=[HBM] + [VMEM] * (len(outs) - 1),
        out_shape=outs,
        input_output_aliases={at: 0},
        scratch_shapes=[
            pltpu.SMEM(table.shape, jnp.int32),
            pltpu.SemaphoreType.DMA((2,)),
            pltpu.SemaphoreType.DMA((2,)),
            pltpu.SemaphoreType.DMA,
        ],
        compiler_params=params(2),
        cost_estimate=pl.CostEstimate(flops=0, bytes_accessed=8 * size, transcendentals=0),
        name="pack",
    )(*args)
    return res[0], list(res[1:])


def lower_kernel(low, high, specials, limbs, *refs):
    order, digit, where, scale, conv, comp, diag, mats, part, store, *refs = refs
    last = high is None
    if last:
        t, plan, in0, in1, store, keep, send, total, got, dg, xs, sem, tile = refs
        copy = pltpu.make_async_copy(plan, tile, sem.at[0])
        copy.start()
        copy.wait()
        _, came = round_of(tile, t[0])

        def arrive(act):
            for i, ref in enumerate((in0, in1)):
                @pl.when(came[i] < store.shape[0])
                def _():
                    act(pltpu.make_async_copy(ref, store.at[came[i]], sem.at[i]))

        arrive(lambda copy: copy.start())
        arrive(lambda copy: copy.wait())
    else:
        total, _, got, dg, xs, sem = refs
    count = diag.shape[0]
    first = where[0] * limbs

    def ripe(k):
        due = comp[k] > low
        return due if last else jnp.logical_and(due, comp[k] <= high)

    total[...] = part[...]

    def turn(k, carry):
        @pl.when(ripe(k))
        def _():
            copies = [
                pltpu.make_async_copy(store.at[pl.ds(k * specials, specials)], got, sem.at[0]),
                pltpu.make_async_copy(diag.at[k], dg, sem.at[1]),
            ]
            for copy in copies:
                copy.start()
            for copy in copies:
                copy.wait()

            def limb(m, carry):
                q = first + m

                @pl.when(digit[q] != DIGITS)
                def _():
                    h = (mats[m, 0], mats[m, 1])
                    w = [conv[q, order[DIGITS * specials + s]] for s in range(specials)]
                    size = scale[q]
                    step = 64
                    for i in range(2):
                        for r in range(0, RADIX, step):
                            x = w[0] * got[0, pl.ds(i * RADIX + r, step), :]
                            for s in range(1, specials):
                                x = x + w[s] * got[s, pl.ds(i * RADIX + r, step), :]
                            hi, lo = split(x)
                            xs[0, pl.ds(r, step), pl.ds(i * LANES, LANES)] = hi
                            xs[1, pl.ds(r, step), pl.ds(i * LANES, LANES)] = lo
                    y = mm(h, split(mm((xs[0], xs[1]), h)))
                    for i in range(2):
                        at = pl.ds(i * limbs + m, RADIX, stride=2 * limbs)
                        total[at, :] = total[at, :] - dg[at, :] * size * y[:, i * LANES : (i + 1) * LANES]

                return carry

            lax.fori_loop(0, limbs, limb, 0)

        return carry

    lax.fori_loop(0, count, turn, 0)
    if last:
        half = total.shape[0] // 2
        mine = where[1]
        keep[...] = total[pl.ds(pl.multiple_of(mine * half, half), half), :]
        send[...] = total[pl.ds(pl.multiple_of((1 - mine) * half, half), half), :]


def lower_call(low, high, order, digit, where, scale, conv, comp, diag, mats, specials, part, store, end=()):
    limbs = mats.shape[0]
    store = in_hbm(store)
    rows = part.shape[0]
    half = jax.ShapeDtypeStruct((rows // 2, LANES), F32)
    last = high is None
    shape = lambda a: jax.ShapeDtypeStruct(a.shape, a.dtype)
    scratch = [
        pltpu.VMEM((specials, 2 * RADIX, LANES), F32),
        pltpu.VMEM((rows, LANES), F32),
        pltpu.VMEM((2, RADIX, RADIX), BF16),
        pltpu.SemaphoreType.DMA((2,)),
    ]
    if last:
        scratch = [pltpu.VMEM((rows, LANES), F32)] + scratch + [pltpu.SMEM(end[1].shape, jnp.int32)]
    return pl.pallas_call(
        functools.partial(lower_kernel, low, high, specials, limbs),
        in_specs=[SMEM] * 6 + [HBM, VMEM, VMEM, HBM] + ([SMEM, ANY, VMEM, VMEM] if last else []),
        out_specs=[HBM, VMEM, VMEM] if last else [VMEM, HBM],
        out_shape=[shape(store), half, half] if last else [shape(part), shape(store)],
        input_output_aliases={9: 0} if last else {9: 1},
        scratch_shapes=scratch,
        compiler_params=params(16),
        cost_estimate=pl.CostEstimate(flops=5 * 10**8, bytes_accessed=4 * 2**20, transcendentals=0),
        name="lower",
    )(order, in_hbm(digit), where, scale, in_hbm(conv), comp, in_hbm(diag), mats, part, store, *end)


def interleave(x):
    *lead, limbs, coeffs = x.shape
    x = x.reshape(*lead, limbs, coeffs // LANES, LANES)
    return jnp.swapaxes(x, -3, -2).reshape(*lead, coeffs // LANES * limbs, LANES)


def per_device(order_of, cipher, rotation_keys, diagonals, shifts, twiddles, moduli, digit_of, conversion):
    n = len(order_of)
    limbs = cipher.shape[0]
    ext = digit_of.shape[0]
    specials = ext // (DIGITS + 1)
    count = rotation_keys.shape[1]
    items = count * specials
    pos_of = np.argsort(np.array(order_of)).astype(np.int32)
    cw = [(order_of[i], order_of[(i + 1) % n]) for i in range(n)]
    ccw = [(b, a) for a, b in cw]
    me, rot = lax.axis_index("limb"), lax.axis_index("rot")
    where = jnp.stack([me, rot]).astype(jnp.int32)
    pos = jnp.asarray(pos_of)
    my_pos = pos[me]
    swap = lambda x: lax.ppermute(x, "rot", [(0, 1), (1, 0)])

    grid = np.arange(RADIX)
    angle = (grid[:, None] * grid[None, :] % RADIX) * (2.0 * math.pi / RADIX)
    base = ((np.cos(angle) + np.sin(angle)) / math.sqrt(RADIX)).astype(np.float32)
    base_hi = base.astype(BF16)
    base_lo = (base - base_hi.astype(np.float32)).astype(BF16)

    rows_c = interleave(cipher)
    keys = interleave(rotation_keys).reshape(count, DIGITS, 2, -1, LANES)
    diag = interleave(diagonals).reshape(count, -1, LANES)

    *coef, mats = coef_call(twiddles, where, jnp.asarray(base_hi), jnp.asarray(base_lo), rows_c, limbs)

    ids = jnp.arange(ext, dtype=jnp.int32)
    before = (digit_of[None, :] < digit_of[:, None]) | (
        (digit_of[None, :] == digit_of[:, None]) & (ids[None, :] < ids[:, None])
    )
    place = jnp.sum(before.astype(jnp.int32), axis=1)
    order = jnp.sum(jnp.where(place[None, :] == ids[:, None], ids[None, :], 0), axis=1)
    slot = lax.dynamic_slice_in_dim(jnp.maximum(place - DIGITS * specials, -1), me * limbs, limbs, 0)
    special = digit_of == DIGITS
    mod = moduli.astype(F32)
    scale = jnp.sum(jnp.where(special[None, :], mod[:, None] / mod[None, :], 0.0), axis=1) / specials
    my_special = lax.dynamic_slice_in_dim(special, me * limbs, limbs, 0)
    my_gain = jnp.where(my_special, 1.0, lax.dynamic_slice_in_dim(scale, me * limbs, limbs, 0))
    rows8 = lambda v: jnp.broadcast_to(jnp.tile(v, 8 // limbs)[:, None], (8, LANES))
    gain = rows8(my_gain)
    fixed = items * n // (2 * n)
    plan, rounds, comp = table_call(n, count, specials, limbs, fixed, order, pos, my_pos.reshape(1))

    cut = limbs // 2
    spans = [(0, cut), (cut, limbs)]
    blocks, lens, steps = list(coef), list(spans), [0, 0]
    right, left = list(coef), list(coef)
    hop = lambda x, ring: lax.ppermute(x, "limb", ring)
    both = (n - 1) // 2
    for r in range(1, both + 1):
        for i in range(2):
            right[i], left[i] = hop(right[i], cw), hop(left[i], ccw)
        blocks += right + left
        lens += spans * 2
        steps += [-r, -r, r, r]
        if r == 2:
            right[1], left[1], order, slot, gain, scale, plan, rounds, comp = lax.optimization_barrier(
                (right[1], left[1], order, slot, gain, scale, plan, rounds, comp)
            )
    if n % 2 == 0:
        blocks += [hop(right[0], cw), hop(left[1], ccw)]
        lens += spans
        steps += [n // 2, n // 2]
    srcs = jnp.asarray(
        np.array([[order_of[(pos_of[d] + s) % n] for s in steps] for d in range(n)], np.int32)
    )[me]

    pad = 64
    mixed = mix_call(n, limbs, tuple(lens), order, digit_of, where, srcs, conversion, blocks)
    raised = raise_call(digit_of, where, mixed, swap(mixed), mats, rows_c, pad)

    def accumulate(k, c, after):
        place = slot if after is None else lax.optimization_barrier((slot, after))[0]
        return accum_call(
            k, c, shifts.reshape(-1), place, raised, keys, diag, mats, gain, specials, pad, part[c], stores[c]
        )

    def lower(low, high, c, end=()):
        return lower_call(
            low, high, order, digit_of, where, scale, conversion, comp, diag, mats, specials, part[c], stores[c], end
        )

    def travel(sends):
        return [lax.ppermute(sends[0], "limb", cw), lax.ppermute(sends[1], "limb", ccw)]

    ready = {2 * k - 1: k for k in range(1, count)}
    gates = [(fixed - 5, fixed - 3, fixed - 1), (fixed - 4, fixed - 2, fixed - 1)]
    part, stores, ins, low = [None, None], [None, None], [None, None], [-1, -1]
    sends = [None, None]
    for t in range(fixed):
        for c in range(2):
            if t == 0:
                part[c], stores[c] = accumulate(0, c, sends[0])
            elif t in ready:
                part[c], stores[c] = accumulate(ready[t], c, sends[0])
            stores[c], sends = pack_call(plan, t, stores[c], ins[c])
            ins[c] = travel(sends)
            if t in gates[c]:
                part[c], stores[c] = lower(low[c], t, c)
                low[c] = t

    def more(state):
        return state[0] < rounds[0]

    def one(state):
        t, stores, ins = state
        stores, ins = list(stores), list(ins)
        for c in range(2):
            stores[c], sends = pack_call(plan, t, stores[c], ins[c])
            ins[c] = travel(sends)
        return t + 1, stores, ins

    t, stores, ins = lax.while_loop(more, one, (jnp.int32(fixed), stores, ins))
    sums = []
    for c in range(2):
        _, keep, send = lower(low[c], None, c, (t.reshape(1), plan, *ins[c]))
        sums.append(keep + swap(send))
    total = jnp.stack(sums)
    total = jnp.swapaxes(total.reshape(2, -1, limbs, LANES), 1, 2)
    return total.reshape(2, limbs, -1)


def solution(mesh):
    in_specs = (
        P(("parts", "limb"), None),
        P("rot", None, None, None, "limb", None),
        P("rot", None, "limb", None),
        P("rot", None),
        P(),
        P(),
        P(),
        P(),
    )
    out_specs = P(None, ("parts", "limb"), "rot")
    return jax.shard_map(
        functools.partial(per_device, ring_order(mesh)),
        mesh=mesh,
        in_specs=in_specs,
        out_specs=out_specs,
        check_vma=False,
    )
```

```python
import functools
import math

import jax
import jax.numpy as jnp
import numpy as np
from jax import lax
from jax.experimental import pallas as pl
from jax.experimental.pallas import tpu as pltpu
from jax.sharding import PartitionSpec as P

RADIX = 256
DIGITS = 3
LANES = 128
PLAN = 4
F32 = jnp.float32
BF16 = jnp.bfloat16


ANY = pl.BlockSpec(memory_space=pl.ANY)
VMEM = pl.BlockSpec(memory_space=pltpu.VMEM)
HBM = pl.BlockSpec(memory_space=pltpu.HBM)
SMEM = pl.BlockSpec(memory_space=pltpu.SMEM)


def ring_order(mesh):
    n = mesh.shape["limb"]
    line = np.moveaxis(mesh.devices, list(mesh.axis_names).index("limb"), 0).reshape(n, -1)[:, 0]
    at = [getattr(d, "coords", None) for d in line]
    if any(c is None for c in at):
        return list(range(n))
    near = [
        [j for j in range(n) if sum(abs(x - y) for x, y in zip(at[i], at[j])) == 1] for i in range(n)
    ]

    def walk(path):
        if len(path) == n:
            return path if 0 in near[path[-1]] else None
        for j in near[path[-1]]:
            if j not in path:
                found = walk(path + [j])
                if found:
                    return found
        return None

    return walk([0]) or list(range(n))


def split(x):
    hi = x.astype(BF16)
    return hi, (x - hi.astype(F32)).astype(BF16)


def mm(a, b):
    dot = functools.partial(jnp.dot, preferred_element_type=F32)
    return dot(a[0], b[0]) + dot(a[1], b[0]) + dot(a[0], b[1])


def spin(x, h):
    return mm(h, split(mm(split(x), h)))


def grid_of(ref, m, limbs):
    left = ref[pl.ds(m, RADIX, stride=2 * limbs), :]
    right = ref[pl.ds(limbs + m, RADIX, stride=2 * limbs), :]
    return jnp.concatenate([left, right], axis=1)


def in_hbm(x):
    return pltpu.with_memory_space_constraint(x, pltpu.HBM)


def params(mib):
    return pltpu.CompilerParams(vmem_limit_bytes=mib * 2**20)


def coef_kernel(tw, where, base_hi, base_lo, cipher, coef0, coef1, mats, grid, bases, sem):
    limbs = mats.shape[0]
    cut = coef0.shape[0]
    copies = [
        pltpu.make_async_copy(base_hi, bases.at[0], sem.at[0]),
        pltpu.make_async_copy(base_lo, bases.at[1], sem.at[1]),
        pltpu.make_async_copy(cipher, grid, sem.at[2]),
    ]
    for copy in copies:
        copy.start()
    row = lax.broadcasted_iota(jnp.int32, (RADIX, RADIX), 0)
    col = lax.broadcasted_iota(jnp.int32, (RADIX, RADIX), 1)
    first = where[1] == 0
    for copy in copies:
        copy.wait()

    def limb(coef, start, m, carry):
        g = tw[where[0] * limbs + m]
        pick = jnp.where(((row * g) & (RADIX - 1)) == col, 1.0, 0.0).astype(BF16)
        hi = jnp.dot(pick, bases[0], preferred_element_type=F32).astype(BF16)
        lo = jnp.dot(pick, bases[1], preferred_element_type=F32).astype(BF16)
        mats[m, 0] = hi
        mats[m, 1] = lo
        u = split(mm((hi, lo), split(grid_of(grid, m, limbs))))
        half = tuple(
            jnp.where(first, h[:, :LANES].astype(F32), h[:, LANES:].astype(F32)).astype(BF16) for h in (hi, lo)
        )
        coef[m - start] = mm(u, half)
        return carry

    lax.fori_loop(0, cut, functools.partial(limb, coef0, 0), 0)
    lax.fori_loop(cut, limbs, functools.partial(limb, coef1, cut), 0)


def coef_call(tw, where, base_hi, base_lo, cipher, limbs):
    return pl.pallas_call(
        coef_kernel,
        in_specs=[SMEM, SMEM, HBM, HBM, HBM],
        out_specs=[VMEM, VMEM, VMEM],
        out_shape=[
            jax.ShapeDtypeStruct((limbs // 2, RADIX, LANES), F32),
            jax.ShapeDtypeStruct((limbs - limbs // 2, RADIX, LANES), F32),
            jax.ShapeDtypeStruct((limbs, 2, RADIX, RADIX), BF16),
        ],
        scratch_shapes=[
            pltpu.VMEM(cipher.shape, F32),
            pltpu.VMEM((2, RADIX, RADIX), BF16),
            pltpu.SemaphoreType.DMA((3,)),
        ],
        compiler_params=params(12),
        name="coef",
    )(in_hbm(tw), where, in_hbm(base_hi), in_hbm(base_lo), in_hbm(cipher))


def mix_kernel(n, limbs, lens, order, digit, where, srcs, conv, *refs):
    blocks, out, got, table, sem = refs[: len(lens)], refs[-4], refs[-3], refs[-2], refs[-1]
    size = got.shape[0] * limbs // (DIGITS + 1)
    copies = []
    for i, (start, stop) in enumerate(lens):
        c = pltpu.make_async_copy(blocks[i], got.at[srcs[i], pl.ds(start, stop - start)], sem.at[i])
        c.start()
        copies.append(c)
    first = where[0] * limbs
    for j in range(DIGITS * size):
        l = order[j]
        for m in range(limbs):
            same = digit[l] == digit[first + m]
            one = jnp.where(first + m == l, 1.0, 0.0)
            table[m, j] = jnp.where(same, one, conv[first + m, l])
    for c in copies:
        c.wait()
    step = 64

    def rows(r, carry):
        r0 = pl.multiple_of(r * step, step)
        for d in range(DIGITS):
            acc = [jnp.zeros((step, LANES), F32) for _ in range(limbs)]
            for j in range(size):
                l = order[d * size + j]
                x = got[l // limbs, l % limbs, pl.ds(r0, step), :]
                for m in range(limbs):
                    acc[m] = acc[m] + table[m, d * size + j] * x
            for m in range(limbs):
                out[d, m, pl.ds(r0, step), :] = acc[m]
        return carry

    lax.fori_loop(0, RADIX // step, rows, 0)


def mix_call(n, limbs, lens, order, digit, where, srcs, conv, blocks):
    vmem = pl.BlockSpec(memory_space=pltpu.VMEM)
    return pl.pallas_call(
        functools.partial(mix_kernel, n, limbs, lens),
        in_specs=[SMEM] * 5 + [HBM] * len(blocks),
        out_specs=vmem,
        out_shape=jax.ShapeDtypeStruct((DIGITS, limbs, RADIX, LANES), F32),
        scratch_shapes=[
            pltpu.VMEM((n, limbs, RADIX, LANES), F32),
            pltpu.SMEM((limbs, n * limbs), F32),
            pltpu.SemaphoreType.DMA((len(blocks),)),
        ],
        compiler_params=params(16),
        name="mix",
    )(order, in_hbm(digit), where, srcs, in_hbm(conv), *blocks)


def raise_kernel(pad, digit, where, own, other, mats, cipher, out, rows_in, sem):
    limbs = mats.shape[0]
    rows = cipher.shape[0]
    swapped = where[1] != 0
    fetch = pltpu.make_async_copy(cipher, rows_in, sem)
    fetch.start()

    def known(d, m):
        return digit[where[0] * limbs + m] == d

    def at(m, h):
        return pl.ds(h * limbs + m, RADIX, stride=2 * limbs)

    def convert(i, carry):
        d, m = lax.div(i, limbs), lax.rem(i, limbs)

        @pl.when(jnp.logical_not(known(d, m)))
        def _():
            a, b = own[d, m], other[d, m]
            x = jnp.concatenate([jnp.where(swapped, b, a), jnp.where(swapped, a, b)], axis=1)
            y = spin(x, (mats[m, 0], mats[m, 1]))
            for h in range(2):
                out[d, at(m, h), :] = y[:, h * LANES : (h + 1) * LANES]

        return carry

    lax.fori_loop(0, DIGITS * limbs, convert, 0)
    fetch.wait()

    def place(m, carry):
        d = digit[where[0] * limbs + m]
        for h in range(2):
            out[d, at(m, h), :] = rows_in[at(m, h), :]

        @pl.when(d != DIGITS)
        def _():
            for h in range(2):
                out[DIGITS, at(m, h), :] = jnp.zeros((RADIX, LANES), F32)

        return carry

    lax.fori_loop(0, limbs, place, 0)
    for d in range(DIGITS + 1):
        out[d, pl.ds(rows, pad), :] = out[d, pl.ds(0, pad), :]


def raise_call(digit, where, own, other, mats, cipher, pad):
    rows = cipher.shape[0]
    return pl.pallas_call(
        functools.partial(raise_kernel, pad),
        in_specs=[SMEM, SMEM] + [VMEM] * 3 + [HBM],
        out_specs=VMEM,
        out_shape=jax.ShapeDtypeStruct((DIGITS + 1, rows + pad, LANES), F32),
        scratch_shapes=[pltpu.VMEM(cipher.shape, F32), pltpu.SemaphoreType.DMA],
        compiler_params=params(16),
        name="raise",
    )(in_hbm(digit), where, own, other, mats, in_hbm(cipher))


def accum_kernel(k, limbs, pad, shifts, raised, keys, diag, gain, *refs):
    part, acc, kbuf, dbuf, small, sem, ksem = refs[-8:-6], *refs[-6:]
    rows = acc.shape[1]
    pieces = ksem.shape[0]
    block = rows // pieces

    def fetch(i):
        at = pl.ds(pl.multiple_of(i * block, block), block)
        return [
            pltpu.make_async_copy(keys.at[k, :, at], kbuf.at[:, at], ksem.at[i, 0]),
            pltpu.make_async_copy(diag.at[k, at], dbuf.at[at], ksem.at[i, 1]),
        ]

    amounts = pltpu.make_async_copy(shifts, small, sem)
    amounts.start()
    for i in range(pieces):
        for copy in fetch(i):
            copy.start()
    amounts.wait()
    s = small[0, k]
    tiles, lane = s // LANES, s % LANES
    here = lax.broadcasted_iota(jnp.int32, (pad, LANES), 1) < LANES - lane
    g8 = jnp.concatenate([gain[...]] * (pad // 8), axis=0)

    def piece(i, carry):
        for copy in fetch(i):
            copy.wait()

        def add(r, carry):
            at = pl.multiple_of(i * block + r * pad, pad)
            u0 = lax.rem(at - limbs * tiles + rows, rows)
            v0 = lax.rem(at - limbs * tiles - limbs + 2 * rows, rows)
            turned = []
            for g in range(DIGITS + 1):
                u = raised[g, pl.ds(pl.multiple_of(u0, limbs), pad), :]
                v = raised[g, pl.ds(pl.multiple_of(v0, limbs), pad), :]
                turned.append(pltpu.roll(jnp.where(here, u, v), lane, axis=1))
            w = dbuf[pl.ds(at, pad), :] * g8
            for c in range(2):
                a = turned[DIGITS]
                for d in range(DIGITS):
                    a = a + turned[d] * kbuf[2 * d + c, pl.ds(at, pad), :]
                acc[c, pl.ds(at, pad), :] = a
                w_a = w * a
                part[c][pl.ds(at, pad), :] = w_a if k == 0 else refs[c][pl.ds(at, pad), :] + w_a
            return carry

        return lax.fori_loop(0, block // pad, add, carry, unroll=2)

    lax.fori_loop(0, pieces, piece, 0)


def accum_call(k, shifts, raised, keys, diag, gain, limbs, pad, part):
    rows = raised.shape[1] - pad
    args = (in_hbm(shifts), raised, in_hbm(keys), in_hbm(diag), gain)
    specs = [HBM, VMEM, HBM, HBM, VMEM]
    alias = {}
    if part is not None:
        alias = {len(args) + i: i for i in range(2)}
        args += tuple(part)
        specs += [VMEM, VMEM]
    one = jax.ShapeDtypeStruct((rows, LANES), F32)
    return pl.pallas_call(
        functools.partial(accum_kernel, k, limbs, pad),
        in_specs=specs,
        out_specs=[VMEM, VMEM, VMEM],
        out_shape=[one, one, jax.ShapeDtypeStruct((2, rows, LANES), F32)],
        input_output_aliases=alias,
        scratch_shapes=[
            pltpu.VMEM(keys.shape[1:], F32),
            pltpu.VMEM((rows, LANES), F32),
            pltpu.SMEM(shifts.shape, jnp.int32),
            pltpu.SemaphoreType.DMA,
            pltpu.SemaphoreType.DMA((8, 2)),
        ],
        compiler_params=params(12),
        cost_estimate=pl.CostEstimate(flops=10**8, bytes_accessed=8 * 2**20, transcendentals=0),
        name="accum",
    )(*args)


def emit_kernel(k, limbs, specials, slot, acc, mats, *refs):
    store, stage, sem = refs[-4:-2], refs[-2], refs[-1]

    def emit(m, carry):
        @pl.when(slot[m] >= 0)
        def _():
            h = (mats[m, 0], mats[m, 1])
            copies = []
            for c in range(2):
                y = spin(grid_of(acc.at[c], m, limbs), h)
                stage[c, 0:RADIX, :] = y[:, :LANES]
                stage[c, RADIX:, :] = y[:, LANES:]
                copies.append(pltpu.make_async_copy(stage.at[c], store[c].at[k * specials + slot[m]], sem.at[c]))
                copies[-1].start()
            for copy in copies:
                copy.wait()

        return carry

    lax.fori_loop(0, limbs, emit, 0)


def emit_call(k, slot, acc, mats, specials, items, store):
    one = jax.ShapeDtypeStruct((items, 2 * RADIX, LANES), F32)
    args, specs, alias = (slot, acc, mats), [SMEM, VMEM, VMEM], {}
    if store is not None:
        alias = {len(args) + i: i for i in range(2)}
        args += tuple(map(in_hbm, store))
        specs += [HBM, HBM]
    return pl.pallas_call(
        functools.partial(emit_kernel, k, mats.shape[0], specials),
        in_specs=specs,
        out_specs=[HBM, HBM],
        out_shape=[one, one],
        input_output_aliases=alias,
        scratch_shapes=[pltpu.VMEM((2, 2 * RADIX, LANES), F32), pltpu.SemaphoreType.DMA((2,))],
        compiler_params=params(8),
        cost_estimate=pl.CostEstimate(flops=10**9, bytes_accessed=2**20, transcendentals=0),
        name="emit",
    )(*args)


def table_kernel(n, count, specials, limbs, least, order, pos, spot, plan, rounds, comp, a_ref, b_ref, end_ref):
    items = count * specials
    shape = (items, LANES)
    row_i = lax.broadcasted_iota(jnp.int32, shape, 0)
    row = row_i.astype(F32)
    lane = lax.broadcasted_iota(jnp.int32, shape, 1).astype(F32)
    kind, turn = lax.rem(row_i, specials), lax.div(row_i, specials)
    ready = jnp.maximum(2 * turn - 1, 0)
    weight = 3.0 * turn.astype(F32)
    p = spot[0]
    before, after = lax.rem(p + n - 1, n), lax.rem(p + 1, n)
    line = lax.broadcasted_iota(jnp.int32, (1, LANES), 1)
    org = jnp.zeros(shape, F32)
    for s in range(specials):
        owner = pos[lax.div(order[DIGITS * specials + s], limbs)]
        org = jnp.where(kind == s, owner.astype(F32), org)
    a_ref[...] = jnp.zeros(shape, F32)
    b_ref[...] = jnp.zeros(shape, F32)
    end_ref[...] = jnp.zeros(shape, F32)
    big = float(items * (2 * n + 3 * count))

    def choose(front, spread, t):
        open_ = jnp.logical_and(spread < n - 1, ready <= t)
        cand = jnp.logical_and(open_, front == lane)
        key = jnp.where(cand, (2.0 * spread + weight) * items + row, big)
        best = jnp.min(key, axis=0, keepdims=True)
        hit = jnp.where(jnp.logical_and(cand, key == best), 1.0, 0.0)
        item = jnp.sum(hit * (row - items), axis=0, keepdims=True) + items
        return item, jnp.sum(hit, axis=1, keepdims=True)

    def note(t, r, item, where):
        t = jnp.asarray(t, jnp.int32)
        mine = jnp.sum(jnp.where(line == where, item, 0.0), axis=1, keepdims=True)
        at = pl.ds(lax.div(PLAN * t + r, LANES), 1)
        here = line == lax.rem(PLAN * t + r, LANES)
        plan[at, :] = jnp.where(here, jnp.broadcast_to(mine, (1, LANES)).astype(jnp.int32), plan[at, :])

    none = jnp.full((1, LANES), float(items), F32)
    plan[...] = jnp.full(plan.shape, items, jnp.int32)
    note(0, 2, none, p)
    note(0, 3, none, p)

    def cond(c):
        return jnp.logical_or(c[1] > 0, c[0] < least)

    def body(c):
        t, _ = c
        a, b = a_ref[...], b_ref[...]
        front = org + a
        item, right = choose(jnp.where(front >= n, front - n, front), a + b, t)
        note(t, 0, item, p)
        note(t + 1, 2, item, before)
        a = a + right
        front = org - b
        item, left = choose(jnp.where(front < 0, front + n, front), a + b, t)
        note(t, 1, item, p)
        note(t + 1, 3, item, after)
        b = b + left
        a_ref[...] = a
        b_ref[...] = b
        end_ref[...] = jnp.where(right + left > 0, (t + 1).astype(F32), end_ref[...])
        return t + 1, jnp.sum(n - 1 - a - b).astype(jnp.int32)

    t, _ = lax.while_loop(cond, body, (jnp.int32(0), jnp.int32(1)))
    rounds[0] = t
    note(t, 0, none, p)
    note(t, 1, none, p)
    for k in range(count):
        comp[k] = jnp.max(end_ref[pl.ds(k * specials, specials), :]).astype(jnp.int32)


def table_call(n, count, specials, limbs, least, order, pos, spot):
    items = count * specials
    most = items * (n - 1) + 2 * count
    return pl.pallas_call(
        functools.partial(table_kernel, n, count, specials, limbs, least),
        in_specs=[SMEM] * 3,
        out_specs=[pl.BlockSpec(memory_space=pltpu.VMEM), SMEM, SMEM],
        out_shape=[
            jax.ShapeDtypeStruct((-(-PLAN * (most + 1) // (8 * LANES)) * 8, LANES), jnp.int32),
            jax.ShapeDtypeStruct((1,), jnp.int32),
            jax.ShapeDtypeStruct((count,), jnp.int32),
        ],
        scratch_shapes=[pltpu.VMEM((items, LANES), F32)] * 3,
        compiler_params=params(8),
        name="table",
    )(order, in_hbm(pos), spot)


def round_of(tile, t):
    got = [tile[lax.div(f, LANES), lax.rem(f, LANES)] for f in (jnp.asarray(PLAN * t + r, jnp.int32) for r in range(PLAN))]
    return got[:2], got[2:]


def pack_kernel(items, t, first, last, *refs):
    refs = list(refs)
    if t is None:
        t = refs.pop(0)[0]
    table, store = refs.pop(0), refs.pop(0)
    ins = () if first else (refs.pop(0), refs.pop(0))
    refs.pop(0)
    outs = () if last else (refs.pop(0), refs.pop(0))
    tile, keep, send, tsem = refs
    plan = pltpu.make_async_copy(table, tile, tsem)
    plan.start()
    plan.wait()
    go, came = round_of(tile, t)
    for i in range(len(ins)):
        @pl.when(came[i] < items)
        def _():
            pltpu.make_async_copy(ins[i], store.at[came[i]], keep.at[i]).start()

    old = []
    for j in range(len(outs)):
        fresh = [jnp.logical_and(go[j] == came[i], came[i] < items) for i in range(len(ins))]
        held = go[j] < items
        for f in fresh:
            held = jnp.logical_and(held, jnp.logical_not(f))
        old.append(held)

        @pl.when(held)
        def _():
            pltpu.make_async_copy(store.at[go[j]], outs[j], send.at[j]).start()

        for i in range(len(ins)):
            @pl.when(fresh[i])
            def _():
                outs[j][...] = ins[i][...]

    for i in range(len(ins)):
        @pl.when(came[i] < items)
        def _():
            pltpu.make_async_copy(ins[i], store.at[came[i]], keep.at[i]).wait()
    for j in range(len(outs)):
        @pl.when(old[j])
        def _():
            pltpu.make_async_copy(store.at[go[j]], outs[j], send.at[j]).wait()


def pack_call(table, t, store, ins=None, last=False):
    first = ins is None
    store = in_hbm(store)
    items = store.shape[0]
    item = jax.ShapeDtypeStruct(store.shape[1:], store.dtype)
    static = isinstance(t, int)
    args = (() if static else (t.reshape(1),)) + (table, store) + (() if first else tuple(ins))
    at = 1 if static else 2
    outs = [jax.ShapeDtypeStruct(store.shape, store.dtype)] + ([] if last else [item, item])
    size = math.prod(item.shape) * 4
    res = pl.pallas_call(
        functools.partial(pack_kernel, items, t if static else None, first, last),
        in_specs=([] if static else [SMEM]) + [ANY, HBM] + [VMEM] * (0 if first else 2),
        out_specs=[HBM] + [VMEM] * (len(outs) - 1),
        out_shape=outs,
        input_output_aliases={at: 0},
        scratch_shapes=[
            pltpu.SMEM(table.shape, jnp.int32),
            pltpu.SemaphoreType.DMA((2,)),
            pltpu.SemaphoreType.DMA((2,)),
            pltpu.SemaphoreType.DMA,
        ],
        compiler_params=params(2),
        cost_estimate=pl.CostEstimate(flops=0, bytes_accessed=8 * size, transcendentals=0),
        name="pack",
    )(*args)
    return res[0], list(res[1:])


def lower_kernel(low, high, guess, specials, limbs, *refs):
    order, digit, where, scale, conv, comp, diag, mats, *refs = refs
    part, store, refs = refs[:2], refs[2:4], refs[4:]
    last = high is None

    def fetch(k):
        return [
            pltpu.make_async_copy(store[c].at[pl.ds(k * specials, specials)], got.at[c], sem.at[c]) for c in range(2)
        ] + [pltpu.make_async_copy(diag.at[k], dg, sem.at[2])]

    if last:
        t, plan, *refs = refs
        ins, store, keep, send, refs = (refs[0:2], refs[2:4]), refs[4:6], refs[6:8], refs[8:10], refs[10:]
        total, got, dg, xs, sem, tile = refs
        total = [total.at[0], total.at[1]]
        pltpu.make_async_copy(diag.at[guess], dg, sem.at[2]).start()
        copy = pltpu.make_async_copy(plan, tile, sem.at[0])
        copy.start()
        copy.wait()
        _, came = round_of(tile, t[0])

        def arrive(act):
            for c in range(2):
                for i in range(2):
                    @pl.when(came[i] < store[c].shape[0])
                    def _():
                        act(pltpu.make_async_copy(ins[c][i], store[c].at[came[i]], sem.at[3 + 2 * c + i]))

        arrive(lambda copy: copy.start())
        arrive(lambda copy: copy.wait())
        for c in range(2):
            pltpu.make_async_copy(store[c].at[pl.ds(guess * specials, specials)], got.at[c], sem.at[c]).start()
    else:
        total, (got, dg, xs, sem) = refs[:2], refs[4:]
        for copy in fetch(guess):
            copy.start()
    count = diag.shape[0]
    first = where[0] * limbs
    for c in range(2):
        total[c][...] = part[c][...]
    for copy in fetch(guess):
        copy.wait()

    def turn(i, carry):
        k = lax.rem(guess + i, count)
        ripe = comp[k] > low
        if not last:
            ripe = jnp.logical_and(ripe, comp[k] <= high)

        @pl.when(ripe)
        def _():
            @pl.when(i > 0)
            def _():
                for copy in fetch(k):
                    copy.start()
                for copy in fetch(k):
                    copy.wait()

            def limb(m, carry):
                q = first + m

                @pl.when(digit[q] != DIGITS)
                def _():
                    h = (mats[m, 0], mats[m, 1])
                    w = [conv[q, order[DIGITS * specials + s]] for s in range(specials)]
                    size = scale[q]
                    step = 64
                    for c in range(2):
                        for i in range(2):
                            for r in range(0, RADIX, step):
                                x = w[0] * got[c, 0, pl.ds(i * RADIX + r, step), :]
                                for s in range(1, specials):
                                    x = x + w[s] * got[c, s, pl.ds(i * RADIX + r, step), :]
                                hi, lo = split(x)
                                xs[c, 0, pl.ds(r, step), pl.ds(i * LANES, LANES)] = hi
                                xs[c, 1, pl.ds(r, step), pl.ds(i * LANES, LANES)] = lo
                    for c in range(2):
                        y = mm(h, split(mm((xs[c, 0], xs[c, 1]), h)))
                        for i in range(2):
                            at = pl.ds(i * limbs + m, RADIX, stride=2 * limbs)
                            total[c][at, :] = total[c][at, :] - dg[at, :] * size * y[:, i * LANES : (i + 1) * LANES]

                return carry

            lax.fori_loop(0, limbs, limb, 0)

        return carry

    lax.fori_loop(0, count, turn, 0)
    if last:
        half = total[0].shape[0] // 2
        mine = where[1]
        for c in range(2):
            keep[c][...] = total[c][pl.ds(pl.multiple_of(mine * half, half), half), :]
            send[c][...] = total[c][pl.ds(pl.multiple_of((1 - mine) * half, half), half), :]


def lower_call(low, high, guess, order, digit, where, scale, conv, comp, diag, mats, specials, part, store, end=()):
    limbs = mats.shape[0]
    store = [in_hbm(s) for s in store]
    rows = part[0].shape[0]
    half = jax.ShapeDtypeStruct((rows // 2, LANES), F32)
    last = high is None
    shape = lambda a: jax.ShapeDtypeStruct(a.shape, a.dtype)
    scratch = [
        pltpu.VMEM((2, specials, 2 * RADIX, LANES), F32),
        pltpu.VMEM((rows, LANES), F32),
        pltpu.VMEM((2, 2, RADIX, RADIX), BF16),
        pltpu.SemaphoreType.DMA((7,)),
    ]
    if last:
        scratch = [pltpu.VMEM((2, rows, LANES), F32)] + scratch + [pltpu.SMEM(end[1].shape, jnp.int32)]
    return pl.pallas_call(
        functools.partial(lower_kernel, low, high, guess, specials, limbs),
        in_specs=[SMEM] * 6 + [HBM, VMEM, VMEM, VMEM, HBM, HBM] + ([SMEM, ANY] + [VMEM] * 4 if last else []),
        out_specs=[HBM, HBM] + [VMEM] * 4 if last else [VMEM, VMEM, HBM, HBM],
        out_shape=[shape(s) for s in store] + [half] * 4 if last else [shape(p) for p in (*part, *store)],
        input_output_aliases={10: 0, 11: 1} if last else {10: 2, 11: 3},
        scratch_shapes=scratch,
        compiler_params=params(12),
        cost_estimate=pl.CostEstimate(flops=10**9, bytes_accessed=8 * 2**20, transcendentals=0),
        name="lower",
    )(order, in_hbm(digit), where, scale, in_hbm(conv), comp, in_hbm(diag), mats, *part, *store, *end)


def interleave(x):
    *lead, limbs, coeffs = x.shape
    x = x.reshape(*lead, limbs, coeffs // LANES, LANES)
    return jnp.swapaxes(x, -3, -2).reshape(*lead, coeffs // LANES * limbs, LANES)


def per_device(order_of, cipher, rotation_keys, diagonals, shifts, twiddles, moduli, digit_of, conversion):
    n = len(order_of)
    limbs = cipher.shape[0]
    ext = digit_of.shape[0]
    specials = ext // (DIGITS + 1)
    count = rotation_keys.shape[1]
    items = count * specials
    pos_of = np.argsort(np.array(order_of)).astype(np.int32)
    cw = [(order_of[i], order_of[(i + 1) % n]) for i in range(n)]
    ccw = [(b, a) for a, b in cw]
    me, rot = lax.axis_index("limb"), lax.axis_index("rot")
    where = jnp.stack([me, rot]).astype(jnp.int32)
    pos = jnp.asarray(pos_of)
    my_pos = pos[me]
    swap = lambda x: lax.ppermute(x, "rot", [(0, 1), (1, 0)])

    grid = np.arange(RADIX)
    angle = (grid[:, None] * grid[None, :] % RADIX) * (2.0 * math.pi / RADIX)
    base = ((np.cos(angle) + np.sin(angle)) / math.sqrt(RADIX)).astype(np.float32)
    base_hi = base.astype(BF16)
    base_lo = (base - base_hi.astype(np.float32)).astype(BF16)

    rows_c = interleave(cipher)
    keys = interleave(rotation_keys).reshape(count, DIGITS * 2, -1, LANES)
    diag = interleave(diagonals).reshape(count, -1, LANES)

    *coef, mats = coef_call(twiddles, where, jnp.asarray(base_hi), jnp.asarray(base_lo), rows_c, limbs)

    ids = jnp.arange(ext, dtype=jnp.int32)
    before = (digit_of[None, :] < digit_of[:, None]) | (
        (digit_of[None, :] == digit_of[:, None]) & (ids[None, :] < ids[:, None])
    )
    place = jnp.sum(before.astype(jnp.int32), axis=1)
    order = jnp.sum(jnp.where(place[None, :] == ids[:, None], ids[None, :], 0), axis=1)
    slot = lax.dynamic_slice_in_dim(jnp.maximum(place - DIGITS * specials, -1), me * limbs, limbs, 0)
    special = digit_of == DIGITS
    mod = moduli.astype(F32)
    scale = jnp.sum(jnp.where(special[None, :], mod[:, None] / mod[None, :], 0.0), axis=1) / specials
    my_special = lax.dynamic_slice_in_dim(special, me * limbs, limbs, 0)
    my_gain = jnp.where(my_special, 1.0, lax.dynamic_slice_in_dim(scale, me * limbs, limbs, 0))
    rows8 = lambda v: jnp.broadcast_to(jnp.tile(v, 8 // limbs)[:, None], (8, LANES))
    gain = rows8(my_gain)
    fixed = items * n // (2 * n)
    plan, rounds, comp = table_call(n, count, specials, limbs, fixed, order, pos, my_pos.reshape(1))

    cut = limbs // 2
    spans = [(0, cut), (cut, limbs)]
    blocks, lens, steps = list(coef), list(spans), [0, 0]
    right, left = list(coef), list(coef)
    hop = lambda x, ring: lax.ppermute(x, "limb", ring)
    both = (n - 1) // 2
    for r in range(1, both + 1):
        for i in range(2):
            right[i], left[i] = hop(right[i], cw), hop(left[i], ccw)
        blocks += right + left
        lens += spans * 2
        steps += [-r, -r, r, r]
        if r == 2:
            right[1], left[1], order, slot, gain, scale, plan, rounds, comp = lax.optimization_barrier(
                (right[1], left[1], order, slot, gain, scale, plan, rounds, comp)
            )
    if n % 2 == 0:
        blocks += [hop(right[0], cw), hop(left[1], ccw)]
        lens += spans
        steps += [n // 2, n // 2]
    srcs = jnp.asarray(
        np.array([[order_of[(pos_of[d] + s) % n] for s in steps] for d in range(n)], np.int32)
    )[me]

    pad = 64
    mixed = mix_call(n, limbs, tuple(lens), order, digit_of, where, srcs, conversion, blocks)
    raised = raise_call(digit_of, where, mixed, swap(mixed), mats, rows_c, pad)

    def accumulate(k, after=None):
        return accum_call(k, tie(shifts, after), raised, keys, diag, gain, limbs, pad, part)

    def lower(low, high, guess, end=()):
        return lower_call(
            low, high, guess, order, digit_of, where, scale, conversion, comp, diag, mats, specials, part, stores, end
        )

    def tie(x, after):
        return x if after is None else lax.optimization_barrier((x, after))[0]

    def travel(sends):
        return [lax.ppermute(sends[0], "limb", cw), lax.ppermute(sends[1], "limb", ccw)]

    tasks = {max(2 * k - 3, 0): k for k in range(1, count)}, {max(2 * k - 2, 0): k for k in range(1, count)}
    gates = {fixed - 5: 0, fixed - 3: 1, fixed - 1: 2}
    part, stores, ins, low = None, None, [None, None], -1
    *part, acc = accumulate(0)
    stores = list(emit_call(0, slot, acc, mats, specials, items, stores))
    for t in range(fixed):
        for c in range(2):
            stores[c], sends = pack_call(plan, t, stores[c], ins[c])
            ins[c] = travel(sends)
        if t in tasks[0]:
            *part, acc = accumulate(tasks[0][t], sends[0])
            stores[0], acc = lax.optimization_barrier((stores[0], acc))
        if t in tasks[1]:
            stores = list(emit_call(tasks[1][t], slot, tie(acc, sends[0]), mats, specials, items, stores))
        if t in gates:
            *part, stores[0], stores[1] = lower(low, t, min(gates[t], count - 1))
            low = t

    def more(state):
        return state[0] < rounds[0]

    def one(state):
        t, stores, ins = state
        stores, ins = list(stores), list(ins)
        for c in range(2):
            stores[c], sends = pack_call(plan, t, stores[c], ins[c])
            ins[c] = travel(sends)
        return t + 1, stores, ins

    t, stores, ins = lax.while_loop(more, one, (jnp.int32(fixed), stores, ins))
    _, _, *halves = lower(low, None, count - 1, (t.reshape(1), plan, *ins[0], *ins[1]))
    total = jnp.stack([keep + swap(send) for keep, send in zip(halves[:2], halves[2:])])
    total = jnp.swapaxes(total.reshape(2, -1, limbs, LANES), 1, 2)
    return total.reshape(2, limbs, -1)


def solution(mesh):
    in_specs = (
        P(("parts", "limb"), None),
        P("rot", None, None, None, "limb", None),
        P("rot", None, "limb", None),
        P("rot", None),
        P(),
        P(),
        P(),
        P(),
    )
    out_specs = P(None, ("parts", "limb"), "rot")
    return jax.shard_map(
        functools.partial(per_device, ring_order(mesh)),
        mesh=mesh,
        in_specs=in_specs,
        out_specs=out_specs,
        check_vma=False,
    )
```

```python
import functools
import math

import jax
import jax.numpy as jnp
import numpy as np
from jax import lax
from jax.experimental import pallas as pl
from jax.experimental.pallas import tpu as pltpu
from jax.sharding import PartitionSpec as P

RADIX = 256
DIGITS = 3
LANES = 128
PLAN = 4
F32 = jnp.float32
BF16 = jnp.bfloat16


ANY = pl.BlockSpec(memory_space=pl.ANY)
VMEM = pl.BlockSpec(memory_space=pltpu.VMEM)
HBM = pl.BlockSpec(memory_space=pltpu.HBM)
SMEM = pl.BlockSpec(memory_space=pltpu.SMEM)


def ring_order(mesh):
    n = mesh.shape["limb"]
    line = np.moveaxis(mesh.devices, list(mesh.axis_names).index("limb"), 0).reshape(n, -1)[:, 0]
    at = [getattr(d, "coords", None) for d in line]
    if any(c is None for c in at):
        return list(range(n))
    near = [
        [j for j in range(n) if sum(abs(x - y) for x, y in zip(at[i], at[j])) == 1] for i in range(n)
    ]

    def walk(path):
        if len(path) == n:
            return path if 0 in near[path[-1]] else None
        for j in near[path[-1]]:
            if j not in path:
                found = walk(path + [j])
                if found:
                    return found
        return None

    return walk([0]) or list(range(n))


def split(x):
    hi = x.astype(BF16)
    return hi, (x - hi.astype(F32)).astype(BF16)


def mm(a, b):
    dot = functools.partial(jnp.dot, preferred_element_type=F32)
    return dot(a[0], b[0]) + dot(a[1], b[0]) + dot(a[0], b[1])


def spin(x, h):
    return mm(h, split(mm(split(x), h)))


def grid_of(ref, m, limbs):
    left = ref[pl.ds(m, RADIX, stride=2 * limbs), :]
    right = ref[pl.ds(limbs + m, RADIX, stride=2 * limbs), :]
    return jnp.concatenate([left, right], axis=1)


def in_hbm(x):
    return pltpu.with_memory_space_constraint(x, pltpu.HBM)


def params(mib):
    return pltpu.CompilerParams(vmem_limit_bytes=mib * 2**20)


def coef_kernel(tw, where, base_hi, base_lo, cipher, coef0, coef1, mats, grid, bases, sem):
    limbs = mats.shape[0]
    cut = coef0.shape[0]
    copies = [
        pltpu.make_async_copy(base_hi, bases.at[0], sem.at[0]),
        pltpu.make_async_copy(base_lo, bases.at[1], sem.at[1]),
        pltpu.make_async_copy(cipher, grid, sem.at[2]),
    ]
    for copy in copies:
        copy.start()
    row = lax.broadcasted_iota(jnp.int32, (RADIX, RADIX), 0)
    col = lax.broadcasted_iota(jnp.int32, (RADIX, RADIX), 1)
    first = where[1] == 0
    for copy in copies:
        copy.wait()

    def limb(coef, start, m, carry):
        g = tw[where[0] * limbs + m]
        pick = jnp.where(((row * g) & (RADIX - 1)) == col, 1.0, 0.0).astype(BF16)
        hi = jnp.dot(pick, bases[0], preferred_element_type=F32).astype(BF16)
        lo = jnp.dot(pick, bases[1], preferred_element_type=F32).astype(BF16)
        mats[m, 0] = hi
        mats[m, 1] = lo
        u = split(mm((hi, lo), split(grid_of(grid, m, limbs))))
        half = tuple(
            jnp.where(first, h[:, :LANES].astype(F32), h[:, LANES:].astype(F32)).astype(BF16) for h in (hi, lo)
        )
        coef[m - start] = mm(u, half)
        return carry

    lax.fori_loop(0, cut, functools.partial(limb, coef0, 0), 0, unroll=True)
    lax.fori_loop(cut, limbs, functools.partial(limb, coef1, cut), 0, unroll=True)


def coef_call(tw, where, base_hi, base_lo, cipher, limbs):
    return pl.pallas_call(
        coef_kernel,
        in_specs=[SMEM, SMEM, HBM, HBM, HBM],
        out_specs=[VMEM, VMEM, VMEM],
        out_shape=[
            jax.ShapeDtypeStruct((limbs // 2, RADIX, LANES), F32),
            jax.ShapeDtypeStruct((limbs - limbs // 2, RADIX, LANES), F32),
            jax.ShapeDtypeStruct((limbs, 2, RADIX, RADIX), BF16),
        ],
        scratch_shapes=[
            pltpu.VMEM(cipher.shape, F32),
            pltpu.VMEM((2, RADIX, RADIX), BF16),
            pltpu.SemaphoreType.DMA((3,)),
        ],
        compiler_params=params(12),
        name="coef",
    )(in_hbm(tw), where, in_hbm(base_hi), in_hbm(base_lo), in_hbm(cipher))


def mix_kernel(n, limbs, lens, order, digit, where, srcs, conv, *refs):
    blocks, out, got, table, sem = refs[: len(lens)], refs[-4], refs[-3], refs[-2], refs[-1]
    size = got.shape[0] * limbs // (DIGITS + 1)
    copies = []
    for i, (start, stop) in enumerate(lens):
        c = pltpu.make_async_copy(blocks[i], got.at[srcs[i], pl.ds(start, stop - start)], sem.at[i])
        c.start()
        copies.append(c)
    first = where[0] * limbs
    for j in range(DIGITS * size):
        l = order[j]
        for m in range(limbs):
            same = digit[l] == digit[first + m]
            one = jnp.where(first + m == l, 1.0, 0.0)
            table[m, j] = jnp.where(same, one, conv[first + m, l])
    for c in copies:
        c.wait()
    step = 64

    def rows(r, carry):
        r0 = pl.multiple_of(r * step, step)
        for d in range(DIGITS):
            acc = [jnp.zeros((step, LANES), F32) for _ in range(limbs)]
            for j in range(size):
                l = order[d * size + j]
                x = got[l // limbs, l % limbs, pl.ds(r0, step), :]
                for m in range(limbs):
                    acc[m] = acc[m] + table[m, d * size + j] * x
            for m in range(limbs):
                out[d, m, pl.ds(r0, step), :] = acc[m]
        return carry

    lax.fori_loop(0, RADIX // step, rows, 0)


def mix_call(n, limbs, lens, order, digit, where, srcs, conv, blocks):
    vmem = pl.BlockSpec(memory_space=pltpu.VMEM)
    return pl.pallas_call(
        functools.partial(mix_kernel, n, limbs, lens),
        in_specs=[SMEM] * 5 + [HBM] * len(blocks),
        out_specs=vmem,
        out_shape=jax.ShapeDtypeStruct((DIGITS, limbs, RADIX, LANES), F32),
        scratch_shapes=[
            pltpu.VMEM((n, limbs, RADIX, LANES), F32),
            pltpu.SMEM((limbs, n * limbs), F32),
            pltpu.SemaphoreType.DMA((len(blocks),)),
        ],
        compiler_params=params(16),
        name="mix",
    )(order, in_hbm(digit), where, srcs, in_hbm(conv), *blocks)


def raise_kernel(pad, digit, where, own, other, mats, cipher, out, rows_in, sem):
    limbs = mats.shape[0]
    rows = cipher.shape[0]
    swapped = where[1] != 0
    fetch = pltpu.make_async_copy(cipher, rows_in, sem)
    fetch.start()

    def at(m, h):
        return pl.ds(h * limbs + m, RADIX, stride=2 * limbs)

    def convert(m, carry):
        h = (mats[m, 0], mats[m, 1])
        for d in range(DIGITS):
            a, b = own[d, m], other[d, m]
            x = jnp.concatenate([jnp.where(swapped, b, a), jnp.where(swapped, a, b)], axis=1)
            y = spin(x, h)
            for i in range(2):
                out[d, at(m, i), :] = y[:, i * LANES : (i + 1) * LANES]
        return carry

    lax.fori_loop(0, limbs, convert, 0)
    fetch.wait()

    def place(m, carry):
        d = digit[where[0] * limbs + m]
        for h in range(2):
            out[d, at(m, h), :] = rows_in[at(m, h), :]

        @pl.when(d != DIGITS)
        def _():
            for h in range(2):
                out[DIGITS, at(m, h), :] = jnp.zeros((RADIX, LANES), F32)

        return carry

    lax.fori_loop(0, limbs, place, 0)
    for d in range(DIGITS + 1):
        out[d, pl.ds(rows, pad), :] = out[d, pl.ds(0, pad), :]


def raise_call(digit, where, own, other, mats, cipher, pad):
    rows = cipher.shape[0]
    return pl.pallas_call(
        functools.partial(raise_kernel, pad),
        in_specs=[SMEM, SMEM] + [VMEM] * 3 + [HBM],
        out_specs=VMEM,
        out_shape=jax.ShapeDtypeStruct((DIGITS + 1, rows + pad, LANES), F32),
        scratch_shapes=[pltpu.VMEM(cipher.shape, F32), pltpu.SemaphoreType.DMA],
        compiler_params=params(16),
        name="raise",
    )(in_hbm(digit), where, own, other, mats, in_hbm(cipher))


def accum_kernel(k, limbs, pad, shifts, raised, keys, diag, gain, *refs):
    part, acc, kbuf, dbuf, small, sem, ksem = refs[-8:-6], *refs[-6:]
    rows = acc.shape[1]
    pieces = ksem.shape[0]
    block = rows // pieces

    def fetch(i):
        at = pl.ds(pl.multiple_of(i * block, block), block)
        return [
            pltpu.make_async_copy(keys.at[k, :, at], kbuf.at[:, at], ksem.at[i, 0]),
            pltpu.make_async_copy(diag.at[k, at], dbuf.at[at], ksem.at[i, 1]),
        ]

    amounts = pltpu.make_async_copy(shifts, small, sem)
    amounts.start()
    for i in range(pieces):
        for copy in fetch(i):
            copy.start()
    amounts.wait()
    s = small[0, k]
    tiles, lane = s // LANES, s % LANES
    here = lax.broadcasted_iota(jnp.int32, (pad, LANES), 1) < LANES - lane
    g8 = jnp.concatenate([gain[...]] * (pad // 8), axis=0)

    def piece(i, carry):
        for copy in fetch(i):
            copy.wait()

        def add(r, carry):
            at = pl.multiple_of(i * block + r * pad, pad)
            u0 = lax.rem(at - limbs * tiles + rows, rows)
            v0 = lax.rem(at - limbs * tiles - limbs + 2 * rows, rows)
            turned = []
            for g in range(DIGITS + 1):
                u = raised[g, pl.ds(pl.multiple_of(u0, limbs), pad), :]
                v = raised[g, pl.ds(pl.multiple_of(v0, limbs), pad), :]
                turned.append(pltpu.roll(jnp.where(here, u, v), lane, axis=1))
            w = dbuf[pl.ds(at, pad), :] * g8
            for c in range(2):
                a = turned[DIGITS]
                for d in range(DIGITS):
                    a = a + turned[d] * kbuf[2 * d + c, pl.ds(at, pad), :]
                acc[c, pl.ds(at, pad), :] = a
                w_a = w * a
                part[c][pl.ds(at, pad), :] = w_a if k == 0 else refs[c][pl.ds(at, pad), :] + w_a
            return carry

        return lax.fori_loop(0, block // pad, add, carry, unroll=2)

    lax.fori_loop(0, pieces, piece, 0)


def accum_call(k, shifts, raised, keys, diag, gain, limbs, pad, part):
    rows = raised.shape[1] - pad
    args = (in_hbm(shifts), raised, in_hbm(keys), in_hbm(diag), gain)
    specs = [HBM, VMEM, HBM, HBM, VMEM]
    alias = {}
    if part is not None:
        alias = {len(args) + i: i for i in range(2)}
        args += tuple(part)
        specs += [VMEM, VMEM]
    one = jax.ShapeDtypeStruct((rows, LANES), F32)
    return pl.pallas_call(
        functools.partial(accum_kernel, k, limbs, pad),
        in_specs=specs,
        out_specs=[VMEM, VMEM, VMEM],
        out_shape=[one, one, jax.ShapeDtypeStruct((2, rows, LANES), F32)],
        input_output_aliases=alias,
        scratch_shapes=[
            pltpu.VMEM(keys.shape[1:], F32),
            pltpu.VMEM((rows, LANES), F32),
            pltpu.SMEM(shifts.shape, jnp.int32),
            pltpu.SemaphoreType.DMA,
            pltpu.SemaphoreType.DMA((8, 2)),
        ],
        compiler_params=params(12),
        cost_estimate=pl.CostEstimate(flops=10**8, bytes_accessed=8 * 2**20, transcendentals=0),
        name="accum",
    )(*args)


def emit_kernel(k, limbs, specials, slot, acc, mats, *refs):
    store, stage, sem = refs[-4:-2], refs[-2], refs[-1]

    def emit(m, carry):
        @pl.when(slot[m] >= 0)
        def _():
            h = (mats[m, 0], mats[m, 1])
            copies = []
            for c in range(2):
                y = spin(grid_of(acc.at[c], m, limbs), h)
                stage[c, 0:RADIX, :] = y[:, :LANES]
                stage[c, RADIX:, :] = y[:, LANES:]
                copies.append(pltpu.make_async_copy(stage.at[c], store[c].at[k * specials + slot[m]], sem.at[c]))
                copies[-1].start()
            for copy in copies:
                copy.wait()

        return carry

    lax.fori_loop(0, limbs, emit, 0)


def emit_call(k, slot, acc, mats, specials, items, store):
    one = jax.ShapeDtypeStruct((items, 2 * RADIX, LANES), F32)
    args, specs, alias = (slot, acc, mats), [SMEM, VMEM, VMEM], {}
    if store is not None:
        alias = {len(args) + i: i for i in range(2)}
        args += tuple(map(in_hbm, store))
        specs += [HBM, HBM]
    return pl.pallas_call(
        functools.partial(emit_kernel, k, mats.shape[0], specials),
        in_specs=specs,
        out_specs=[HBM, HBM],
        out_shape=[one, one],
        input_output_aliases=alias,
        scratch_shapes=[pltpu.VMEM((2, 2 * RADIX, LANES), F32), pltpu.SemaphoreType.DMA((2,))],
        compiler_params=params(8),
        cost_estimate=pl.CostEstimate(flops=10**9, bytes_accessed=2**20, transcendentals=0),
        name="emit",
    )(*args)


def table_kernel(n, count, specials, limbs, least, order, pos, spot, plan, rounds, comp, a_ref, b_ref, end_ref):
    items = count * specials
    shape = (items, LANES)
    row_i = lax.broadcasted_iota(jnp.int32, shape, 0)
    row = row_i.astype(F32)
    lane = lax.broadcasted_iota(jnp.int32, shape, 1).astype(F32)
    kind, turn = lax.rem(row_i, specials), lax.div(row_i, specials)
    ready = jnp.maximum(2 * turn - 1, 0)
    weight = 3.0 * turn.astype(F32)
    p = spot[0]
    before, after = lax.rem(p + n - 1, n), lax.rem(p + 1, n)
    line = lax.broadcasted_iota(jnp.int32, (1, LANES), 1)
    org = jnp.zeros(shape, F32)
    for s in range(specials):
        owner = pos[lax.div(order[DIGITS * specials + s], limbs)]
        org = jnp.where(kind == s, owner.astype(F32), org)
    a_ref[...] = jnp.zeros(shape, F32)
    b_ref[...] = jnp.zeros(shape, F32)
    end_ref[...] = jnp.zeros(shape, F32)
    big = float(items * (2 * n + 3 * count))

    def choose(front, spread, t):
        open_ = jnp.logical_and(spread < n - 1, ready <= t)
        cand = jnp.logical_and(open_, front == lane)
        key = jnp.where(cand, (2.0 * spread + weight) * items + row, big)
        best = jnp.min(key, axis=0, keepdims=True)
        hit = jnp.where(jnp.logical_and(cand, key == best), 1.0, 0.0)
        item = jnp.sum(hit * (row - items), axis=0, keepdims=True) + items
        return item, jnp.sum(hit, axis=1, keepdims=True)

    def note(t, r, item, where):
        t = jnp.asarray(t, jnp.int32)
        mine = jnp.sum(jnp.where(line == where, item, 0.0), axis=1, keepdims=True)
        at = pl.ds(lax.div(PLAN * t + r, LANES), 1)
        here = line == lax.rem(PLAN * t + r, LANES)
        plan[at, :] = jnp.where(here, jnp.broadcast_to(mine, (1, LANES)).astype(jnp.int32), plan[at, :])

    none = jnp.full((1, LANES), float(items), F32)
    plan[...] = jnp.full(plan.shape, items, jnp.int32)
    note(0, 2, none, p)
    note(0, 3, none, p)

    def step(t, carry):
        a, b = a_ref[...], b_ref[...]
        front = org + a
        item, right = choose(jnp.where(front >= n, front - n, front), a + b, t)
        note(t, 0, item, p)
        note(t + 1, 2, item, before)
        a = a + right
        front = org - b
        item, left = choose(jnp.where(front < 0, front + n, front), a + b, t)
        note(t, 1, item, p)
        note(t + 1, 3, item, after)
        b = b + left
        a_ref[...] = a
        b_ref[...] = b
        end_ref[...] = jnp.where(right + left > 0, (t + 1).astype(F32), end_ref[...])
        return carry

    def missing():
        return jnp.sum(n - 1 - a_ref[...] - b_ref[...]).astype(jnp.int32)

    def more(c):
        step(c[0], 0)
        return c[0] + 1, missing()

    lax.fori_loop(0, least, step, 0)
    t, _ = lax.while_loop(lambda c: c[1] > 0, more, (jnp.int32(least), missing()))
    rounds[0] = t
    note(t, 0, none, p)
    note(t, 1, none, p)
    for k in range(count):
        comp[k] = jnp.max(end_ref[pl.ds(k * specials, specials), :]).astype(jnp.int32)


def table_call(n, count, specials, limbs, least, order, pos, spot):
    items = count * specials
    most = items * (n - 1) + 2 * count
    return pl.pallas_call(
        functools.partial(table_kernel, n, count, specials, limbs, least),
        in_specs=[SMEM] * 3,
        out_specs=[pl.BlockSpec(memory_space=pltpu.VMEM), SMEM, SMEM],
        out_shape=[
            jax.ShapeDtypeStruct((-(-PLAN * (most + 1) // (8 * LANES)) * 8, LANES), jnp.int32),
            jax.ShapeDtypeStruct((1,), jnp.int32),
            jax.ShapeDtypeStruct((count,), jnp.int32),
        ],
        scratch_shapes=[pltpu.VMEM((items, LANES), F32)] * 3,
        compiler_params=params(8),
        name="table",
    )(order, in_hbm(pos), spot)


def round_of(tile, t):
    got = [tile[lax.div(f, LANES), lax.rem(f, LANES)] for f in (jnp.asarray(PLAN * t + r, jnp.int32) for r in range(PLAN))]
    return got[:2], got[2:]


def pack_kernel(items, t, first, last, *refs):
    refs = list(refs)
    if t is None:
        t = refs.pop(0)[0]
    table, store = refs.pop(0), refs.pop(0)
    ins = () if first else (refs.pop(0), refs.pop(0))
    refs.pop(0)
    outs = () if last else (refs.pop(0), refs.pop(0))
    tile, keep, send, tsem = refs
    plan = pltpu.make_async_copy(table, tile, tsem)
    plan.start()
    plan.wait()
    go, came = round_of(tile, t)
    for i in range(len(ins)):
        @pl.when(came[i] < items)
        def _():
            pltpu.make_async_copy(ins[i], store.at[came[i]], keep.at[i]).start()

    old = []
    for j in range(len(outs)):
        fresh = [jnp.logical_and(go[j] == came[i], came[i] < items) for i in range(len(ins))]
        held = go[j] < items
        for f in fresh:
            held = jnp.logical_and(held, jnp.logical_not(f))
        old.append(held)

        @pl.when(held)
        def _():
            pltpu.make_async_copy(store.at[go[j]], outs[j], send.at[j]).start()

        for i in range(len(ins)):
            @pl.when(fresh[i])
            def _():
                outs[j][...] = ins[i][...]

    for i in range(len(ins)):
        @pl.when(came[i] < items)
        def _():
            pltpu.make_async_copy(ins[i], store.at[came[i]], keep.at[i]).wait()
    for j in range(len(outs)):
        @pl.when(old[j])
        def _():
            pltpu.make_async_copy(store.at[go[j]], outs[j], send.at[j]).wait()


def pack_call(table, t, store, ins=None, last=False):
    first = ins is None
    store = in_hbm(store)
    items = store.shape[0]
    item = jax.ShapeDtypeStruct(store.shape[1:], store.dtype)
    static = isinstance(t, int)
    args = (() if static else (t.reshape(1),)) + (table, store) + (() if first else tuple(ins))
    at = 1 if static else 2
    outs = [jax.ShapeDtypeStruct(store.shape, store.dtype)] + ([] if last else [item, item])
    size = math.prod(item.shape) * 4
    res = pl.pallas_call(
        functools.partial(pack_kernel, items, t if static else None, first, last),
        in_specs=([] if static else [SMEM]) + [ANY, HBM] + [VMEM] * (0 if first else 2),
        out_specs=[HBM] + [VMEM] * (len(outs) - 1),
        out_shape=outs,
        input_output_aliases={at: 0},
        scratch_shapes=[
            pltpu.SMEM(table.shape, jnp.int32),
            pltpu.SemaphoreType.DMA((2,)),
            pltpu.SemaphoreType.DMA((2,)),
            pltpu.SemaphoreType.DMA,
        ],
        compiler_params=params(2),
        cost_estimate=pl.CostEstimate(flops=0, bytes_accessed=8 * size, transcendentals=0),
        name="pack",
    )(*args)
    return res[0], list(res[1:])


def lower_kernel(low, high, guess, specials, limbs, *refs):
    order, digit, where, scale, conv, comp, diag, mats, *refs = refs
    part, store, refs = refs[:2], refs[2:4], refs[4:]
    last = high is None

    def fetch(k):
        return [
            pltpu.make_async_copy(store[c].at[pl.ds(k * specials, specials)], got.at[c], sem.at[c]) for c in range(2)
        ] + [pltpu.make_async_copy(diag.at[k], dg, sem.at[2])]

    if last:
        t, plan, *refs = refs
        ins, store, keep, send, refs = (refs[0:2], refs[2:4]), refs[4:6], refs[6:8], refs[8:10], refs[10:]
        total, got, dg, xs, sem, tile = refs
        total = [total.at[0], total.at[1]]
        copy = pltpu.make_async_copy(plan, tile, sem.at[7])
        copy.start()
    else:
        total, (got, dg, xs, sem) = refs[:2], refs[4:]
    for copy in fetch(guess):
        copy.start()
    count = diag.shape[0]
    first = where[0] * limbs
    for c in range(2):
        total[c][...] = part[c][...]
    for copy in fetch(guess):
        copy.wait()

    if last:
        pltpu.make_async_copy(plan, tile, sem.at[7]).wait()
        _, came = round_of(tile, t[0])

        def arrive(act):
            for c in range(2):
                for i in range(2):
                    @pl.when(came[i] < store[c].shape[0])
                    def _():
                        act(pltpu.make_async_copy(ins[c][i], store[c].at[came[i]], sem.at[3 + 2 * c + i]))

        arrive(lambda copy: copy.start())
        for i in range(2):
            place = came[i] - guess * specials

            @pl.when(jnp.logical_and(place >= 0, place < specials))
            def _():
                for c in range(2):
                    got[c, place] = ins[c][i][...]

    def turn(i, carry):
        if last:
            @pl.when(i == 1)
            def _():
                arrive(lambda copy: copy.wait())

        k = lax.rem(guess + i, count)
        ripe = comp[k] > low
        if not last:
            ripe = jnp.logical_and(ripe, comp[k] <= high)

        @pl.when(ripe)
        def _():
            @pl.when(i > 0)
            def _():
                for copy in fetch(k):
                    copy.start()
                for copy in fetch(k):
                    copy.wait()

            def limb(m, carry):
                q = first + m

                @pl.when(digit[q] != DIGITS)
                def _():
                    h = (mats[m, 0], mats[m, 1])
                    w = [conv[q, order[DIGITS * specials + s]] for s in range(specials)]
                    size = scale[q]
                    step = 64
                    for c in range(2):
                        for i in range(2):
                            for r in range(0, RADIX, step):
                                x = w[0] * got[c, 0, pl.ds(i * RADIX + r, step), :]
                                for s in range(1, specials):
                                    x = x + w[s] * got[c, s, pl.ds(i * RADIX + r, step), :]
                                hi, lo = split(x)
                                xs[c, 0, pl.ds(r, step), pl.ds(i * LANES, LANES)] = hi
                                xs[c, 1, pl.ds(r, step), pl.ds(i * LANES, LANES)] = lo
                    for c in range(2):
                        y = mm(h, split(mm((xs[c, 0], xs[c, 1]), h)))
                        for i in range(2):
                            at = pl.ds(i * limbs + m, RADIX, stride=2 * limbs)
                            total[c][at, :] = total[c][at, :] - dg[at, :] * size * y[:, i * LANES : (i + 1) * LANES]

                return carry

            lax.fori_loop(0, limbs, limb, 0)

        return carry

    lax.fori_loop(0, count, turn, 0)
    if last:
        half = total[0].shape[0] // 2
        mine = where[1]
        for c in range(2):
            keep[c][...] = total[c][pl.ds(pl.multiple_of(mine * half, half), half), :]
            send[c][...] = total[c][pl.ds(pl.multiple_of((1 - mine) * half, half), half), :]


def lower_call(low, high, guess, order, digit, where, scale, conv, comp, diag, mats, specials, part, store, end=()):
    limbs = mats.shape[0]
    store = [in_hbm(s) for s in store]
    rows = part[0].shape[0]
    half = jax.ShapeDtypeStruct((rows // 2, LANES), F32)
    last = high is None
    shape = lambda a: jax.ShapeDtypeStruct(a.shape, a.dtype)
    scratch = [
        pltpu.VMEM((2, specials, 2 * RADIX, LANES), F32),
        pltpu.VMEM((rows, LANES), F32),
        pltpu.VMEM((2, 2, RADIX, RADIX), BF16),
        pltpu.SemaphoreType.DMA((8,)),
    ]
    if last:
        scratch = [pltpu.VMEM((2, rows, LANES), F32)] + scratch + [pltpu.SMEM(end[1].shape, jnp.int32)]
    return pl.pallas_call(
        functools.partial(lower_kernel, low, high, guess, specials, limbs),
        in_specs=[SMEM] * 6 + [HBM, VMEM, VMEM, VMEM, HBM, HBM] + ([SMEM, ANY] + [VMEM] * 4 if last else []),
        out_specs=[HBM, HBM] + [VMEM] * 4 if last else [VMEM, VMEM, HBM, HBM],
        out_shape=[shape(s) for s in store] + [half] * 4 if last else [shape(p) for p in (*part, *store)],
        input_output_aliases={10: 0, 11: 1} if last else {10: 2, 11: 3},
        scratch_shapes=scratch,
        compiler_params=params(12),
        cost_estimate=pl.CostEstimate(flops=10**9, bytes_accessed=8 * 2**20, transcendentals=0),
        name="lower",
    )(order, in_hbm(digit), where, scale, in_hbm(conv), comp, in_hbm(diag), mats, *part, *store, *end)


def interleave(x):
    *lead, limbs, coeffs = x.shape
    x = x.reshape(*lead, limbs, coeffs // LANES, LANES)
    return jnp.swapaxes(x, -3, -2).reshape(*lead, coeffs // LANES * limbs, LANES)


def per_device(order_of, cipher, rotation_keys, diagonals, shifts, twiddles, moduli, digit_of, conversion):
    n = len(order_of)
    limbs = cipher.shape[0]
    ext = digit_of.shape[0]
    specials = ext // (DIGITS + 1)
    count = rotation_keys.shape[1]
    items = count * specials
    pos_of = np.argsort(np.array(order_of)).astype(np.int32)
    cw = [(order_of[i], order_of[(i + 1) % n]) for i in range(n)]
    ccw = [(b, a) for a, b in cw]
    me, rot = lax.axis_index("limb"), lax.axis_index("rot")
    where = jnp.stack([me, rot]).astype(jnp.int32)
    pos = jnp.asarray(pos_of)
    my_pos = pos[me]
    swap = lambda x: lax.ppermute(x, "rot", [(0, 1), (1, 0)])

    grid = np.arange(RADIX)
    angle = (grid[:, None] * grid[None, :] % RADIX) * (2.0 * math.pi / RADIX)
    base = ((np.cos(angle) + np.sin(angle)) / math.sqrt(RADIX)).astype(np.float32)
    base_hi = base.astype(BF16)
    base_lo = (base - base_hi.astype(np.float32)).astype(BF16)

    rows_c = interleave(cipher)
    keys = interleave(rotation_keys).reshape(count, DIGITS * 2, -1, LANES)
    diag = interleave(diagonals).reshape(count, -1, LANES)

    *coef, mats = coef_call(twiddles, where, jnp.asarray(base_hi), jnp.asarray(base_lo), rows_c, limbs)

    ids = jnp.arange(ext, dtype=jnp.int32)
    before = (digit_of[None, :] < digit_of[:, None]) | (
        (digit_of[None, :] == digit_of[:, None]) & (ids[None, :] < ids[:, None])
    )
    place = jnp.sum(before.astype(jnp.int32), axis=1)
    order = jnp.sum(jnp.where(place[None, :] == ids[:, None], ids[None, :], 0), axis=1)
    slot = lax.dynamic_slice_in_dim(jnp.maximum(place - DIGITS * specials, -1), me * limbs, limbs, 0)
    special = digit_of == DIGITS
    mod = moduli.astype(F32)
    scale = jnp.sum(jnp.where(special[None, :], mod[:, None] / mod[None, :], 0.0), axis=1) / specials
    my_special = lax.dynamic_slice_in_dim(special, me * limbs, limbs, 0)
    my_gain = jnp.where(my_special, 1.0, lax.dynamic_slice_in_dim(scale, me * limbs, limbs, 0))
    rows8 = lambda v: jnp.broadcast_to(jnp.tile(v, 8 // limbs)[:, None], (8, LANES))
    gain = rows8(my_gain)
    fixed = items * n // (2 * n)
    plan, rounds, comp = table_call(n, count, specials, limbs, fixed, order, pos, my_pos.reshape(1))

    cut = limbs // 2
    spans = [(0, cut), (cut, limbs)]
    blocks, lens, steps = list(coef), list(spans), [0, 0]
    right, left = list(coef), list(coef)
    hop = lambda x, ring: lax.ppermute(x, "limb", ring)
    both = (n - 1) // 2
    for r in range(1, both + 1):
        for i in range(2):
            right[i], left[i] = hop(right[i], cw), hop(left[i], ccw)
        blocks += right + left
        lens += spans * 2
        steps += [-r, -r, r, r]
        if r == 2:
            right[1], left[1], order, slot, gain, scale, plan, rounds, comp = lax.optimization_barrier(
                (right[1], left[1], order, slot, gain, scale, plan, rounds, comp)
            )
    if n % 2 == 0:
        blocks += [hop(right[0], cw), hop(left[1], ccw)]
        lens += spans
        steps += [n // 2, n // 2]
    srcs = jnp.asarray(
        np.array([[order_of[(pos_of[d] + s) % n] for s in steps] for d in range(n)], np.int32)
    )[me]

    pad = 64
    mixed = mix_call(n, limbs, tuple(lens), order, digit_of, where, srcs, conversion, blocks)
    raised = raise_call(digit_of, where, mixed, swap(mixed), mats, rows_c, pad)

    def accumulate(k, after=None):
        return accum_call(k, tie(shifts, after), raised, keys, diag, gain, limbs, pad, part)

    def lower(low, high, guess, end=()):
        return lower_call(
            low, high, guess, order, digit_of, where, scale, conversion, comp, diag, mats, specials, part, stores, end
        )

    def tie(x, after):
        return x if after is None else lax.optimization_barrier((x, after))[0]

    def travel(sends):
        return [lax.ppermute(sends[0], "limb", cw), lax.ppermute(sends[1], "limb", ccw)]

    tasks = {max(2 * k - 3, 0): k for k in range(1, count)}, {max(2 * k - 2, 0): k for k in range(1, count)}
    gates = {fixed - 5: 0, fixed - 3: 1, fixed - 1: 2}
    part, stores, ins, low = None, None, [None, None], -1
    *part, acc = accumulate(0)
    stores = list(emit_call(0, slot, acc, mats, specials, items, stores))
    for t in range(fixed):
        for c in range(2):
            stores[c], sends = pack_call(plan, t, stores[c], ins[c])
            ins[c] = travel(sends)
        if t in tasks[0]:
            *part, acc = accumulate(tasks[0][t], sends[0])
            stores[0], acc = lax.optimization_barrier((stores[0], acc))
        if t in tasks[1]:
            stores = list(emit_call(tasks[1][t], slot, tie(acc, sends[0]), mats, specials, items, stores))
        if t in gates:
            *part, stores[0], stores[1] = lower(low, t, min(gates[t], count - 1))
            low = t

    def more(state):
        return state[0] < rounds[0]

    def one(state):
        t, stores, ins = state
        stores, ins = list(stores), list(ins)
        for c in range(2):
            stores[c], sends = pack_call(plan, t, stores[c], ins[c])
            ins[c] = travel(sends)
        return t + 1, stores, ins

    t, stores, ins = lax.while_loop(more, one, (jnp.int32(fixed), stores, ins))
    _, _, *halves = lower(low, None, count - 1, (t.reshape(1), plan, *ins[0], *ins[1]))
    total = jnp.stack([keep + swap(send) for keep, send in zip(halves[:2], halves[2:])])
    total = jnp.swapaxes(total.reshape(2, -1, limbs, LANES), 1, 2)
    return total.reshape(2, limbs, -1)


def solution(mesh):
    in_specs = (
        P(("parts", "limb"), None),
        P("rot", None, None, None, "limb", None),
        P("rot", None, "limb", None),
        P("rot", None),
        P(),
        P(),
        P(),
        P(),
    )
    out_specs = P(None, ("parts", "limb"), "rot")
    return jax.shard_map(
        functools.partial(per_device, ring_order(mesh)),
        mesh=mesh,
        in_specs=in_specs,
        out_specs=out_specs,
        check_vma=False,
    )
```

```python
import functools
import math

import jax
import jax.numpy as jnp
import numpy as np
from jax import lax
from jax.experimental import pallas as pl
from jax.experimental.pallas import tpu as pltpu
from jax.sharding import PartitionSpec as P

RADIX = 256
DIGITS = 3
LANES = 128
PLAN = 4
F32 = jnp.float32
BF16 = jnp.bfloat16


ANY = pl.BlockSpec(memory_space=pl.ANY)
VMEM = pl.BlockSpec(memory_space=pltpu.VMEM)
HBM = pl.BlockSpec(memory_space=pltpu.HBM)
SMEM = pl.BlockSpec(memory_space=pltpu.SMEM)


def ring_order(mesh):
    n = mesh.shape["limb"]
    line = np.moveaxis(mesh.devices, list(mesh.axis_names).index("limb"), 0).reshape(n, -1)[:, 0]
    at = [getattr(d, "coords", None) for d in line]
    if any(c is None for c in at):
        return list(range(n))
    near = [
        [j for j in range(n) if sum(abs(x - y) for x, y in zip(at[i], at[j])) == 1] for i in range(n)
    ]

    def walk(path):
        if len(path) == n:
            return path if 0 in near[path[-1]] else None
        for j in near[path[-1]]:
            if j not in path:
                found = walk(path + [j])
                if found:
                    return found
        return None

    return walk([0]) or list(range(n))


def split(x):
    hi = x.astype(BF16)
    return hi, (x - hi.astype(F32)).astype(BF16)


def mm(a, b):
    dot = functools.partial(jnp.dot, preferred_element_type=F32)
    return dot(a[0], b[0]) + dot(a[1], b[0]) + dot(a[0], b[1])


def spin(x, h):
    return mm(h, split(mm(split(x), h)))


def grid_of(ref, m, limbs):
    left = ref[pl.ds(m, RADIX, stride=2 * limbs), :]
    right = ref[pl.ds(limbs + m, RADIX, stride=2 * limbs), :]
    return jnp.concatenate([left, right], axis=1)


def in_hbm(x):
    return pltpu.with_memory_space_constraint(x, pltpu.HBM)


def params(mib):
    return pltpu.CompilerParams(vmem_limit_bytes=mib * 2**20)


def coef_kernel(tw, where, base_hi, base_lo, cipher, coef0, coef1, mats, grid, bases, sem):
    limbs = mats.shape[0]
    cut = coef0.shape[0]
    copies = [
        pltpu.make_async_copy(base_hi, bases.at[0], sem.at[0]),
        pltpu.make_async_copy(base_lo, bases.at[1], sem.at[1]),
        pltpu.make_async_copy(cipher, grid, sem.at[2]),
    ]
    for copy in copies:
        copy.start()
    row = lax.broadcasted_iota(jnp.int32, (RADIX, RADIX), 0)
    col = lax.broadcasted_iota(jnp.int32, (RADIX, RADIX), 1)
    first = where[1] == 0
    for copy in copies:
        copy.wait()

    def limb(coef, start, m, carry):
        g = tw[where[0] * limbs + m]
        pick = jnp.where(((row * g) & (RADIX - 1)) == col, 1.0, 0.0).astype(BF16)
        hi = jnp.dot(pick, bases[0], preferred_element_type=F32).astype(BF16)
        lo = jnp.dot(pick, bases[1], preferred_element_type=F32).astype(BF16)
        mats[m, 0] = hi
        mats[m, 1] = lo
        u = split(mm((hi, lo), split(grid_of(grid, m, limbs))))
        half = tuple(
            jnp.where(first, h[:, :LANES].astype(F32), h[:, LANES:].astype(F32)).astype(BF16) for h in (hi, lo)
        )
        coef[m - start] = mm(u, half)
        return carry

    lax.fori_loop(0, cut, functools.partial(limb, coef0, 0), 0, unroll=True)
    lax.fori_loop(cut, limbs, functools.partial(limb, coef1, cut), 0, unroll=True)


def coef_call(tw, where, base_hi, base_lo, cipher, limbs):
    return pl.pallas_call(
        coef_kernel,
        in_specs=[SMEM, SMEM, HBM, HBM, HBM],
        out_specs=[VMEM, VMEM, VMEM],
        out_shape=[
            jax.ShapeDtypeStruct((limbs // 2, RADIX, LANES), F32),
            jax.ShapeDtypeStruct((limbs - limbs // 2, RADIX, LANES), F32),
            jax.ShapeDtypeStruct((limbs, 2, RADIX, RADIX), BF16),
        ],
        scratch_shapes=[
            pltpu.VMEM(cipher.shape, F32),
            pltpu.VMEM((2, RADIX, RADIX), BF16),
            pltpu.SemaphoreType.DMA((3,)),
        ],
        compiler_params=params(12),
        name="coef",
    )(in_hbm(tw), where, in_hbm(base_hi), in_hbm(base_lo), in_hbm(cipher))


def mix_kernel(n, limbs, lens, order, digit, where, srcs, conv, *refs):
    blocks, out, got, table, sem = refs[: len(lens)], refs[-4], refs[-3], refs[-2], refs[-1]
    size = got.shape[0] * limbs // (DIGITS + 1)
    copies = []
    for i, (start, stop) in enumerate(lens):
        c = pltpu.make_async_copy(blocks[i], got.at[srcs[i], pl.ds(start, stop - start)], sem.at[i])
        c.start()
        copies.append(c)
    first = where[0] * limbs
    for j in range(DIGITS * size):
        l = order[j]
        for m in range(limbs):
            same = digit[l] == digit[first + m]
            one = jnp.where(first + m == l, 1.0, 0.0)
            table[m, j] = jnp.where(same, one, conv[first + m, l])
    for c in copies:
        c.wait()
    step = 64

    def rows(r, carry):
        r0 = pl.multiple_of(r * step, step)
        for d in range(DIGITS):
            acc = [jnp.zeros((step, LANES), F32) for _ in range(limbs)]
            for j in range(size):
                l = order[d * size + j]
                x = got[l // limbs, l % limbs, pl.ds(r0, step), :]
                for m in range(limbs):
                    acc[m] = acc[m] + table[m, d * size + j] * x
            for m in range(limbs):
                out[d, m, pl.ds(r0, step), :] = acc[m]
        return carry

    lax.fori_loop(0, RADIX // step, rows, 0)


def mix_call(n, limbs, lens, order, digit, where, srcs, conv, blocks):
    vmem = pl.BlockSpec(memory_space=pltpu.VMEM)
    return pl.pallas_call(
        functools.partial(mix_kernel, n, limbs, lens),
        in_specs=[SMEM] * 5 + [HBM] * len(blocks),
        out_specs=vmem,
        out_shape=jax.ShapeDtypeStruct((DIGITS, limbs, RADIX, LANES), F32),
        scratch_shapes=[
            pltpu.VMEM((n, limbs, RADIX, LANES), F32),
            pltpu.SMEM((limbs, n * limbs), F32),
            pltpu.SemaphoreType.DMA((len(blocks),)),
        ],
        compiler_params=params(16),
        name="mix",
    )(order, in_hbm(digit), where, srcs, in_hbm(conv), *blocks)


def raise_kernel(pad, digit, where, own, other, mats, cipher, out, rows_in, sem):
    limbs = mats.shape[0]
    rows = cipher.shape[0]
    swapped = where[1] != 0
    fetch = pltpu.make_async_copy(cipher, rows_in, sem)
    fetch.start()

    def at(m, h):
        return pl.ds(h * limbs + m, RADIX, stride=2 * limbs)

    def convert(m, carry):
        h = (mats[m, 0], mats[m, 1])
        for d in range(DIGITS):
            a, b = own[d, m], other[d, m]
            x = jnp.concatenate([jnp.where(swapped, b, a), jnp.where(swapped, a, b)], axis=1)
            y = spin(x, h)
            for i in range(2):
                out[d, at(m, i), :] = y[:, i * LANES : (i + 1) * LANES]
        return carry

    lax.fori_loop(0, limbs, convert, 0)
    fetch.wait()

    def place(m, carry):
        d = digit[where[0] * limbs + m]
        for h in range(2):
            out[d, at(m, h), :] = rows_in[at(m, h), :]

        @pl.when(d != DIGITS)
        def _():
            for h in range(2):
                out[DIGITS, at(m, h), :] = jnp.zeros((RADIX, LANES), F32)

        return carry

    lax.fori_loop(0, limbs, place, 0)
    for d in range(DIGITS + 1):
        out[d, pl.ds(rows, pad), :] = out[d, pl.ds(0, pad), :]


def raise_call(digit, where, own, other, mats, cipher, pad):
    rows = cipher.shape[0]
    return pl.pallas_call(
        functools.partial(raise_kernel, pad),
        in_specs=[SMEM, SMEM] + [VMEM] * 3 + [HBM],
        out_specs=VMEM,
        out_shape=jax.ShapeDtypeStruct((DIGITS + 1, rows + pad, LANES), F32),
        scratch_shapes=[pltpu.VMEM(cipher.shape, F32), pltpu.SemaphoreType.DMA],
        compiler_params=params(16),
        name="raise",
    )(in_hbm(digit), where, own, other, mats, in_hbm(cipher))


def accum_kernel(k, limbs, pad, shifts, raised, keys, diag, gain, *refs):
    part, acc, kbuf, dbuf, small, sem, ksem = refs[-8:-6], *refs[-6:]
    rows = acc.shape[1]
    pieces = ksem.shape[0]
    block = rows // pieces

    def fetch(i):
        at = pl.ds(pl.multiple_of(i * block, block), block)
        return [
            pltpu.make_async_copy(keys.at[k, :, at], kbuf.at[:, at], ksem.at[i, 0]),
            pltpu.make_async_copy(diag.at[k, at], dbuf.at[at], ksem.at[i, 1]),
        ]

    amounts = pltpu.make_async_copy(shifts, small, sem)
    amounts.start()
    for i in range(pieces):
        for copy in fetch(i):
            copy.start()
    amounts.wait()
    s = small[0, k]
    tiles, lane = s // LANES, s % LANES
    here = lax.broadcasted_iota(jnp.int32, (pad, LANES), 1) < LANES - lane
    g8 = jnp.concatenate([gain[...]] * (pad // 8), axis=0)

    def piece(i, carry):
        for copy in fetch(i):
            copy.wait()

        def add(r, carry):
            at = pl.multiple_of(i * block + r * pad, pad)
            u0 = lax.rem(at - limbs * tiles + rows, rows)
            v0 = lax.rem(at - limbs * tiles - limbs + 2 * rows, rows)
            turned = []
            for g in range(DIGITS + 1):
                u = raised[g, pl.ds(pl.multiple_of(u0, limbs), pad), :]
                v = raised[g, pl.ds(pl.multiple_of(v0, limbs), pad), :]
                turned.append(pltpu.roll(jnp.where(here, u, v), lane, axis=1))
            w = dbuf[pl.ds(at, pad), :] * g8
            for c in range(2):
                a = turned[DIGITS]
                for d in range(DIGITS):
                    a = a + turned[d] * kbuf[2 * d + c, pl.ds(at, pad), :]
                acc[c, pl.ds(at, pad), :] = a
                w_a = w * a
                part[c][pl.ds(at, pad), :] = w_a if k == 0 else refs[c][pl.ds(at, pad), :] + w_a
            return carry

        return lax.fori_loop(0, block // pad, add, carry, unroll=2)

    lax.fori_loop(0, pieces, piece, 0)


def accum_call(k, shifts, raised, keys, diag, gain, limbs, pad, part):
    rows = raised.shape[1] - pad
    args = (in_hbm(shifts), raised, in_hbm(keys), in_hbm(diag), gain)
    specs = [HBM, VMEM, HBM, HBM, VMEM]
    alias = {}
    if part is not None:
        alias = {len(args) + i: i for i in range(2)}
        args += tuple(part)
        specs += [VMEM, VMEM]
    one = jax.ShapeDtypeStruct((rows, LANES), F32)
    return pl.pallas_call(
        functools.partial(accum_kernel, k, limbs, pad),
        in_specs=specs,
        out_specs=[VMEM, VMEM, VMEM],
        out_shape=[one, one, jax.ShapeDtypeStruct((2, rows, LANES), F32)],
        input_output_aliases=alias,
        scratch_shapes=[
            pltpu.VMEM(keys.shape[1:], F32),
            pltpu.VMEM((rows, LANES), F32),
            pltpu.SMEM(shifts.shape, jnp.int32),
            pltpu.SemaphoreType.DMA,
            pltpu.SemaphoreType.DMA((8, 2)),
        ],
        compiler_params=params(12),
        cost_estimate=pl.CostEstimate(flops=10**8, bytes_accessed=8 * 2**20, transcendentals=0),
        name="accum",
    )(*args)


def emit_kernel(k, limbs, specials, slot, acc, mats, *refs):
    store, stage, sem = refs[-4:-2], refs[-2], refs[-1]

    def emit(m, carry):
        @pl.when(slot[m] >= 0)
        def _():
            h = (mats[m, 0], mats[m, 1])
            copies = []
            for c in range(2):
                y = spin(grid_of(acc.at[c], m, limbs), h)
                stage[c, 0:RADIX, :] = y[:, :LANES]
                stage[c, RADIX:, :] = y[:, LANES:]
                copies.append(pltpu.make_async_copy(stage.at[c], store[c].at[k * specials + slot[m]], sem.at[c]))
                copies[-1].start()
            for copy in copies:
                copy.wait()

        return carry

    lax.fori_loop(0, limbs, emit, 0)


def emit_call(k, slot, acc, mats, specials, items, store):
    one = jax.ShapeDtypeStruct((items, 2 * RADIX, LANES), F32)
    args, specs, alias = (slot, acc, mats), [SMEM, VMEM, VMEM], {}
    if store is not None:
        alias = {len(args) + i: i for i in range(2)}
        args += tuple(map(in_hbm, store))
        specs += [HBM, HBM]
    return pl.pallas_call(
        functools.partial(emit_kernel, k, mats.shape[0], specials),
        in_specs=specs,
        out_specs=[HBM, HBM],
        out_shape=[one, one],
        input_output_aliases=alias,
        scratch_shapes=[pltpu.VMEM((2, 2 * RADIX, LANES), F32), pltpu.SemaphoreType.DMA((2,))],
        compiler_params=params(8),
        cost_estimate=pl.CostEstimate(flops=10**9, bytes_accessed=2**20, transcendentals=0),
        name="emit",
    )(*args)


def table_kernel(n, count, specials, limbs, least, order, pos, spot, plan, rounds, comp, a_ref, b_ref, end_ref):
    items = count * specials
    shape = (items, LANES)
    row_i = lax.broadcasted_iota(jnp.int32, shape, 0)
    row = row_i.astype(F32)
    lane = lax.broadcasted_iota(jnp.int32, shape, 1).astype(F32)
    kind, turn = lax.rem(row_i, specials), lax.div(row_i, specials)
    ready = jnp.maximum(2 * turn - 1, 0)
    weight = 3.0 * turn.astype(F32)
    p = spot[0]
    before, after = lax.rem(p + n - 1, n), lax.rem(p + 1, n)
    line = lax.broadcasted_iota(jnp.int32, (1, LANES), 1)
    org = jnp.zeros(shape, F32)
    for s in range(specials):
        owner = pos[lax.div(order[DIGITS * specials + s], limbs)]
        org = jnp.where(kind == s, owner.astype(F32), org)
    a_ref[...] = jnp.zeros(shape, F32)
    b_ref[...] = jnp.zeros(shape, F32)
    end_ref[...] = jnp.zeros(shape, F32)
    big = float(items * (2 * n + 3 * count))

    def choose(front, spread, t):
        open_ = jnp.logical_and(spread < n - 1, ready <= t)
        cand = jnp.logical_and(open_, front == lane)
        key = jnp.where(cand, (2.0 * spread + weight) * items + row, big)
        best = jnp.min(key, axis=0, keepdims=True)
        hit = jnp.where(jnp.logical_and(cand, key == best), 1.0, 0.0)
        item = jnp.sum(hit * (row - items), axis=0, keepdims=True) + items
        return item, jnp.sum(hit, axis=1, keepdims=True)

    def note(t, r, item, where):
        t = jnp.asarray(t, jnp.int32)
        mine = jnp.sum(jnp.where(line == where, item, 0.0), axis=1, keepdims=True)
        at = pl.ds(lax.div(PLAN * t + r, LANES), 1)
        here = line == lax.rem(PLAN * t + r, LANES)
        plan[at, :] = jnp.where(here, jnp.broadcast_to(mine, (1, LANES)).astype(jnp.int32), plan[at, :])

    none = jnp.full((1, LANES), float(items), F32)
    plan[...] = jnp.full(plan.shape, items, jnp.int32)
    note(0, 2, none, p)
    note(0, 3, none, p)

    def step(t, carry):
        a, b = a_ref[...], b_ref[...]
        front = org + a
        item, right = choose(jnp.where(front >= n, front - n, front), a + b, t)
        note(t, 0, item, p)
        note(t + 1, 2, item, before)
        a = a + right
        front = org - b
        item, left = choose(jnp.where(front < 0, front + n, front), a + b, t)
        note(t, 1, item, p)
        note(t + 1, 3, item, after)
        b = b + left
        a_ref[...] = a
        b_ref[...] = b
        end_ref[...] = jnp.where(right + left > 0, (t + 1).astype(F32), end_ref[...])
        return carry

    def missing():
        return jnp.sum(n - 1 - a_ref[...] - b_ref[...]).astype(jnp.int32)

    def more(c):
        step(c[0], 0)
        return c[0] + 1, missing()

    lax.fori_loop(0, least, step, 0)
    t, _ = lax.while_loop(lambda c: c[1] > 0, more, (jnp.int32(least), missing()))
    rounds[0] = t
    note(t, 0, none, p)
    note(t, 1, none, p)
    for k in range(count):
        comp[k] = jnp.max(end_ref[pl.ds(k * specials, specials), :]).astype(jnp.int32)


def table_call(n, count, specials, limbs, least, order, pos, spot):
    items = count * specials
    most = items * (n - 1) + 2 * count
    return pl.pallas_call(
        functools.partial(table_kernel, n, count, specials, limbs, least),
        in_specs=[SMEM] * 3,
        out_specs=[pl.BlockSpec(memory_space=pltpu.VMEM), SMEM, SMEM],
        out_shape=[
            jax.ShapeDtypeStruct((-(-PLAN * (most + 1) // (8 * LANES)) * 8, LANES), jnp.int32),
            jax.ShapeDtypeStruct((1,), jnp.int32),
            jax.ShapeDtypeStruct((count,), jnp.int32),
        ],
        scratch_shapes=[pltpu.VMEM((items, LANES), F32)] * 3,
        compiler_params=params(8),
        name="table",
    )(order, in_hbm(pos), spot)


def round_of(tile, t):
    got = [tile[lax.div(f, LANES), lax.rem(f, LANES)] for f in (jnp.asarray(PLAN * t + r, jnp.int32) for r in range(PLAN))]
    return got[:2], got[2:]


def pack_kernel(items, t, first, last, *refs):
    refs = list(refs)
    if t is None:
        t = refs.pop(0)[0]
    table, store = refs.pop(0), refs.pop(0)
    ins = () if first else (refs.pop(0), refs.pop(0))
    refs.pop(0)
    outs = () if last else (refs.pop(0), refs.pop(0))
    tile, keep, send, tsem = refs
    plan = pltpu.make_async_copy(table, tile, tsem)
    plan.start()
    plan.wait()
    go, came = round_of(tile, t)
    for i in range(len(ins)):
        @pl.when(came[i] < items)
        def _():
            pltpu.make_async_copy(ins[i], store.at[came[i]], keep.at[i]).start()

    old = []
    for j in range(len(outs)):
        fresh = [jnp.logical_and(go[j] == came[i], came[i] < items) for i in range(len(ins))]
        held = go[j] < items
        for f in fresh:
            held = jnp.logical_and(held, jnp.logical_not(f))
        old.append(held)

        @pl.when(held)
        def _():
            pltpu.make_async_copy(store.at[go[j]], outs[j], send.at[j]).start()

        for i in range(len(ins)):
            @pl.when(fresh[i])
            def _():
                outs[j][...] = ins[i][...]

    for i in range(len(ins)):
        @pl.when(came[i] < items)
        def _():
            pltpu.make_async_copy(ins[i], store.at[came[i]], keep.at[i]).wait()
    for j in range(len(outs)):
        @pl.when(old[j])
        def _():
            pltpu.make_async_copy(store.at[go[j]], outs[j], send.at[j]).wait()


def pack_call(table, t, store, ins=None, last=False):
    first = ins is None
    store = in_hbm(store)
    items = store.shape[0]
    item = jax.ShapeDtypeStruct(store.shape[1:], store.dtype)
    static = isinstance(t, int)
    args = (() if static else (t.reshape(1),)) + (table, store) + (() if first else tuple(ins))
    at = 1 if static else 2
    outs = [jax.ShapeDtypeStruct(store.shape, store.dtype)] + ([] if last else [item, item])
    size = math.prod(item.shape) * 4
    res = pl.pallas_call(
        functools.partial(pack_kernel, items, t if static else None, first, last),
        in_specs=([] if static else [SMEM]) + [ANY, HBM] + [VMEM] * (0 if first else 2),
        out_specs=[HBM] + [VMEM] * (len(outs) - 1),
        out_shape=outs,
        input_output_aliases={at: 0},
        scratch_shapes=[
            pltpu.SMEM(table.shape, jnp.int32),
            pltpu.SemaphoreType.DMA((2,)),
            pltpu.SemaphoreType.DMA((2,)),
            pltpu.SemaphoreType.DMA,
        ],
        compiler_params=params(2),
        cost_estimate=pl.CostEstimate(flops=0, bytes_accessed=8 * size, transcendentals=0),
        name="pack",
    )(*args)
    return res[0], list(res[1:])


def lower_kernel(low, high, guess, specials, limbs, *refs):
    tables, (diag, mats, *refs) = refs[:6], refs[6:]
    small, smem, refs = refs[-7:-1], refs[-1], refs[:-7]
    part, store, refs = refs[:2], refs[2:4], refs[4:]
    last = high is None
    scalars = [pltpu.make_async_copy(a, b, smem.at[i]) for i, (a, b) in enumerate(zip(tables, small))]
    order, digit, where, scale, conv, comp = small

    def fetch(k):
        return [
            pltpu.make_async_copy(store[c].at[pl.ds(k * specials, specials)], got.at[c], sem.at[c]) for c in range(2)
        ] + [pltpu.make_async_copy(diag.at[k], dg, sem.at[2])]

    if last:
        t, plan, *refs = refs
        ins, store, keep, send, refs = (refs[0:2], refs[2:4]), refs[4:6], refs[6:8], refs[8:10], refs[10:]
        total, got, dg, xs, sem, tile = refs
        total = [total.at[0], total.at[1]]
        copy = pltpu.make_async_copy(plan, tile, sem.at[7])
        copy.start()
    else:
        total, (got, dg, xs, sem) = refs[:2], refs[4:]
    scalars += [pltpu.make_async_copy(part[c], total[c], smem.at[len(small) + c]) for c in range(2)]
    for copy in fetch(guess) + scalars:
        copy.start()
    for copy in scalars + fetch(guess):
        copy.wait()
    count = diag.shape[0]
    first = where[0] * limbs

    if last:
        pltpu.make_async_copy(plan, tile, sem.at[7]).wait()
        _, came = round_of(tile, t[0])

        def arrive(act):
            for c in range(2):
                for i in range(2):
                    @pl.when(came[i] < store[c].shape[0])
                    def _():
                        act(pltpu.make_async_copy(ins[c][i], store[c].at[came[i]], sem.at[3 + 2 * c + i]))

        arrive(lambda copy: copy.start())
        for i in range(2):
            place = came[i] - guess * specials

            @pl.when(jnp.logical_and(place >= 0, place < specials))
            def _():
                for c in range(2):
                    got[c, place] = ins[c][i][...]

    def turn(i, carry):
        if last:
            @pl.when(i == 1)
            def _():
                arrive(lambda copy: copy.wait())

        k = lax.rem(guess + i, count)
        ripe = comp[k] > low
        if not last:
            ripe = jnp.logical_and(ripe, comp[k] <= high)

        @pl.when(ripe)
        def _():
            @pl.when(i > 0)
            def _():
                for copy in fetch(k):
                    copy.start()
                for copy in fetch(k):
                    copy.wait()

            def limb(m, carry):
                q = first + m

                @pl.when(digit[q] != DIGITS)
                def _():
                    h = (mats[m, 0], mats[m, 1])
                    w = [conv[q, order[DIGITS * specials + s]] for s in range(specials)]
                    size = scale[q]
                    step = 64
                    for c in range(2):
                        for i in range(2):
                            for r in range(0, RADIX, step):
                                x = w[0] * got[c, 0, pl.ds(i * RADIX + r, step), :]
                                for s in range(1, specials):
                                    x = x + w[s] * got[c, s, pl.ds(i * RADIX + r, step), :]
                                hi, lo = split(x)
                                xs[c, 0, pl.ds(r, step), pl.ds(i * LANES, LANES)] = hi
                                xs[c, 1, pl.ds(r, step), pl.ds(i * LANES, LANES)] = lo
                    for c in range(2):
                        y = mm(h, split(mm((xs[c, 0], xs[c, 1]), h)))
                        for i in range(2):
                            at = pl.ds(i * limbs + m, RADIX, stride=2 * limbs)
                            total[c][at, :] = total[c][at, :] - dg[at, :] * size * y[:, i * LANES : (i + 1) * LANES]

                return carry

            lax.fori_loop(0, limbs, limb, 0)

        return carry

    lax.fori_loop(0, count, turn, 0)
    if last:
        half = total[0].shape[0] // 2
        mine = where[1]
        for c in range(2):
            keep[c][...] = total[c][pl.ds(pl.multiple_of(mine * half, half), half), :]
            send[c][...] = total[c][pl.ds(pl.multiple_of((1 - mine) * half, half), half), :]


def lower_call(low, high, guess, order, digit, where, scale, conv, comp, diag, mats, specials, part, store, end=()):
    limbs = mats.shape[0]
    store = [in_hbm(s) for s in store]
    rows = part[0].shape[0]
    half = jax.ShapeDtypeStruct((rows // 2, LANES), F32)
    last = high is None
    part = part if last else [in_hbm(p) for p in part]
    shape = lambda a: jax.ShapeDtypeStruct(a.shape, a.dtype)
    scratch = [
        pltpu.VMEM((2, specials, 2 * RADIX, LANES), F32),
        pltpu.VMEM((rows, LANES), F32),
        pltpu.VMEM((2, 2, RADIX, RADIX), BF16),
        pltpu.SemaphoreType.DMA((8,)),
    ]
    if last:
        scratch = [pltpu.VMEM((2, rows, LANES), F32)] + scratch + [pltpu.SMEM(end[1].shape, jnp.int32)]
    tables = (order, in_hbm(digit), where, scale, in_hbm(conv), comp)
    scratch += [pltpu.SMEM(a.shape, a.dtype) for a in tables] + [pltpu.SemaphoreType.DMA((len(tables) + 2,))]
    return pl.pallas_call(
        functools.partial(lower_kernel, low, high, guess, specials, limbs),
        in_specs=[ANY] * 6 + [HBM, VMEM, ANY, ANY, HBM, HBM] + ([SMEM, ANY] + [VMEM] * 4 if last else []),
        out_specs=[HBM, HBM] + [VMEM] * 4 if last else [VMEM, VMEM, HBM, HBM],
        out_shape=[shape(s) for s in store] + [half] * 4 if last else [shape(p) for p in (*part, *store)],
        input_output_aliases={10: 0, 11: 1} if last else {10: 2, 11: 3},
        scratch_shapes=scratch,
        compiler_params=params(12),
        cost_estimate=pl.CostEstimate(flops=10**9, bytes_accessed=8 * 2**20, transcendentals=0),
        name="lower",
    )(*tables, in_hbm(diag), mats, *part, *store, *end)


def interleave(x):
    *lead, limbs, coeffs = x.shape
    x = x.reshape(*lead, limbs, coeffs // LANES, LANES)
    return jnp.swapaxes(x, -3, -2).reshape(*lead, coeffs // LANES * limbs, LANES)


def per_device(order_of, cipher, rotation_keys, diagonals, shifts, twiddles, moduli, digit_of, conversion):
    n = len(order_of)
    limbs = cipher.shape[0]
    ext = digit_of.shape[0]
    specials = ext // (DIGITS + 1)
    count = rotation_keys.shape[1]
    items = count * specials
    pos_of = np.argsort(np.array(order_of)).astype(np.int32)
    cw = [(order_of[i], order_of[(i + 1) % n]) for i in range(n)]
    ccw = [(b, a) for a, b in cw]
    me, rot = lax.axis_index("limb"), lax.axis_index("rot")
    where = jnp.stack([me, rot]).astype(jnp.int32)
    pos = jnp.asarray(pos_of)
    my_pos = pos[me]
    swap = lambda x: lax.ppermute(x, "rot", [(0, 1), (1, 0)])

    grid = np.arange(RADIX)
    angle = (grid[:, None] * grid[None, :] % RADIX) * (2.0 * math.pi / RADIX)
    base = ((np.cos(angle) + np.sin(angle)) / math.sqrt(RADIX)).astype(np.float32)
    base_hi = base.astype(BF16)
    base_lo = (base - base_hi.astype(np.float32)).astype(BF16)

    rows_c = interleave(cipher)
    keys = interleave(rotation_keys).reshape(count, DIGITS * 2, -1, LANES)
    diag = interleave(diagonals).reshape(count, -1, LANES)

    *coef, mats = coef_call(twiddles, where, jnp.asarray(base_hi), jnp.asarray(base_lo), rows_c, limbs)

    ids = jnp.arange(ext, dtype=jnp.int32)
    before = (digit_of[None, :] < digit_of[:, None]) | (
        (digit_of[None, :] == digit_of[:, None]) & (ids[None, :] < ids[:, None])
    )
    place = jnp.sum(before.astype(jnp.int32), axis=1)
    order = jnp.sum(jnp.where(place[None, :] == ids[:, None], ids[None, :], 0), axis=1)
    slot = lax.dynamic_slice_in_dim(jnp.maximum(place - DIGITS * specials, -1), me * limbs, limbs, 0)
    special = digit_of == DIGITS
    mod = moduli.astype(F32)
    scale = jnp.sum(jnp.where(special[None, :], mod[:, None] / mod[None, :], 0.0), axis=1) / specials
    my_special = lax.dynamic_slice_in_dim(special, me * limbs, limbs, 0)
    my_gain = jnp.where(my_special, 1.0, lax.dynamic_slice_in_dim(scale, me * limbs, limbs, 0))
    rows8 = lambda v: jnp.broadcast_to(jnp.tile(v, 8 // limbs)[:, None], (8, LANES))
    gain = rows8(my_gain)
    fixed = items * n // (2 * n)
    plan, rounds, comp = table_call(n, count, specials, limbs, fixed, order, pos, my_pos.reshape(1))

    cut = limbs // 2
    spans = [(0, cut), (cut, limbs)]
    blocks, lens, steps = list(coef), list(spans), [0, 0]
    right, left = list(coef), list(coef)
    hop = lambda x, ring: lax.ppermute(x, "limb", ring)
    both = (n - 1) // 2
    for r in range(1, both + 1):
        for i in range(2):
            right[i], left[i] = hop(right[i], cw), hop(left[i], ccw)
        blocks += right + left
        lens += spans * 2
        steps += [-r, -r, r, r]
        if r == 2:
            right[1], left[1], order, slot, gain, scale, plan, rounds, comp = lax.optimization_barrier(
                (right[1], left[1], order, slot, gain, scale, plan, rounds, comp)
            )
    if n % 2 == 0:
        blocks += [hop(right[0], cw), hop(left[1], ccw)]
        lens += spans
        steps += [n // 2, n // 2]
    srcs = jnp.asarray(
        np.array([[order_of[(pos_of[d] + s) % n] for s in steps] for d in range(n)], np.int32)
    )[me]

    pad = 64
    mixed = mix_call(n, limbs, tuple(lens), order, digit_of, where, srcs, conversion, blocks)
    raised = raise_call(digit_of, where, mixed, swap(mixed), mats, rows_c, pad)

    def accumulate(k, after=None):
        return accum_call(k, tie(shifts, after), raised, keys, diag, gain, limbs, pad, part)

    def lower(low, high, guess, end=()):
        return lower_call(
            low, high, guess, order, digit_of, where, scale, conversion, comp, diag, mats, specials, part, stores, end
        )

    def tie(x, after):
        return x if after is None else lax.optimization_barrier((x, after))[0]

    def travel(sends):
        return [lax.ppermute(sends[0], "limb", cw), lax.ppermute(sends[1], "limb", ccw)]

    tasks = {max(2 * k - 3, 0): k for k in range(1, count)}, {max(2 * k - 2, 0): k for k in range(1, count)}
    gates = {fixed - 5: 0, fixed - 3: 1, fixed - 1: 2}
    part, stores, ins, low = None, None, [None, None], -1
    *part, acc = accumulate(0)
    stores = list(emit_call(0, slot, acc, mats, specials, items, stores))
    for t in range(fixed):
        for c in range(2):
            stores[c], sends = pack_call(plan, t, stores[c], ins[c])
            ins[c] = travel(sends)
        if t in tasks[0]:
            *part, acc = accumulate(tasks[0][t], sends[0])
            stores[0], acc = lax.optimization_barrier((stores[0], acc))
        if t in tasks[1]:
            stores = list(emit_call(tasks[1][t], slot, tie(acc, sends[0]), mats, specials, items, stores))
        if t in gates:
            *part, stores[0], stores[1] = lower(low, t, min(gates[t], count - 1))
            low = t

    def more(state):
        return state[0] < rounds[0]

    def one(state):
        t, stores, ins = state
        stores, ins = list(stores), list(ins)
        for c in range(2):
            stores[c], sends = pack_call(plan, t, stores[c], ins[c])
            ins[c] = travel(sends)
        return t + 1, stores, ins

    t, stores, ins = lax.while_loop(more, one, (jnp.int32(fixed), stores, ins))
    _, _, *halves = lower(low, None, count - 1, (t.reshape(1), plan, *ins[0], *ins[1]))
    total = jnp.stack([keep + swap(send) for keep, send in zip(halves[:2], halves[2:])])
    total = jnp.swapaxes(total.reshape(2, -1, limbs, LANES), 1, 2)
    return total.reshape(2, limbs, -1)


def solution(mesh):
    in_specs = (
        P(("parts", "limb"), None),
        P("rot", None, None, None, "limb", None),
        P("rot", None, "limb", None),
        P("rot", None),
        P(),
        P(),
        P(),
        P(),
    )
    out_specs = P(None, ("parts", "limb"), "rot")
    return jax.shard_map(
        functools.partial(per_device, ring_order(mesh)),
        mesh=mesh,
        in_specs=in_specs,
        out_specs=out_specs,
        check_vma=False,
    )
```

```python
import functools
import math

import jax
import jax.numpy as jnp
import numpy as np
from jax import lax
from jax.experimental import pallas as pl
from jax.experimental.pallas import tpu as pltpu
from jax.sharding import PartitionSpec as P

RADIX = 256
DIGITS = 3
LANES = 128
PLAN = 4
F32 = jnp.float32
BF16 = jnp.bfloat16


ANY = pl.BlockSpec(memory_space=pl.ANY)
VMEM = pl.BlockSpec(memory_space=pltpu.VMEM)
HBM = pl.BlockSpec(memory_space=pltpu.HBM)
SMEM = pl.BlockSpec(memory_space=pltpu.SMEM)


def ring_order(mesh):
    n = mesh.shape["limb"]
    line = np.moveaxis(mesh.devices, list(mesh.axis_names).index("limb"), 0).reshape(n, -1)[:, 0]
    at = [getattr(d, "coords", None) for d in line]
    if any(c is None for c in at):
        return list(range(n))
    near = [
        [j for j in range(n) if sum(abs(x - y) for x, y in zip(at[i], at[j])) == 1] for i in range(n)
    ]

    def walk(path):
        if len(path) == n:
            return path if 0 in near[path[-1]] else None
        for j in near[path[-1]]:
            if j not in path:
                found = walk(path + [j])
                if found:
                    return found
        return None

    return walk([0]) or list(range(n))


def split(x):
    hi = x.astype(BF16)
    return hi, (x - hi.astype(F32)).astype(BF16)


def mm(a, b):
    dot = functools.partial(jnp.dot, preferred_element_type=F32)
    return dot(a[0], b[0]) + dot(a[1], b[0]) + dot(a[0], b[1])


def spin(x, h):
    return mm(h, split(mm(split(x), h)))


def grid_of(ref, m, limbs):
    left = ref[pl.ds(m, RADIX, stride=2 * limbs), :]
    right = ref[pl.ds(limbs + m, RADIX, stride=2 * limbs), :]
    return jnp.concatenate([left, right], axis=1)


def in_hbm(x):
    return pltpu.with_memory_space_constraint(x, pltpu.HBM)


def params(mib):
    return pltpu.CompilerParams(vmem_limit_bytes=mib * 2**20)


def coef_kernel(start, limbs, tw, where, base_hi, base_lo, cipher, *refs):
    coef, mats, grid, bases, sem = refs[-5:]
    copies = [
        pltpu.make_async_copy(base_hi, bases.at[0], sem.at[0]),
        pltpu.make_async_copy(base_lo, bases.at[1], sem.at[1]),
        pltpu.make_async_copy(cipher, grid, sem.at[2]),
    ]
    for copy in copies:
        copy.start()
    row = lax.broadcasted_iota(jnp.int32, (RADIX, RADIX), 0)
    col = lax.broadcasted_iota(jnp.int32, (RADIX, RADIX), 1)
    first = where[1] == 0
    if start:
        mats[:start] = refs[0][...]
    for copy in copies:
        copy.wait()
    for i in range(coef.shape[0]):
        m = start + i
        g = tw[where[0] * limbs + m]
        pick = jnp.where(((row * g) & (RADIX - 1)) == col, 1.0, 0.0).astype(BF16)
        hi = jnp.dot(pick, bases[0], preferred_element_type=F32).astype(BF16)
        lo = jnp.dot(pick, bases[1], preferred_element_type=F32).astype(BF16)
        mats[m, 0] = hi
        mats[m, 1] = lo
        u = split(mm((hi, lo), split(grid_of(grid, m, limbs))))
        half = tuple(
            jnp.where(first, h[:, :LANES].astype(F32), h[:, LANES:].astype(F32)).astype(BF16) for h in (hi, lo)
        )
        coef[i] = mm(u, half)


def coef_call(start, stop, limbs, tw, where, base_hi, base_lo, cipher, before=()):
    return pl.pallas_call(
        functools.partial(coef_kernel, start, limbs),
        in_specs=[SMEM, SMEM, HBM, HBM, HBM] + [VMEM] * len(before),
        out_specs=[VMEM, VMEM],
        out_shape=[
            jax.ShapeDtypeStruct((stop - start, RADIX, LANES), F32),
            jax.ShapeDtypeStruct((stop, 2, RADIX, RADIX), BF16),
        ],
        scratch_shapes=[
            pltpu.VMEM(cipher.shape, F32),
            pltpu.VMEM((2, RADIX, RADIX), BF16),
            pltpu.SemaphoreType.DMA((3,)),
        ],
        compiler_params=params(12),
        cost_estimate=pl.CostEstimate(flops=10**9, bytes_accessed=2**20, transcendentals=0),
        name="coef",
    )(in_hbm(tw), where, in_hbm(base_hi), in_hbm(base_lo), in_hbm(cipher), *before)


def mix_kernel(limbs, lens, order, digit, where, srcs, conv, *refs):
    blocks, out, got, table, sem = refs[: len(lens)], refs[-4], refs[-3], refs[-2], refs[-1]
    size = got.shape[0] * limbs // (DIGITS + 1)
    copies = []
    for i, (start, stop) in enumerate(lens):
        c = pltpu.make_async_copy(blocks[i], got.at[srcs[i], pl.ds(start, stop - start)], sem.at[i])
        c.start()
        copies.append(c)
    first = where[0] * limbs
    for j in range(DIGITS * size):
        l = order[j]
        for m in range(limbs):
            same = digit[l] == digit[first + m]
            one = jnp.where(first + m == l, 1.0, 0.0)
            table[m, j] = jnp.where(same, one, conv[first + m, l])
    for c in copies:
        c.wait()
    step = 64

    def rows(r, carry):
        r0 = pl.multiple_of(r * step, step)
        for d in range(DIGITS):
            acc = [jnp.zeros((step, LANES), F32) for _ in range(limbs)]
            for j in range(size):
                l = order[d * size + j]
                x = got[l // limbs, l % limbs, pl.ds(r0, step), :]
                for m in range(limbs):
                    acc[m] = acc[m] + table[m, d * size + j] * x
            for m in range(limbs):
                out[d, m, pl.ds(r0, step), :] = acc[m]
        return carry

    lax.fori_loop(0, RADIX // step, rows, 0)


def mix_call(n, limbs, lens, order, digit, where, srcs, conv, blocks):
    vmem = pl.BlockSpec(memory_space=pltpu.VMEM)
    return pl.pallas_call(
        functools.partial(mix_kernel, limbs, lens),
        in_specs=[SMEM] * 5 + [HBM] * len(blocks),
        out_specs=vmem,
        out_shape=jax.ShapeDtypeStruct((DIGITS, limbs, RADIX, LANES), F32),
        scratch_shapes=[
            pltpu.VMEM((n, limbs, RADIX, LANES), F32),
            pltpu.SMEM((limbs, n * limbs), F32),
            pltpu.SemaphoreType.DMA((len(blocks),)),
        ],
        compiler_params=params(16),
        name="mix",
    )(order, in_hbm(digit), where, srcs, in_hbm(conv), *blocks)


def raise_kernel(pad, digit, where, own, other, mats, cipher, out, rows_in, sem):
    limbs = mats.shape[0]
    rows = cipher.shape[0]
    swapped = where[1] != 0
    fetch = pltpu.make_async_copy(cipher, rows_in, sem)
    fetch.start()

    def at(m, h):
        return pl.ds(h * limbs + m, RADIX, stride=2 * limbs)

    def convert(m, carry):
        h = (mats[m, 0], mats[m, 1])
        for d in range(DIGITS):
            a, b = own[d, m], other[d, m]
            x = jnp.concatenate([jnp.where(swapped, b, a), jnp.where(swapped, a, b)], axis=1)
            y = spin(x, h)
            for i in range(2):
                out[d, at(m, i), :] = y[:, i * LANES : (i + 1) * LANES]
        return carry

    lax.fori_loop(0, limbs, convert, 0)
    fetch.wait()

    def place(m, carry):
        d = digit[where[0] * limbs + m]
        for h in range(2):
            out[d, at(m, h), :] = rows_in[at(m, h), :]

        @pl.when(d != DIGITS)
        def _():
            for h in range(2):
                out[DIGITS, at(m, h), :] = jnp.zeros((RADIX, LANES), F32)

        return carry

    lax.fori_loop(0, limbs, place, 0)
    for d in range(DIGITS + 1):
        out[d, pl.ds(rows, pad), :] = out[d, pl.ds(0, pad), :]


def raise_call(digit, where, own, other, mats, cipher, pad):
    rows = cipher.shape[0]
    return pl.pallas_call(
        functools.partial(raise_kernel, pad),
        in_specs=[SMEM, SMEM] + [VMEM] * 3 + [HBM],
        out_specs=VMEM,
        out_shape=jax.ShapeDtypeStruct((DIGITS + 1, rows + pad, LANES), F32),
        scratch_shapes=[pltpu.VMEM(cipher.shape, F32), pltpu.SemaphoreType.DMA],
        compiler_params=params(16),
        name="raise",
    )(in_hbm(digit), where, own, other, mats, in_hbm(cipher))


def accum_kernel(k, limbs, pad, shifts, raised, keys, diag, gain, *refs):
    part, acc, kbuf, dbuf, small, sem, ksem = refs[-8:-6], *refs[-6:]
    rows = acc.shape[1]
    pieces = ksem.shape[0]
    block = rows // pieces

    def fetch(i):
        at = pl.ds(pl.multiple_of(i * block, block), block)
        return [
            pltpu.make_async_copy(keys.at[k, :, at], kbuf.at[:, at], ksem.at[i, 0]),
            pltpu.make_async_copy(diag.at[k, at], dbuf.at[at], ksem.at[i, 1]),
        ]

    amounts = pltpu.make_async_copy(shifts, small, sem)
    amounts.start()
    for i in range(pieces):
        for copy in fetch(i):
            copy.start()
    amounts.wait()
    s = small[0, k]
    tiles, lane = s // LANES, s % LANES
    here = lax.broadcasted_iota(jnp.int32, (pad, LANES), 1) < LANES - lane
    g8 = jnp.concatenate([gain[...]] * (pad // 8), axis=0)

    def piece(i, carry):
        for copy in fetch(i):
            copy.wait()

        def add(r, carry):
            at = pl.multiple_of(i * block + r * pad, pad)
            u0 = lax.rem(at - limbs * tiles + rows, rows)
            v0 = lax.rem(at - limbs * tiles - limbs + 2 * rows, rows)
            turned = []
            for g in range(DIGITS + 1):
                u = raised[g, pl.ds(pl.multiple_of(u0, limbs), pad), :]
                v = raised[g, pl.ds(pl.multiple_of(v0, limbs), pad), :]
                turned.append(pltpu.roll(jnp.where(here, u, v), lane, axis=1))
            w = dbuf[pl.ds(at, pad), :] * g8
            for c in range(2):
                a = turned[DIGITS]
                for d in range(DIGITS):
                    a = a + turned[d] * kbuf[2 * d + c, pl.ds(at, pad), :]
                acc[c, pl.ds(at, pad), :] = a
                w_a = w * a
                part[c][pl.ds(at, pad), :] = w_a if k == 0 else refs[c][pl.ds(at, pad), :] + w_a
            return carry

        return lax.fori_loop(0, block // pad, add, carry, unroll=2)

    lax.fori_loop(0, pieces, piece, 0)


def accum_call(k, shifts, raised, keys, diag, gain, limbs, pad, part):
    rows = raised.shape[1] - pad
    args = (in_hbm(shifts), raised, in_hbm(keys), in_hbm(diag), gain)
    specs = [HBM, VMEM, HBM, HBM, VMEM]
    alias = {}
    if part is not None:
        alias = {len(args) + i: i for i in range(2)}
        args += tuple(part)
        specs += [VMEM, VMEM]
    one = jax.ShapeDtypeStruct((rows, LANES), F32)
    return pl.pallas_call(
        functools.partial(accum_kernel, k, limbs, pad),
        in_specs=specs,
        out_specs=[VMEM, VMEM, VMEM],
        out_shape=[one, one, jax.ShapeDtypeStruct((2, rows, LANES), F32)],
        input_output_aliases=alias,
        scratch_shapes=[
            pltpu.VMEM(keys.shape[1:], F32),
            pltpu.VMEM((rows, LANES), F32),
            pltpu.SMEM(shifts.shape, jnp.int32),
            pltpu.SemaphoreType.DMA,
            pltpu.SemaphoreType.DMA((8, 2)),
        ],
        compiler_params=params(12),
        cost_estimate=pl.CostEstimate(flops=10**8, bytes_accessed=8 * 2**20, transcendentals=0),
        name="accum",
    )(*args)


def emit_kernel(k, limbs, specials, slot, acc, mats, *refs):
    store, stage, sem = refs[-4:-2], refs[-2], refs[-1]

    def emit(m, carry):
        @pl.when(slot[m] >= 0)
        def _():
            h = (mats[m, 0], mats[m, 1])
            copies = []
            for c in range(2):
                y = spin(grid_of(acc.at[c], m, limbs), h)
                stage[c, 0:RADIX, :] = y[:, :LANES]
                stage[c, RADIX:, :] = y[:, LANES:]
                copies.append(pltpu.make_async_copy(stage.at[c], store[c].at[k * specials + slot[m]], sem.at[c]))
                copies[-1].start()
            for copy in copies:
                copy.wait()

        return carry

    lax.fori_loop(0, limbs, emit, 0)


def emit_call(k, slot, acc, mats, specials, items, store):
    one = jax.ShapeDtypeStruct((items, 2 * RADIX, LANES), F32)
    args, specs, alias = (slot, acc, mats), [SMEM, VMEM, VMEM], {}
    if store is not None:
        alias = {len(args) + i: i for i in range(2)}
        args += tuple(map(in_hbm, store))
        specs += [HBM, HBM]
    return pl.pallas_call(
        functools.partial(emit_kernel, k, mats.shape[0], specials),
        in_specs=specs,
        out_specs=[HBM, HBM],
        out_shape=[one, one],
        input_output_aliases=alias,
        scratch_shapes=[pltpu.VMEM((2, 2 * RADIX, LANES), F32), pltpu.SemaphoreType.DMA((2,))],
        compiler_params=params(8),
        cost_estimate=pl.CostEstimate(flops=10**9, bytes_accessed=2**20, transcendentals=0),
        name="emit",
    )(*args)


def table_kernel(n, count, specials, limbs, least, order, pos, spot, plan, rounds, comp, a_ref, b_ref, end_ref):
    items = count * specials
    shape = (items, LANES)
    row_i = lax.broadcasted_iota(jnp.int32, shape, 0)
    row = row_i.astype(F32)
    lane = lax.broadcasted_iota(jnp.int32, shape, 1).astype(F32)
    kind, turn = lax.rem(row_i, specials), lax.div(row_i, specials)
    ready = jnp.maximum(2 * turn - 1, 0)
    weight = 3.0 * turn.astype(F32)
    p = spot[0]
    before, after = lax.rem(p + n - 1, n), lax.rem(p + 1, n)
    line = lax.broadcasted_iota(jnp.int32, (1, LANES), 1)
    org = jnp.zeros(shape, F32)
    for s in range(specials):
        owner = pos[lax.div(order[DIGITS * specials + s], limbs)]
        org = jnp.where(kind == s, owner.astype(F32), org)
    a_ref[...] = jnp.zeros(shape, F32)
    b_ref[...] = jnp.zeros(shape, F32)
    end_ref[...] = jnp.zeros(shape, F32)
    big = float(items * (2 * n + 3 * count))

    def choose(front, spread, t):
        open_ = jnp.logical_and(spread < n - 1, ready <= t)
        cand = jnp.logical_and(open_, front == lane)
        key = jnp.where(cand, (2.0 * spread + weight) * items + row, big)
        best = jnp.min(key, axis=0, keepdims=True)
        hit = jnp.where(jnp.logical_and(cand, key == best), 1.0, 0.0)
        item = jnp.sum(hit * (row - items), axis=0, keepdims=True) + items
        return item, jnp.sum(hit, axis=1, keepdims=True)

    def note(t, r, item, where):
        t = jnp.asarray(t, jnp.int32)
        mine = jnp.sum(jnp.where(line == where, item, 0.0), axis=1, keepdims=True)
        at = pl.ds(lax.div(PLAN * t + r, LANES), 1)
        here = line == lax.rem(PLAN * t + r, LANES)
        plan[at, :] = jnp.where(here, jnp.broadcast_to(mine, (1, LANES)).astype(jnp.int32), plan[at, :])

    none = jnp.full((1, LANES), float(items), F32)
    plan[...] = jnp.full(plan.shape, items, jnp.int32)
    note(0, 2, none, p)
    note(0, 3, none, p)

    def step(t, carry):
        a, b = a_ref[...], b_ref[...]
        front = org + a
        item, right = choose(jnp.where(front >= n, front - n, front), a + b, t)
        note(t, 0, item, p)
        note(t + 1, 2, item, before)
        a = a + right
        front = org - b
        item, left = choose(jnp.where(front < 0, front + n, front), a + b, t)
        note(t, 1, item, p)
        note(t + 1, 3, item, after)
        b = b + left
        a_ref[...] = a
        b_ref[...] = b
        end_ref[...] = jnp.where(right + left > 0, (t + 1).astype(F32), end_ref[...])
        return carry

    def missing():
        return jnp.sum(n - 1 - a_ref[...] - b_ref[...]).astype(jnp.int32)

    def more(c):
        step(c[0], 0)
        return c[0] + 1, missing()

    lax.fori_loop(0, least, step, 0)
    t, _ = lax.while_loop(lambda c: c[1] > 0, more, (jnp.int32(least), missing()))
    rounds[0] = t
    note(t, 0, none, p)
    note(t, 1, none, p)
    for k in range(count):
        comp[k] = jnp.max(end_ref[pl.ds(k * specials, specials), :]).astype(jnp.int32)


def table_call(n, count, specials, limbs, least, order, pos, spot):
    items = count * specials
    most = items * (n - 1) + 2 * count
    return pl.pallas_call(
        functools.partial(table_kernel, n, count, specials, limbs, least),
        in_specs=[SMEM] * 3,
        out_specs=[pl.BlockSpec(memory_space=pltpu.VMEM), SMEM, SMEM],
        out_shape=[
            jax.ShapeDtypeStruct((-(-PLAN * (most + 1) // (8 * LANES)) * 8, LANES), jnp.int32),
            jax.ShapeDtypeStruct((1,), jnp.int32),
            jax.ShapeDtypeStruct((count,), jnp.int32),
        ],
        scratch_shapes=[pltpu.VMEM((items, LANES), F32)] * 3,
        compiler_params=params(8),
        name="table",
    )(order, in_hbm(pos), spot)


def round_of(tile, t):
    got = [tile[lax.div(f, LANES), lax.rem(f, LANES)] for f in (jnp.asarray(PLAN * t + r, jnp.int32) for r in range(PLAN))]
    return got[:2], got[2:]


def pack_kernel(items, t, first, last, *refs):
    refs = list(refs)
    if t is None:
        t = refs.pop(0)[0]
    table, store = refs.pop(0), refs.pop(0)
    ins = () if first else (refs.pop(0), refs.pop(0))
    refs.pop(0)
    outs = () if last else (refs.pop(0), refs.pop(0))
    tile, keep, send, tsem = refs
    plan = pltpu.make_async_copy(table, tile, tsem)
    plan.start()
    plan.wait()
    go, came = round_of(tile, t)
    for i in range(len(ins)):
        @pl.when(came[i] < items)
        def _():
            pltpu.make_async_copy(ins[i], store.at[came[i]], keep.at[i]).start()

    old = []
    for j in range(len(outs)):
        fresh = [jnp.logical_and(go[j] == came[i], came[i] < items) for i in range(len(ins))]
        held = go[j] < items
        for f in fresh:
            held = jnp.logical_and(held, jnp.logical_not(f))
        old.append(held)

        @pl.when(held)
        def _():
            pltpu.make_async_copy(store.at[go[j]], outs[j], send.at[j]).start()

        for i in range(len(ins)):
            @pl.when(fresh[i])
            def _():
                outs[j][...] = ins[i][...]

    for i in range(len(ins)):
        @pl.when(came[i] < items)
        def _():
            pltpu.make_async_copy(ins[i], store.at[came[i]], keep.at[i]).wait()
    for j in range(len(outs)):
        @pl.when(old[j])
        def _():
            pltpu.make_async_copy(store.at[go[j]], outs[j], send.at[j]).wait()


def pack_call(table, t, store, ins=None, last=False):
    first = ins is None
    store = in_hbm(store)
    items = store.shape[0]
    item = jax.ShapeDtypeStruct(store.shape[1:], store.dtype)
    static = isinstance(t, int)
    args = (() if static else (t.reshape(1),)) + (table, store) + (() if first else tuple(ins))
    at = 1 if static else 2
    outs = [jax.ShapeDtypeStruct(store.shape, store.dtype)] + ([] if last else [item, item])
    size = math.prod(item.shape) * 4
    res = pl.pallas_call(
        functools.partial(pack_kernel, items, t if static else None, first, last),
        in_specs=([] if static else [SMEM]) + [ANY, HBM] + [VMEM] * (0 if first else 2),
        out_specs=[HBM] + [VMEM] * (len(outs) - 1),
        out_shape=outs,
        input_output_aliases={at: 0},
        scratch_shapes=[
            pltpu.SMEM(table.shape, jnp.int32),
            pltpu.SemaphoreType.DMA((2,)),
            pltpu.SemaphoreType.DMA((2,)),
            pltpu.SemaphoreType.DMA,
        ],
        compiler_params=params(2),
        cost_estimate=pl.CostEstimate(flops=0, bytes_accessed=8 * size, transcendentals=0),
        name="pack",
    )(*args)
    return res[0], list(res[1:])


def lower_kernel(low, high, guess, specials, limbs, *refs):
    tables, (diag, mats, *refs) = refs[:6], refs[6:]
    small, smem, refs = refs[-7:-1], refs[-1], refs[:-7]
    part, store, refs = refs[:2], refs[2:4], refs[4:]
    last = high is None
    scalars = [pltpu.make_async_copy(a, b, smem.at[i]) for i, (a, b) in enumerate(zip(tables, small))]
    order, digit, where, scale, conv, comp = small

    def fetch(k):
        return [
            pltpu.make_async_copy(store[c].at[pl.ds(k * specials, specials)], got.at[c], sem.at[c]) for c in range(2)
        ] + [pltpu.make_async_copy(diag.at[k], dg, sem.at[2])]

    if last:
        t, plan, *refs = refs
        ins, store, keep, send, refs = (refs[0:2], refs[2:4]), refs[4:6], refs[6:8], refs[8:10], refs[10:]
        total, got, dg, xs, sem, tile = refs
        total = [total.at[0], total.at[1]]
        copy = pltpu.make_async_copy(plan, tile, sem.at[7])
        copy.start()
    else:
        total, (got, dg, xs, sem) = refs[:2], refs[4:]
    scalars += [pltpu.make_async_copy(part[c], total[c], smem.at[len(small) + c]) for c in range(2)]
    for copy in fetch(guess) + scalars:
        copy.start()
    for copy in scalars + fetch(guess):
        copy.wait()
    count = diag.shape[0]
    first = where[0] * limbs

    if last:
        pltpu.make_async_copy(plan, tile, sem.at[7]).wait()
        _, came = round_of(tile, t[0])

        def arrive(act):
            for c in range(2):
                for i in range(2):
                    @pl.when(came[i] < store[c].shape[0])
                    def _():
                        act(pltpu.make_async_copy(ins[c][i], store[c].at[came[i]], sem.at[3 + 2 * c + i]))

        arrive(lambda copy: copy.start())
        for i in range(2):
            place = came[i] - guess * specials

            @pl.when(jnp.logical_and(place >= 0, place < specials))
            def _():
                for c in range(2):
                    got[c, place] = ins[c][i][...]

    def turn(i, carry):
        if last:
            @pl.when(i == 1)
            def _():
                arrive(lambda copy: copy.wait())

        k = lax.rem(guess + i, count)
        ripe = comp[k] > low
        if not last:
            ripe = jnp.logical_and(ripe, comp[k] <= high)

        @pl.when(ripe)
        def _():
            @pl.when(i > 0)
            def _():
                for copy in fetch(k):
                    copy.start()
                for copy in fetch(k):
                    copy.wait()

            def limb(m, carry):
                q = first + m

                @pl.when(digit[q] != DIGITS)
                def _():
                    h = (mats[m, 0], mats[m, 1])
                    w = [conv[q, order[DIGITS * specials + s]] for s in range(specials)]
                    size = scale[q]
                    step = 64
                    for c in range(2):
                        for i in range(2):
                            for r in range(0, RADIX, step):
                                x = w[0] * got[c, 0, pl.ds(i * RADIX + r, step), :]
                                for s in range(1, specials):
                                    x = x + w[s] * got[c, s, pl.ds(i * RADIX + r, step), :]
                                hi, lo = split(x)
                                xs[c, 0, pl.ds(r, step), pl.ds(i * LANES, LANES)] = hi
                                xs[c, 1, pl.ds(r, step), pl.ds(i * LANES, LANES)] = lo
                    for c in range(2):
                        y = mm(h, split(mm((xs[c, 0], xs[c, 1]), h)))
                        for i in range(2):
                            at = pl.ds(i * limbs + m, RADIX, stride=2 * limbs)
                            total[c][at, :] = total[c][at, :] - dg[at, :] * size * y[:, i * LANES : (i + 1) * LANES]

                return carry

            lax.fori_loop(0, limbs, limb, 0)

        return carry

    lax.fori_loop(0, count, turn, 0)
    if last:
        half = total[0].shape[0] // 2
        mine = where[1]
        for c in range(2):
            keep[c][...] = total[c][pl.ds(pl.multiple_of(mine * half, half), half), :]
            send[c][...] = total[c][pl.ds(pl.multiple_of((1 - mine) * half, half), half), :]


def lower_call(low, high, guess, order, digit, where, scale, conv, comp, diag, mats, specials, part, store, end=()):
    limbs = mats.shape[0]
    store = [in_hbm(s) for s in store]
    rows = part[0].shape[0]
    half = jax.ShapeDtypeStruct((rows // 2, LANES), F32)
    last = high is None
    part = part if last else [in_hbm(p) for p in part]
    shape = lambda a: jax.ShapeDtypeStruct(a.shape, a.dtype)
    scratch = [
        pltpu.VMEM((2, specials, 2 * RADIX, LANES), F32),
        pltpu.VMEM((rows, LANES), F32),
        pltpu.VMEM((2, 2, RADIX, RADIX), BF16),
        pltpu.SemaphoreType.DMA((8,)),
    ]
    if last:
        scratch = [pltpu.VMEM((2, rows, LANES), F32)] + scratch + [pltpu.SMEM(end[1].shape, jnp.int32)]
    tables = (order, in_hbm(digit), where, scale, in_hbm(conv), comp)
    scratch += [pltpu.SMEM(a.shape, a.dtype) for a in tables] + [pltpu.SemaphoreType.DMA((len(tables) + 2,))]
    return pl.pallas_call(
        functools.partial(lower_kernel, low, high, guess, specials, limbs),
        in_specs=[ANY] * 6 + [HBM, VMEM, ANY, ANY, HBM, HBM] + ([SMEM, ANY] + [VMEM] * 4 if last else []),
        out_specs=[HBM, HBM] + [VMEM] * 4 if last else [VMEM, VMEM, HBM, HBM],
        out_shape=[shape(s) for s in store] + [half] * 4 if last else [shape(p) for p in (*part, *store)],
        input_output_aliases={10: 0, 11: 1} if last else {10: 2, 11: 3},
        scratch_shapes=scratch,
        compiler_params=params(12),
        cost_estimate=pl.CostEstimate(flops=10**9, bytes_accessed=8 * 2**20, transcendentals=0),
        name="lower",
    )(*tables, in_hbm(diag), mats, *part, *store, *end)


def interleave(x):
    *lead, limbs, coeffs = x.shape
    x = x.reshape(*lead, limbs, coeffs // LANES, LANES)
    return jnp.swapaxes(x, -3, -2).reshape(*lead, coeffs // LANES * limbs, LANES)


def per_device(order_of, cipher, rotation_keys, diagonals, shifts, twiddles, moduli, digit_of, conversion):
    n = len(order_of)
    limbs = cipher.shape[0]
    ext = digit_of.shape[0]
    specials = ext // (DIGITS + 1)
    count = rotation_keys.shape[1]
    items = count * specials
    pos_of = np.argsort(np.array(order_of)).astype(np.int32)
    cw = [(order_of[i], order_of[(i + 1) % n]) for i in range(n)]
    ccw = [(b, a) for a, b in cw]
    me, rot = lax.axis_index("limb"), lax.axis_index("rot")
    where = jnp.stack([me, rot]).astype(jnp.int32)
    pos = jnp.asarray(pos_of)
    my_pos = pos[me]
    swap = lambda x: lax.ppermute(x, "rot", [(0, 1), (1, 0)])

    grid = np.arange(RADIX)
    angle = (grid[:, None] * grid[None, :] % RADIX) * (2.0 * math.pi / RADIX)
    base = ((np.cos(angle) + np.sin(angle)) / math.sqrt(RADIX)).astype(np.float32)
    base_hi = base.astype(BF16)
    base_lo = (base - base_hi.astype(np.float32)).astype(BF16)

    rows_c = interleave(cipher)
    keys = interleave(rotation_keys).reshape(count, DIGITS * 2, -1, LANES)
    diag = interleave(diagonals).reshape(count, -1, LANES)

    cut = limbs // 2
    given = (limbs, twiddles, where, jnp.asarray(base_hi), jnp.asarray(base_lo), rows_c)
    coef, mats = [None, None], None
    coef[0], mats = coef_call(0, cut, *given)
    coef[1], mats = coef_call(cut, limbs, *given, (mats,))

    ids = jnp.arange(ext, dtype=jnp.int32)
    before = (digit_of[None, :] < digit_of[:, None]) | (
        (digit_of[None, :] == digit_of[:, None]) & (ids[None, :] < ids[:, None])
    )
    place = jnp.sum(before.astype(jnp.int32), axis=1)
    order = jnp.sum(jnp.where(place[None, :] == ids[:, None], ids[None, :], 0), axis=1)
    slot = lax.dynamic_slice_in_dim(jnp.maximum(place - DIGITS * specials, -1), me * limbs, limbs, 0)
    special = digit_of == DIGITS
    mod = moduli.astype(F32)
    scale = jnp.sum(jnp.where(special[None, :], mod[:, None] / mod[None, :], 0.0), axis=1) / specials
    my_special = lax.dynamic_slice_in_dim(special, me * limbs, limbs, 0)
    my_gain = jnp.where(my_special, 1.0, lax.dynamic_slice_in_dim(scale, me * limbs, limbs, 0))
    rows8 = lambda v: jnp.broadcast_to(jnp.tile(v, 8 // limbs)[:, None], (8, LANES))
    gain = rows8(my_gain)
    fixed = items * n // (2 * n)
    plan, rounds, comp = table_call(n, count, specials, limbs, fixed, order, pos, my_pos.reshape(1))

    spans = [(0, cut), (cut, limbs)]
    blocks, lens, steps = list(coef), list(spans), [0, 0]
    right, left = list(coef), list(coef)
    hop = lambda x, ring: lax.ppermute(x, "limb", ring)
    both = (n - 1) // 2
    for r in range(1, both + 1):
        for i in range(2):
            right[i] = hop(right[i], cw)
            left[i] = hop(left[i], ccw)
        blocks += right + left
        lens += spans * 2
        steps += [-r, -r, r, r]
        if r == 2:
            right[1], left[1], order, slot, gain, scale, plan, rounds, comp = lax.optimization_barrier(
                (right[1], left[1], order, slot, gain, scale, plan, rounds, comp)
            )
    if n % 2 == 0:
        blocks += [hop(right[0], cw), hop(left[1], ccw)]
        lens += spans
        steps += [n // 2, n // 2]
    srcs = jnp.asarray(
        np.array([[order_of[(pos_of[d] + s) % n] for s in steps] for d in range(n)], np.int32)
    )[me]

    pad = 64
    mixed = mix_call(n, limbs, tuple(lens), order, digit_of, where, srcs, conversion, blocks)
    raised = raise_call(digit_of, where, mixed, swap(mixed), mats, rows_c, pad)

    def accumulate(k, after=None):
        return accum_call(k, tie(shifts, after), raised, keys, diag, gain, limbs, pad, part)

    def lower(low, high, guess, end=()):
        return lower_call(
            low, high, guess, order, digit_of, where, scale, conversion, comp, diag, mats, specials, part, stores, end
        )

    def tie(x, after):
        return x if after is None else lax.optimization_barrier((x, after))[0]

    def travel(sends):
        return [lax.ppermute(sends[0], "limb", cw), lax.ppermute(sends[1], "limb", ccw)]

    tasks = {max(2 * k - 3, 0): k for k in range(1, count)}, {max(2 * k - 2, 0): k for k in range(1, count)}
    gates = {fixed - 5: 0, fixed - 3: 1, fixed - 1: 2}
    part, stores, ins, low = None, None, [None, None], -1
    *part, acc = accumulate(0)
    stores = list(emit_call(0, slot, acc, mats, specials, items, stores))
    for t in range(fixed):
        for c in range(2):
            stores[c], sends = pack_call(plan, t, stores[c], ins[c])
            ins[c] = travel(sends)
        if t in tasks[0]:
            *part, acc = accumulate(tasks[0][t], sends[0])
            stores[0], acc = lax.optimization_barrier((stores[0], acc))
        if t in tasks[1]:
            stores = list(emit_call(tasks[1][t], slot, tie(acc, sends[0]), mats, specials, items, stores))
        if t in gates:
            *part, stores[0], stores[1] = lower(low, t, min(gates[t], count - 1))
            low = t

    def more(state):
        return state[0] < rounds[0]

    def one(state):
        t, stores, ins = state
        stores, ins = list(stores), list(ins)
        for c in range(2):
            stores[c], sends = pack_call(plan, t, stores[c], ins[c])
            ins[c] = travel(sends)
        return t + 1, stores, ins

    t, stores, ins = lax.while_loop(more, one, (jnp.int32(fixed), stores, ins))
    _, _, *halves = lower(low, None, count - 1, (t.reshape(1), plan, *ins[0], *ins[1]))
    total = jnp.stack([keep + swap(send) for keep, send in zip(halves[:2], halves[2:])])
    total = jnp.swapaxes(total.reshape(2, -1, limbs, LANES), 1, 2)
    return total.reshape(2, limbs, -1)


def solution(mesh):
    in_specs = (
        P(("parts", "limb"), None),
        P("rot", None, None, None, "limb", None),
        P("rot", None, "limb", None),
        P("rot", None),
        P(),
        P(),
        P(),
        P(),
    )
    out_specs = P(None, ("parts", "limb"), "rot")

    def step(*args):
        return per_device(ring_order(mesh), *args)

    return jax.shard_map(step, mesh=mesh, in_specs=in_specs, out_specs=out_specs, check_vma=False)
```

```python
import functools
import math

import jax
import jax.numpy as jnp
import numpy as np
from jax import lax
from jax.experimental import pallas as pl
from jax.experimental.pallas import tpu as pltpu
from jax.sharding import PartitionSpec as P

RADIX = 256
DIGITS = 3
LANES = 128
PLAN = 4
F32 = jnp.float32
BF16 = jnp.bfloat16


ANY = pl.BlockSpec(memory_space=pl.ANY)
VMEM = pl.BlockSpec(memory_space=pltpu.VMEM)
HBM = pl.BlockSpec(memory_space=pltpu.HBM)
SMEM = pl.BlockSpec(memory_space=pltpu.SMEM)


def ring_order(mesh):
    n = mesh.shape["limb"]
    line = np.moveaxis(mesh.devices, list(mesh.axis_names).index("limb"), 0).reshape(n, -1)[:, 0]
    at = [getattr(d, "coords", None) for d in line]
    if any(c is None for c in at):
        return list(range(n))
    near = [
        [j for j in range(n) if sum(abs(x - y) for x, y in zip(at[i], at[j])) == 1] for i in range(n)
    ]

    def walk(path):
        if len(path) == n:
            return path if 0 in near[path[-1]] else None
        for j in near[path[-1]]:
            if j not in path:
                found = walk(path + [j])
                if found:
                    return found
        return None

    return walk([0]) or list(range(n))


def split(x):
    hi = x.astype(BF16)
    return hi, (x - hi.astype(F32)).astype(BF16)


def mm(a, b):
    dot = functools.partial(jnp.dot, preferred_element_type=F32)
    return dot(a[0], b[0]) + dot(a[1], b[0]) + dot(a[0], b[1])


def spin(x, h):
    return mm(h, split(mm(split(x), h)))


def grid_of(ref, m, limbs):
    left = ref[pl.ds(m, RADIX, stride=2 * limbs), :]
    right = ref[pl.ds(limbs + m, RADIX, stride=2 * limbs), :]
    return jnp.concatenate([left, right], axis=1)


def in_hbm(x):
    return pltpu.with_memory_space_constraint(x, pltpu.HBM)


def params(mib):
    return pltpu.CompilerParams(vmem_limit_bytes=mib * 2**20)


def coef_kernel(start, limbs, tw, where, base_hi, base_lo, cipher, *refs):
    coef, mats, grid, bases, sem = refs[-5:]
    copies = [
        pltpu.make_async_copy(base_hi, bases.at[0], sem.at[0]),
        pltpu.make_async_copy(base_lo, bases.at[1], sem.at[1]),
        pltpu.make_async_copy(cipher, grid, sem.at[2]),
    ]
    for copy in copies:
        copy.start()
    row = lax.broadcasted_iota(jnp.int32, (RADIX, RADIX), 0)
    col = lax.broadcasted_iota(jnp.int32, (RADIX, RADIX), 1)
    first = where[1] == 0
    if start:
        mats[:start] = refs[0][...]
    for copy in copies:
        copy.wait()
    for i in range(coef.shape[0]):
        m = start + i
        g = tw[where[0] * limbs + m]
        pick = jnp.where(((row * g) & (RADIX - 1)) == col, 1.0, 0.0).astype(BF16)
        hi = jnp.dot(pick, bases[0], preferred_element_type=F32).astype(BF16)
        lo = jnp.dot(pick, bases[1], preferred_element_type=F32).astype(BF16)
        mats[m, 0] = hi
        mats[m, 1] = lo
        u = split(mm((hi, lo), split(grid_of(grid, m, limbs))))
        half = tuple(
            jnp.where(first, h[:, :LANES].astype(F32), h[:, LANES:].astype(F32)).astype(BF16) for h in (hi, lo)
        )
        coef[i] = mm(u, half)


def coef_call(start, stop, limbs, tw, where, base_hi, base_lo, cipher, before=()):
    return pl.pallas_call(
        functools.partial(coef_kernel, start, limbs),
        in_specs=[SMEM, SMEM, HBM, HBM, HBM] + [VMEM] * len(before),
        out_specs=[VMEM, VMEM],
        out_shape=[
            jax.ShapeDtypeStruct((stop - start, RADIX, LANES), F32),
            jax.ShapeDtypeStruct((stop, 2, RADIX, RADIX), BF16),
        ],
        scratch_shapes=[
            pltpu.VMEM(cipher.shape, F32),
            pltpu.VMEM((2, RADIX, RADIX), BF16),
            pltpu.SemaphoreType.DMA((3,)),
        ],
        compiler_params=params(12),
        cost_estimate=pl.CostEstimate(flops=10**9, bytes_accessed=2**20, transcendentals=0),
        name="coef",
    )(in_hbm(tw), where, in_hbm(base_hi), in_hbm(base_lo), in_hbm(cipher), *before)


def mix_kernel(limbs, lens, order, digit, where, srcs, conv, *refs):
    blocks, out, got, table, sem = refs[: len(lens)], refs[-4], refs[-3], refs[-2], refs[-1]
    size = got.shape[0] * limbs // (DIGITS + 1)
    copies = []
    for i, (start, stop) in enumerate(lens):
        c = pltpu.make_async_copy(blocks[i], got.at[srcs[i], pl.ds(start, stop - start)], sem.at[i])
        c.start()
        copies.append(c)
    first = where[0] * limbs
    for j in range(DIGITS * size):
        l = order[j]
        for m in range(limbs):
            same = digit[l] == digit[first + m]
            one = jnp.where(first + m == l, 1.0, 0.0)
            table[m, j] = jnp.where(same, one, conv[first + m, l])
    for c in copies:
        c.wait()
    step = 64

    def rows(r, carry):
        r0 = pl.multiple_of(r * step, step)
        for d in range(DIGITS):
            acc = [jnp.zeros((step, LANES), F32) for _ in range(limbs)]
            for j in range(size):
                l = order[d * size + j]
                x = got[l // limbs, l % limbs, pl.ds(r0, step), :]
                for m in range(limbs):
                    acc[m] = acc[m] + table[m, d * size + j] * x
            for m in range(limbs):
                out[d, m, pl.ds(r0, step), :] = acc[m]
        return carry

    lax.fori_loop(0, RADIX // step, rows, 0)


def mix_call(n, limbs, lens, order, digit, where, srcs, conv, blocks):
    vmem = pl.BlockSpec(memory_space=pltpu.VMEM)
    return pl.pallas_call(
        functools.partial(mix_kernel, limbs, lens),
        in_specs=[SMEM] * 5 + [HBM] * len(blocks),
        out_specs=vmem,
        out_shape=jax.ShapeDtypeStruct((DIGITS, limbs, RADIX, LANES), F32),
        scratch_shapes=[
            pltpu.VMEM((n, limbs, RADIX, LANES), F32),
            pltpu.SMEM((limbs, n * limbs), F32),
            pltpu.SemaphoreType.DMA((len(blocks),)),
        ],
        compiler_params=params(16),
        name="mix",
    )(order, in_hbm(digit), where, srcs, in_hbm(conv), *blocks)


def raise_kernel(pad, digit, where, own, other, mats, cipher, out, rows_in, sem):
    limbs = mats.shape[0]
    rows = cipher.shape[0]
    swapped = where[1] != 0
    fetch = pltpu.make_async_copy(cipher, rows_in, sem)
    fetch.start()

    def at(m, h):
        return pl.ds(h * limbs + m, RADIX, stride=2 * limbs)

    def convert(m, carry):
        h = (mats[m, 0], mats[m, 1])
        for d in range(DIGITS):
            a, b = own[d, m], other[d, m]
            x = jnp.concatenate([jnp.where(swapped, b, a), jnp.where(swapped, a, b)], axis=1)
            y = spin(x, h)
            for i in range(2):
                out[d, at(m, i), :] = y[:, i * LANES : (i + 1) * LANES]
        return carry

    lax.fori_loop(0, limbs, convert, 0)
    fetch.wait()

    def place(m, carry):
        d = digit[where[0] * limbs + m]
        for h in range(2):
            out[d, at(m, h), :] = rows_in[at(m, h), :]

        @pl.when(d != DIGITS)
        def _():
            for h in range(2):
                out[DIGITS, at(m, h), :] = jnp.zeros((RADIX, LANES), F32)

        return carry

    lax.fori_loop(0, limbs, place, 0)
    for d in range(DIGITS + 1):
        out[d, pl.ds(rows, pad), :] = out[d, pl.ds(0, pad), :]


def raise_call(digit, where, own, other, mats, cipher, pad):
    rows = cipher.shape[0]
    return pl.pallas_call(
        functools.partial(raise_kernel, pad),
        in_specs=[SMEM, SMEM] + [VMEM] * 3 + [HBM],
        out_specs=VMEM,
        out_shape=jax.ShapeDtypeStruct((DIGITS + 1, rows + pad, LANES), F32),
        scratch_shapes=[pltpu.VMEM(cipher.shape, F32), pltpu.SemaphoreType.DMA],
        compiler_params=params(16),
        name="raise",
    )(in_hbm(digit), where, own, other, mats, in_hbm(cipher))


def accum_kernel(k, limbs, pad, shifts, raised, keys, diag, gain, *refs):
    part, acc, kbuf, dbuf, small, sem, ksem = refs[-8:-6], *refs[-6:]
    rows = acc.shape[1]
    pieces = ksem.shape[0]
    block = rows // pieces

    def fetch(i):
        at = pl.ds(pl.multiple_of(i * block, block), block)
        return [
            pltpu.make_async_copy(keys.at[k, :, at], kbuf.at[:, at], ksem.at[i, 0]),
            pltpu.make_async_copy(diag.at[k, at], dbuf.at[at], ksem.at[i, 1]),
        ]

    amounts = pltpu.make_async_copy(shifts, small, sem)
    amounts.start()
    for i in range(pieces):
        for copy in fetch(i):
            copy.start()
    amounts.wait()
    s = small[0, k]
    tiles, lane = s // LANES, s % LANES
    here = lax.broadcasted_iota(jnp.int32, (pad, LANES), 1) < LANES - lane
    g8 = jnp.concatenate([gain[...]] * (pad // 8), axis=0)

    def piece(i, carry):
        for copy in fetch(i):
            copy.wait()

        def add(r, carry):
            at = pl.multiple_of(i * block + r * pad, pad)
            u0 = lax.rem(at - limbs * tiles + rows, rows)
            v0 = lax.rem(at - limbs * tiles - limbs + 2 * rows, rows)
            turned = []
            for g in range(DIGITS + 1):
                u = raised[g, pl.ds(pl.multiple_of(u0, limbs), pad), :]
                v = raised[g, pl.ds(pl.multiple_of(v0, limbs), pad), :]
                turned.append(pltpu.roll(jnp.where(here, u, v), lane, axis=1))
            w = dbuf[pl.ds(at, pad), :] * g8
            for c in range(2):
                a = turned[DIGITS]
                for d in range(DIGITS):
                    a = a + turned[d] * kbuf[2 * d + c, pl.ds(at, pad), :]
                acc[c, pl.ds(at, pad), :] = a
                w_a = w * a
                part[c][pl.ds(at, pad), :] = w_a if k == 0 else refs[c][pl.ds(at, pad), :] + w_a
            return carry

        return lax.fori_loop(0, block // pad, add, carry, unroll=2)

    lax.fori_loop(0, pieces, piece, 0)


def accum_call(k, shifts, raised, keys, diag, gain, limbs, pad, part):
    rows = raised.shape[1] - pad
    args = (in_hbm(shifts), raised, in_hbm(keys), in_hbm(diag), gain)
    specs = [HBM, VMEM, HBM, HBM, VMEM]
    alias = {}
    if part is not None:
        alias = {len(args) + i: i for i in range(2)}
        args += tuple(part)
        specs += [VMEM, VMEM]
    one = jax.ShapeDtypeStruct((rows, LANES), F32)
    return pl.pallas_call(
        functools.partial(accum_kernel, k, limbs, pad),
        in_specs=specs,
        out_specs=[VMEM, VMEM, VMEM],
        out_shape=[one, one, jax.ShapeDtypeStruct((2, rows, LANES), F32)],
        input_output_aliases=alias,
        scratch_shapes=[
            pltpu.VMEM(keys.shape[1:], F32),
            pltpu.VMEM((rows, LANES), F32),
            pltpu.SMEM(shifts.shape, jnp.int32),
            pltpu.SemaphoreType.DMA,
            pltpu.SemaphoreType.DMA((8, 2)),
        ],
        compiler_params=params(12),
        cost_estimate=pl.CostEstimate(flops=10**8, bytes_accessed=8 * 2**20, transcendentals=0),
        name="accum",
    )(*args)


def emit_kernel(k, limbs, specials, slot, acc, mats, *refs):
    store, stage, sem = refs[-4:-2], refs[-2], refs[-1]

    def emit(m, carry):
        @pl.when(slot[m] >= 0)
        def _():
            h = (mats[m, 0], mats[m, 1])
            copies = []
            for c in range(2):
                y = spin(grid_of(acc.at[c], m, limbs), h)
                stage[c, 0:RADIX, :] = y[:, :LANES]
                stage[c, RADIX:, :] = y[:, LANES:]
                copies.append(pltpu.make_async_copy(stage.at[c], store[c].at[k * specials + slot[m]], sem.at[c]))
                copies[-1].start()
            for copy in copies:
                copy.wait()

        return carry

    lax.fori_loop(0, limbs, emit, 0)


def emit_call(k, slot, acc, mats, specials, items, store):
    one = jax.ShapeDtypeStruct((items, 2 * RADIX, LANES), F32)
    args, specs, alias = (slot, acc, mats), [SMEM, VMEM, VMEM], {}
    if store is not None:
        alias = {len(args) + i: i for i in range(2)}
        args += tuple(map(in_hbm, store))
        specs += [HBM, HBM]
    return pl.pallas_call(
        functools.partial(emit_kernel, k, mats.shape[0], specials),
        in_specs=specs,
        out_specs=[HBM, HBM],
        out_shape=[one, one],
        input_output_aliases=alias,
        scratch_shapes=[pltpu.VMEM((2, 2 * RADIX, LANES), F32), pltpu.SemaphoreType.DMA((2,))],
        compiler_params=params(8),
        cost_estimate=pl.CostEstimate(flops=10**9, bytes_accessed=2**20, transcendentals=0),
        name="emit",
    )(*args)


def table_kernel(n, count, specials, limbs, least, order, pos, spot, plan, rounds, comp, a_ref, b_ref, end_ref):
    items = count * specials
    shape = (items, LANES)
    row_i = lax.broadcasted_iota(jnp.int32, shape, 0)
    row = row_i.astype(F32)
    lane = lax.broadcasted_iota(jnp.int32, shape, 1).astype(F32)
    kind, turn = lax.rem(row_i, specials), lax.div(row_i, specials)
    ready = jnp.maximum(2 * turn - 1, 0)
    weight = 3.0 * turn.astype(F32)
    p = spot[0]
    before, after = lax.rem(p + n - 1, n), lax.rem(p + 1, n)
    line = lax.broadcasted_iota(jnp.int32, (1, LANES), 1)
    org = jnp.zeros(shape, F32)
    for s in range(specials):
        owner = pos[lax.div(order[DIGITS * specials + s], limbs)]
        org = jnp.where(kind == s, owner.astype(F32), org)
    a_ref[...] = jnp.zeros(shape, F32)
    b_ref[...] = jnp.zeros(shape, F32)
    end_ref[...] = jnp.zeros(shape, F32)
    big = float(items * (2 * n + 3 * count))

    def choose(front, spread, t):
        open_ = jnp.logical_and(spread < n - 1, ready <= t)
        cand = jnp.logical_and(open_, front == lane)
        key = jnp.where(cand, (2.0 * spread + weight) * items + row, big)
        best = jnp.min(key, axis=0, keepdims=True)
        hit = jnp.where(jnp.logical_and(cand, key == best), 1.0, 0.0)
        item = jnp.sum(hit * (row - items), axis=0, keepdims=True) + items
        return item, jnp.sum(hit, axis=1, keepdims=True)

    def note(t, r, item, where):
        t = jnp.asarray(t, jnp.int32)
        mine = jnp.sum(jnp.where(line == where, item, 0.0), axis=1, keepdims=True)
        at = pl.ds(lax.div(PLAN * t + r, LANES), 1)
        here = line == lax.rem(PLAN * t + r, LANES)
        plan[at, :] = jnp.where(here, jnp.broadcast_to(mine, (1, LANES)).astype(jnp.int32), plan[at, :])

    none = jnp.full((1, LANES), float(items), F32)
    plan[...] = jnp.full(plan.shape, items, jnp.int32)
    note(0, 2, none, p)
    note(0, 3, none, p)

    def step(t, carry):
        a, b = a_ref[...], b_ref[...]
        front = org + a
        item, right = choose(jnp.where(front >= n, front - n, front), a + b, t)
        note(t, 0, item, p)
        note(t + 1, 2, item, before)
        a = a + right
        front = org - b
        item, left = choose(jnp.where(front < 0, front + n, front), a + b, t)
        note(t, 1, item, p)
        note(t + 1, 3, item, after)
        b = b + left
        a_ref[...] = a
        b_ref[...] = b
        end_ref[...] = jnp.where(right + left > 0, (t + 1).astype(F32), end_ref[...])
        return carry

    def missing():
        return jnp.sum(n - 1 - a_ref[...] - b_ref[...]).astype(jnp.int32)

    def more(c):
        step(c[0], 0)
        return c[0] + 1, missing()

    lax.fori_loop(0, least, step, 0)
    t, _ = lax.while_loop(lambda c: c[1] > 0, more, (jnp.int32(least), missing()))
    rounds[0] = t
    note(t, 0, none, p)
    note(t, 1, none, p)
    for k in range(count):
        comp[k] = jnp.max(end_ref[pl.ds(k * specials, specials), :]).astype(jnp.int32)


def table_call(n, count, specials, limbs, least, order, pos, spot):
    items = count * specials
    most = items * (n - 1) + 2 * count
    return pl.pallas_call(
        functools.partial(table_kernel, n, count, specials, limbs, least),
        in_specs=[SMEM] * 3,
        out_specs=[pl.BlockSpec(memory_space=pltpu.VMEM), SMEM, SMEM],
        out_shape=[
            jax.ShapeDtypeStruct((-(-PLAN * (most + 1) // (8 * LANES)) * 8, LANES), jnp.int32),
            jax.ShapeDtypeStruct((1,), jnp.int32),
            jax.ShapeDtypeStruct((count,), jnp.int32),
        ],
        scratch_shapes=[pltpu.VMEM((items, LANES), F32)] * 3,
        compiler_params=params(8),
        name="table",
    )(order, in_hbm(pos), spot)


def round_of(tile, t):
    got = [tile[lax.div(f, LANES), lax.rem(f, LANES)] for f in (jnp.asarray(PLAN * t + r, jnp.int32) for r in range(PLAN))]
    return got[:2], got[2:]


def pack_kernel(items, t, first, last, *refs):
    refs = list(refs)
    if t is None:
        t = refs.pop(0)[0]
    table, store = refs.pop(0), refs.pop(0)
    ins = () if first else (refs.pop(0), refs.pop(0))
    refs.pop(0)
    outs = () if last else (refs.pop(0), refs.pop(0))
    tile, keep, send, tsem = refs
    plan = pltpu.make_async_copy(table, tile, tsem)
    plan.start()
    plan.wait()
    go, came = round_of(tile, t)
    for i in range(len(ins)):
        @pl.when(came[i] < items)
        def _():
            pltpu.make_async_copy(ins[i], store.at[came[i]], keep.at[i]).start()

    old = []
    for j in range(len(outs)):
        fresh = [jnp.logical_and(go[j] == came[i], came[i] < items) for i in range(len(ins))]
        held = go[j] < items
        for f in fresh:
            held = jnp.logical_and(held, jnp.logical_not(f))
        old.append(held)

        @pl.when(held)
        def _():
            pltpu.make_async_copy(store.at[go[j]], outs[j], send.at[j]).start()

        for i in range(len(ins)):
            @pl.when(fresh[i])
            def _():
                outs[j][...] = ins[i][...]

    for i in range(len(ins)):
        @pl.when(came[i] < items)
        def _():
            pltpu.make_async_copy(ins[i], store.at[came[i]], keep.at[i]).wait()
    for j in range(len(outs)):
        @pl.when(old[j])
        def _():
            pltpu.make_async_copy(store.at[go[j]], outs[j], send.at[j]).wait()


def pack_call(table, t, store, ins=None, last=False):
    first = ins is None
    store = in_hbm(store)
    items = store.shape[0]
    item = jax.ShapeDtypeStruct(store.shape[1:], store.dtype)
    static = isinstance(t, int)
    args = (() if static else (t.reshape(1),)) + (table, store) + (() if first else tuple(ins))
    at = 1 if static else 2
    outs = [jax.ShapeDtypeStruct(store.shape, store.dtype)] + ([] if last else [item, item])
    size = math.prod(item.shape) * 4
    res = pl.pallas_call(
        functools.partial(pack_kernel, items, t if static else None, first, last),
        in_specs=([] if static else [SMEM]) + [ANY, HBM] + [VMEM] * (0 if first else 2),
        out_specs=[HBM] + [VMEM] * (len(outs) - 1),
        out_shape=outs,
        input_output_aliases={at: 0},
        scratch_shapes=[
            pltpu.SMEM(table.shape, jnp.int32),
            pltpu.SemaphoreType.DMA((2,)),
            pltpu.SemaphoreType.DMA((2,)),
            pltpu.SemaphoreType.DMA,
        ],
        compiler_params=params(2),
        cost_estimate=pl.CostEstimate(flops=0, bytes_accessed=8 * size, transcendentals=0),
        name="pack",
    )(*args)
    return res[0], list(res[1:])


def lower_kernel(low, high, guess, specials, limbs, *refs):
    tables, (diag, mats, *refs) = refs[:6], refs[6:]
    small, smem, refs = refs[-7:-1], refs[-1], refs[:-7]
    part, store, refs = refs[:2], refs[2:4], refs[4:]
    last = high is None
    scalars = [pltpu.make_async_copy(a, b, smem.at[i]) for i, (a, b) in enumerate(zip(tables, small))]
    order, digit, where, scale, conv, comp = small

    def fetch(k):
        return [
            pltpu.make_async_copy(store[c].at[pl.ds(k * specials, specials)], got.at[c], sem.at[c]) for c in range(2)
        ] + [pltpu.make_async_copy(diag.at[k], dg, sem.at[2])]

    if last:
        t, plan, *refs = refs
        ins, store, keep, send, refs = (refs[0:2], refs[2:4]), refs[4:6], refs[6:8], refs[8:10], refs[10:]
        total, got, dg, xs, sem, tile = refs
        total = [total.at[0], total.at[1]]
        copy = pltpu.make_async_copy(plan, tile, sem.at[7])
        copy.start()
    else:
        total, (got, dg, xs, sem) = refs[:2], refs[4:]
    scalars += [pltpu.make_async_copy(part[c], total[c], smem.at[len(small) + c]) for c in range(2)]
    for copy in fetch(guess) + scalars:
        copy.start()
    for copy in scalars + fetch(guess):
        copy.wait()
    count = diag.shape[0]
    first = where[0] * limbs

    if last:
        pltpu.make_async_copy(plan, tile, sem.at[7]).wait()
        _, came = round_of(tile, t[0])

        def arrive(act):
            for c in range(2):
                for i in range(2):
                    @pl.when(came[i] < store[c].shape[0])
                    def _():
                        act(pltpu.make_async_copy(ins[c][i], store[c].at[came[i]], sem.at[3 + 2 * c + i]))

        arrive(lambda copy: copy.start())
        for i in range(2):
            place = came[i] - guess * specials

            @pl.when(jnp.logical_and(place >= 0, place < specials))
            def _():
                for c in range(2):
                    got[c, place] = ins[c][i][...]

    def turn(i, carry):
        if last:
            @pl.when(i == 1)
            def _():
                arrive(lambda copy: copy.wait())

        k = lax.rem(guess + i, count)
        ripe = comp[k] > low
        if not last:
            ripe = jnp.logical_and(ripe, comp[k] <= high)

        @pl.when(ripe)
        def _():
            @pl.when(i > 0)
            def _():
                for copy in fetch(k):
                    copy.start()
                for copy in fetch(k):
                    copy.wait()

            def limb(m, carry):
                q = first + m

                @pl.when(digit[q] != DIGITS)
                def _():
                    h = (mats[m, 0], mats[m, 1])
                    w = [conv[q, order[DIGITS * specials + s]] for s in range(specials)]
                    size = scale[q]
                    step = 64
                    for c in range(2):
                        for i in range(2):
                            for r in range(0, RADIX, step):
                                x = w[0] * got[c, 0, pl.ds(i * RADIX + r, step), :]
                                for s in range(1, specials):
                                    x = x + w[s] * got[c, s, pl.ds(i * RADIX + r, step), :]
                                hi, lo = split(x)
                                xs[c, 0, pl.ds(r, step), pl.ds(i * LANES, LANES)] = hi
                                xs[c, 1, pl.ds(r, step), pl.ds(i * LANES, LANES)] = lo
                    for c in range(2):
                        y = mm(h, split(mm((xs[c, 0], xs[c, 1]), h)))
                        for i in range(2):
                            at = pl.ds(i * limbs + m, RADIX, stride=2 * limbs)
                            total[c][at, :] = total[c][at, :] - dg[at, :] * size * y[:, i * LANES : (i + 1) * LANES]

                return carry

            lax.fori_loop(0, limbs, limb, 0)

        return carry

    lax.fori_loop(0, count, turn, 0)
    if last:
        half = total[0].shape[0] // 2
        mine = where[1]
        for c in range(2):
            keep[c][...] = total[c][pl.ds(pl.multiple_of(mine * half, half), half), :]
            send[c][...] = total[c][pl.ds(pl.multiple_of((1 - mine) * half, half), half), :]


def lower_call(low, high, guess, order, digit, where, scale, conv, comp, diag, mats, specials, part, store, end=()):
    limbs = mats.shape[0]
    store = [in_hbm(s) for s in store]
    rows = part[0].shape[0]
    half = jax.ShapeDtypeStruct((rows // 2, LANES), F32)
    last = high is None
    part = part if last else [in_hbm(p) for p in part]
    shape = lambda a: jax.ShapeDtypeStruct(a.shape, a.dtype)
    scratch = [
        pltpu.VMEM((2, specials, 2 * RADIX, LANES), F32),
        pltpu.VMEM((rows, LANES), F32),
        pltpu.VMEM((2, 2, RADIX, RADIX), BF16),
        pltpu.SemaphoreType.DMA((8,)),
    ]
    if last:
        scratch = [pltpu.VMEM((2, rows, LANES), F32)] + scratch + [pltpu.SMEM(end[1].shape, jnp.int32)]
    tables = (order, in_hbm(digit), where, scale, in_hbm(conv), comp)
    scratch += [pltpu.SMEM(a.shape, a.dtype) for a in tables] + [pltpu.SemaphoreType.DMA((len(tables) + 2,))]
    return pl.pallas_call(
        functools.partial(lower_kernel, low, high, guess, specials, limbs),
        in_specs=[ANY] * 6 + [HBM, VMEM, ANY, ANY, HBM, HBM] + ([SMEM, ANY] + [VMEM] * 4 if last else []),
        out_specs=[HBM, HBM] + [VMEM] * 4 if last else [VMEM, VMEM, HBM, HBM],
        out_shape=[shape(s) for s in store] + [half] * 4 if last else [shape(p) for p in (*part, *store)],
        input_output_aliases={10: 0, 11: 1} if last else {10: 2, 11: 3},
        scratch_shapes=scratch,
        compiler_params=params(12),
        cost_estimate=pl.CostEstimate(flops=10**9, bytes_accessed=8 * 2**20, transcendentals=0),
        name="lower",
    )(*tables, in_hbm(diag), mats, *part, *store, *end)


def interleave(x):
    *lead, limbs, coeffs = x.shape
    x = x.reshape(*lead, limbs, coeffs // LANES, LANES)
    return jnp.swapaxes(x, -3, -2).reshape(*lead, coeffs // LANES * limbs, LANES)


def per_device(order_of, cipher, rotation_keys, diagonals, shifts, twiddles, moduli, digit_of, conversion):
    n = len(order_of)
    limbs = cipher.shape[0]
    ext = digit_of.shape[0]
    specials = ext // (DIGITS + 1)
    count = rotation_keys.shape[1]
    items = count * specials
    pos_of = np.argsort(np.array(order_of)).astype(np.int32)
    cw = [(order_of[i], order_of[(i + 1) % n]) for i in range(n)]
    ccw = [(b, a) for a, b in cw]
    me, rot = lax.axis_index("limb"), lax.axis_index("rot")
    where = jnp.stack([me, rot]).astype(jnp.int32)
    pos = jnp.asarray(pos_of)
    my_pos = pos[me]
    swap = lambda x: lax.ppermute(x, "rot", [(0, 1), (1, 0)])

    grid = np.arange(RADIX)
    angle = (grid[:, None] * grid[None, :] % RADIX) * (2.0 * math.pi / RADIX)
    base = ((np.cos(angle) + np.sin(angle)) / math.sqrt(RADIX)).astype(np.float32)
    base_hi = base.astype(BF16)
    base_lo = (base - base_hi.astype(np.float32)).astype(BF16)

    rows_c = interleave(cipher)
    keys = interleave(rotation_keys).reshape(count, DIGITS * 2, -1, LANES)
    diag = interleave(diagonals).reshape(count, -1, LANES)

    cut = limbs // 2
    given = (limbs, twiddles, where, jnp.asarray(base_hi), jnp.asarray(base_lo), rows_c)
    coef, mats = [None, None], None
    coef[0], mats = coef_call(0, cut, *given)
    coef[1], mats = coef_call(cut, limbs, *given, (mats,))

    ids = jnp.arange(ext, dtype=jnp.int32)
    before = (digit_of[None, :] < digit_of[:, None]) | (
        (digit_of[None, :] == digit_of[:, None]) & (ids[None, :] < ids[:, None])
    )
    place = jnp.sum(before.astype(jnp.int32), axis=1)
    order = jnp.sum(jnp.where(place[None, :] == ids[:, None], ids[None, :], 0), axis=1)
    slot = lax.dynamic_slice_in_dim(jnp.maximum(place - DIGITS * specials, -1), me * limbs, limbs, 0)
    special = digit_of == DIGITS
    mod = moduli.astype(F32)
    scale = jnp.sum(jnp.where(special[None, :], mod[:, None] / mod[None, :], 0.0), axis=1) / specials
    my_special = lax.dynamic_slice_in_dim(special, me * limbs, limbs, 0)
    my_gain = jnp.where(my_special, 1.0, lax.dynamic_slice_in_dim(scale, me * limbs, limbs, 0))
    rows8 = lambda v: jnp.broadcast_to(jnp.tile(v, 8 // limbs)[:, None], (8, LANES))
    gain = rows8(my_gain)
    fixed = items * n // (2 * n)
    plan, rounds, comp = table_call(n, count, specials, limbs, fixed, order, pos, my_pos.reshape(1))

    spans = [(0, cut), (cut, limbs)]
    blocks, lens, steps = list(coef), list(spans), [0, 0]
    right, left = list(coef), list(coef)
    hop = lambda x, ring: lax.ppermute(x, "limb", ring)
    both = (n - 1) // 2
    for r in range(1, both + 1):
        for i in range(2):
            right[i] = hop(right[i], cw)
            left[i] = hop(left[i], ccw)
        blocks += right + left
        lens += spans * 2
        steps += [-r, -r, r, r]
    if n % 2 == 0:
        right[0] = hop(right[0], cw)
        left[1] = hop(left[1], ccw)
        blocks += [right[0], left[1]]
        lens += spans
        steps += [n // 2, n // 2]
    blocks[-1], order, slot, gain, scale, plan, rounds, comp = lax.optimization_barrier(
        (blocks[-1], order, slot, gain, scale, plan, rounds, comp)
    )
    srcs = jnp.asarray(
        np.array([[order_of[(pos_of[d] + s) % n] for s in steps] for d in range(n)], np.int32)
    )[me]

    pad = 64
    mixed = mix_call(n, limbs, tuple(lens), order, digit_of, where, srcs, conversion, blocks)
    raised = raise_call(digit_of, where, mixed, swap(mixed), mats, rows_c, pad)

    def accumulate(k, after=None):
        return accum_call(k, tie(shifts, after), raised, keys, diag, gain, limbs, pad, part)

    def lower(low, high, guess, end=()):
        return lower_call(
            low, high, guess, order, digit_of, where, scale, conversion, comp, diag, mats, specials, part, stores, end
        )

    def tie(x, after):
        return x if after is None else lax.optimization_barrier((x, after))[0]

    def travel(sends):
        return [lax.ppermute(sends[0], "limb", cw), lax.ppermute(sends[1], "limb", ccw)]

    tasks = {max(2 * k - 3, 0): k for k in range(1, count)}, {max(2 * k - 2, 0): k for k in range(1, count)}
    gates = {fixed - 5: 0, fixed - 3: 1, fixed - 1: 2}
    part, stores, ins, low = None, None, [None, None], -1
    *part, acc = accumulate(0)
    stores = list(emit_call(0, slot, acc, mats, specials, items, stores))
    for t in range(fixed):
        for c in range(2):
            stores[c], sends = pack_call(plan, t, stores[c], ins[c])
            ins[c] = travel(sends)
        if t in tasks[0]:
            *part, acc = accumulate(tasks[0][t], sends[0])
            stores[0], acc = lax.optimization_barrier((stores[0], acc))
        if t in tasks[1]:
            stores = list(emit_call(tasks[1][t], slot, tie(acc, sends[0]), mats, specials, items, stores))
        if t in gates:
            *part, stores[0], stores[1] = lower(low, t, min(gates[t], count - 1))
            low = t

    def more(state):
        return state[0] < rounds[0]

    def one(state):
        t, stores, ins = state
        stores, ins = list(stores), list(ins)
        for c in range(2):
            stores[c], sends = pack_call(plan, t, stores[c], ins[c])
            ins[c] = travel(sends)
        return t + 1, stores, ins

    t, stores, ins = lax.while_loop(more, one, (jnp.int32(fixed), stores, ins))
    _, _, *halves = lower(low, None, count - 1, (t.reshape(1), plan, *ins[0], *ins[1]))
    total = jnp.stack([keep + swap(send) for keep, send in zip(halves[:2], halves[2:])])
    total = jnp.swapaxes(total.reshape(2, -1, limbs, LANES), 1, 2)
    return total.reshape(2, limbs, -1)


def solution(mesh):
    in_specs = (
        P(("parts", "limb"), None),
        P("rot", None, None, None, "limb", None),
        P("rot", None, "limb", None),
        P("rot", None),
        P(),
        P(),
        P(),
        P(),
    )
    out_specs = P(None, ("parts", "limb"), "rot")

    def step(*args):
        return per_device(ring_order(mesh), *args)

    return jax.shard_map(step, mesh=mesh, in_specs=in_specs, out_specs=out_specs, check_vma=False)
```

```python
import functools
import math

import jax
import jax.numpy as jnp
import numpy as np
from jax import lax
from jax.experimental import pallas as pl
from jax.experimental.pallas import tpu as pltpu
from jax.sharding import PartitionSpec as P

RADIX = 256
DIGITS = 3
LANES = 128
PLAN = 4
F32 = jnp.float32
BF16 = jnp.bfloat16


ANY = pl.BlockSpec(memory_space=pl.ANY)
VMEM = pl.BlockSpec(memory_space=pltpu.VMEM)
HBM = pl.BlockSpec(memory_space=pltpu.HBM)
SMEM = pl.BlockSpec(memory_space=pltpu.SMEM)


def ring_order(mesh):
    n = mesh.shape["limb"]
    line = np.moveaxis(mesh.devices, list(mesh.axis_names).index("limb"), 0).reshape(n, -1)[:, 0]
    at = [getattr(d, "coords", None) for d in line]
    if any(c is None for c in at):
        return list(range(n))
    near = [
        [j for j in range(n) if sum(abs(x - y) for x, y in zip(at[i], at[j])) == 1] for i in range(n)
    ]

    def walk(path):
        if len(path) == n:
            return path if 0 in near[path[-1]] else None
        for j in near[path[-1]]:
            if j not in path:
                found = walk(path + [j])
                if found:
                    return found
        return None

    return walk([0]) or list(range(n))


def split(x):
    hi = x.astype(BF16)
    return hi, (x - hi.astype(F32)).astype(BF16)


def mm(a, b):
    dot = functools.partial(jnp.dot, preferred_element_type=F32)
    return dot(a[0], b[0]) + dot(a[1], b[0]) + dot(a[0], b[1])


def spin(x, h):
    return mm(h, split(mm(split(x), h)))


def grid_of(ref, m, limbs):
    left = ref[pl.ds(m, RADIX, stride=2 * limbs), :]
    right = ref[pl.ds(limbs + m, RADIX, stride=2 * limbs), :]
    return jnp.concatenate([left, right], axis=1)


def in_hbm(x):
    return pltpu.with_memory_space_constraint(x, pltpu.HBM)


def params(mib):
    return pltpu.CompilerParams(vmem_limit_bytes=mib * 2**20)


def coef_kernel(start, limbs, tw, where, base_hi, base_lo, cipher, *refs):
    coef, mats, grid, bases, sem = refs[-5:]
    copies = [
        pltpu.make_async_copy(base_hi, bases.at[0], sem.at[0]),
        pltpu.make_async_copy(base_lo, bases.at[1], sem.at[1]),
        pltpu.make_async_copy(cipher, grid, sem.at[2]),
    ]
    for copy in copies:
        copy.start()
    row = lax.broadcasted_iota(jnp.int32, (RADIX, RADIX), 0)
    col = lax.broadcasted_iota(jnp.int32, (RADIX, RADIX), 1)
    first = where[1] == 0
    if start:
        mats[:start] = refs[0][...]
    for copy in copies:
        copy.wait()
    for i in range(coef.shape[0]):
        m = start + i
        g = tw[where[0] * limbs + m]
        pick = jnp.where(((row * g) & (RADIX - 1)) == col, 1.0, 0.0).astype(BF16)
        hi = jnp.dot(pick, bases[0], preferred_element_type=F32).astype(BF16)
        lo = jnp.dot(pick, bases[1], preferred_element_type=F32).astype(BF16)
        mats[m, 0] = hi
        mats[m, 1] = lo
        u = split(mm((hi, lo), split(grid_of(grid, m, limbs))))
        half = tuple(
            jnp.where(first, h[:, :LANES].astype(F32), h[:, LANES:].astype(F32)).astype(BF16) for h in (hi, lo)
        )
        coef[i] = mm(u, half)


def coef_call(start, stop, limbs, tw, where, base_hi, base_lo, cipher, before=()):
    return pl.pallas_call(
        functools.partial(coef_kernel, start, limbs),
        in_specs=[SMEM, SMEM, HBM, HBM, HBM] + [VMEM] * len(before),
        out_specs=[VMEM, VMEM],
        out_shape=[
            jax.ShapeDtypeStruct((stop - start, RADIX, LANES), F32),
            jax.ShapeDtypeStruct((stop, 2, RADIX, RADIX), BF16),
        ],
        scratch_shapes=[
            pltpu.VMEM(cipher.shape, F32),
            pltpu.VMEM((2, RADIX, RADIX), BF16),
            pltpu.SemaphoreType.DMA((3,)),
        ],
        compiler_params=params(12),
        cost_estimate=pl.CostEstimate(flops=10**9, bytes_accessed=2**20, transcendentals=0),
        name="coef",
    )(in_hbm(tw), where, in_hbm(base_hi), in_hbm(base_lo), in_hbm(cipher), *before)


def mix_kernel(limbs, lens, order, digit, where, srcs, conv, *refs):
    blocks, out, got, table, sem = refs[: len(lens)], refs[-4], refs[-3], refs[-2], refs[-1]
    size = got.shape[0] * limbs // (DIGITS + 1)
    copies = []
    for i, (start, stop) in enumerate(lens):
        c = pltpu.make_async_copy(blocks[i], got.at[srcs[i], pl.ds(start, stop - start)], sem.at[i])
        c.start()
        copies.append(c)
    first = where[0] * limbs
    for j in range(DIGITS * size):
        l = order[j]
        for m in range(limbs):
            same = digit[l] == digit[first + m]
            one = jnp.where(first + m == l, 1.0, 0.0)
            table[m, j] = jnp.where(same, one, conv[first + m, l])
    for c in copies:
        c.wait()
    step = 64

    def rows(r, carry):
        r0 = pl.multiple_of(r * step, step)
        for d in range(DIGITS):
            acc = [jnp.zeros((step, LANES), F32) for _ in range(limbs)]
            for j in range(size):
                l = order[d * size + j]
                x = got[l // limbs, l % limbs, pl.ds(r0, step), :]
                for m in range(limbs):
                    acc[m] = acc[m] + table[m, d * size + j] * x
            for m in range(limbs):
                out[d, m, pl.ds(r0, step), :] = acc[m]
        return carry

    lax.fori_loop(0, RADIX // step, rows, 0)


def mix_call(n, limbs, lens, order, digit, where, srcs, conv, blocks):
    vmem = pl.BlockSpec(memory_space=pltpu.VMEM)
    return pl.pallas_call(
        functools.partial(mix_kernel, limbs, lens),
        in_specs=[SMEM] * 5 + [HBM] * len(blocks),
        out_specs=vmem,
        out_shape=jax.ShapeDtypeStruct((DIGITS, limbs, RADIX, LANES), F32),
        scratch_shapes=[
            pltpu.VMEM((n, limbs, RADIX, LANES), F32),
            pltpu.SMEM((limbs, n * limbs), F32),
            pltpu.SemaphoreType.DMA((len(blocks),)),
        ],
        compiler_params=params(16),
        name="mix",
    )(order, in_hbm(digit), where, srcs, in_hbm(conv), *blocks)


def raise_kernel(pad, digit, where, own, other, mats, cipher, out, rows_in, sem):
    limbs = mats.shape[0]
    rows = cipher.shape[0]
    swapped = where[1] != 0
    fetch = pltpu.make_async_copy(cipher, rows_in, sem)
    fetch.start()

    def at(m, h):
        return pl.ds(h * limbs + m, RADIX, stride=2 * limbs)

    def convert(m, carry):
        h = (mats[m, 0], mats[m, 1])
        for d in range(DIGITS):
            a, b = own[d, m], other[d, m]
            x = jnp.concatenate([jnp.where(swapped, b, a), jnp.where(swapped, a, b)], axis=1)
            y = spin(x, h)
            for i in range(2):
                out[d, at(m, i), :] = y[:, i * LANES : (i + 1) * LANES]
        return carry

    lax.fori_loop(0, limbs, convert, 0)
    fetch.wait()

    def place(m, carry):
        d = digit[where[0] * limbs + m]
        for h in range(2):
            out[d, at(m, h), :] = rows_in[at(m, h), :]

        @pl.when(d != DIGITS)
        def _():
            for h in range(2):
                out[DIGITS, at(m, h), :] = jnp.zeros((RADIX, LANES), F32)

        return carry

    lax.fori_loop(0, limbs, place, 0)
    for d in range(DIGITS + 1):
        out[d, pl.ds(rows, pad), :] = out[d, pl.ds(0, pad), :]


def raise_call(digit, where, own, other, mats, cipher, pad):
    rows = cipher.shape[0]
    return pl.pallas_call(
        functools.partial(raise_kernel, pad),
        in_specs=[SMEM, SMEM] + [VMEM] * 3 + [HBM],
        out_specs=VMEM,
        out_shape=jax.ShapeDtypeStruct((DIGITS + 1, rows + pad, LANES), F32),
        scratch_shapes=[pltpu.VMEM(cipher.shape, F32), pltpu.SemaphoreType.DMA],
        compiler_params=params(16),
        name="raise",
    )(in_hbm(digit), where, own, other, mats, in_hbm(cipher))


def accum_kernel(k, limbs, pad, shifts, raised, keys, diag, gain, *refs):
    part, acc, kbuf, dbuf, small, sem, ksem = refs[-8:-6], *refs[-6:]
    rows = acc.shape[1]
    pieces = ksem.shape[0]
    block = rows // pieces

    def fetch(i):
        at = pl.ds(pl.multiple_of(i * block, block), block)
        return [
            pltpu.make_async_copy(keys.at[k, :, at], kbuf.at[:, at], ksem.at[i, 0]),
            pltpu.make_async_copy(diag.at[k, at], dbuf.at[at], ksem.at[i, 1]),
        ]

    amounts = pltpu.make_async_copy(shifts, small, sem)
    amounts.start()
    for i in range(pieces):
        for copy in fetch(i):
            copy.start()
    amounts.wait()
    s = small[0, k]
    tiles, lane = s // LANES, s % LANES
    here = lax.broadcasted_iota(jnp.int32, (pad, LANES), 1) < LANES - lane
    g8 = jnp.concatenate([gain[...]] * (pad // 8), axis=0)

    def piece(i, carry):
        for copy in fetch(i):
            copy.wait()

        def add(r, carry):
            at = pl.multiple_of(i * block + r * pad, pad)
            u0 = lax.rem(at - limbs * tiles + rows, rows)
            v0 = lax.rem(at - limbs * tiles - limbs + 2 * rows, rows)
            turned = []
            for g in range(DIGITS + 1):
                u = raised[g, pl.ds(pl.multiple_of(u0, limbs), pad), :]
                v = raised[g, pl.ds(pl.multiple_of(v0, limbs), pad), :]
                turned.append(pltpu.roll(jnp.where(here, u, v), lane, axis=1))
            w = dbuf[pl.ds(at, pad), :] * g8
            for c in range(2):
                a = turned[DIGITS]
                for d in range(DIGITS):
                    a = a + turned[d] * kbuf[2 * d + c, pl.ds(at, pad), :]
                acc[c, pl.ds(at, pad), :] = a
                w_a = w * a
                part[c][pl.ds(at, pad), :] = w_a if k == 0 else refs[c][pl.ds(at, pad), :] + w_a
            return carry

        return lax.fori_loop(0, block // pad, add, carry, unroll=4)

    lax.fori_loop(0, pieces, piece, 0)


def accum_call(k, shifts, raised, keys, diag, gain, limbs, pad, part):
    rows = raised.shape[1] - pad
    args = (in_hbm(shifts), raised, in_hbm(keys), in_hbm(diag), gain)
    specs = [HBM, VMEM, HBM, HBM, VMEM]
    alias = {}
    if part is not None:
        alias = {len(args) + i: i for i in range(2)}
        args += tuple(part)
        specs += [VMEM, VMEM]
    one = jax.ShapeDtypeStruct((rows, LANES), F32)
    return pl.pallas_call(
        functools.partial(accum_kernel, k, limbs, pad),
        in_specs=specs,
        out_specs=[VMEM, VMEM, VMEM],
        out_shape=[one, one, jax.ShapeDtypeStruct((2, rows, LANES), F32)],
        input_output_aliases=alias,
        scratch_shapes=[
            pltpu.VMEM(keys.shape[1:], F32),
            pltpu.VMEM((rows, LANES), F32),
            pltpu.SMEM(shifts.shape, jnp.int32),
            pltpu.SemaphoreType.DMA,
            pltpu.SemaphoreType.DMA((8, 2)),
        ],
        compiler_params=params(12),
        cost_estimate=pl.CostEstimate(flops=10**8, bytes_accessed=8 * 2**20, transcendentals=0),
        name="accum",
    )(*args)


def emit_kernel(k, limbs, specials, slot, acc, mats, *refs):
    store, stage, sem = refs[-4:-2], refs[-2], refs[-1]

    def away(m, c):
        return pltpu.make_async_copy(stage.at[m, c], store[c].at[k * specials + slot[m]], sem.at[m, c])

    def emit(m, carry):
        @pl.when(slot[m] >= 0)
        def _():
            h = (mats[m, 0], mats[m, 1])
            for c in range(2):
                y = spin(grid_of(acc.at[c], m, limbs), h)
                stage[m, c, 0:RADIX, :] = y[:, :LANES]
                stage[m, c, RADIX:, :] = y[:, LANES:]
                away(m, c).start()

        return carry

    def finish(m, carry):
        @pl.when(slot[m] >= 0)
        def _():
            for c in range(2):
                away(m, c).wait()

        return carry

    lax.fori_loop(0, limbs, emit, 0)
    lax.fori_loop(0, limbs, finish, 0)


def emit_call(k, slot, acc, mats, specials, items, store):
    one = jax.ShapeDtypeStruct((items, 2 * RADIX, LANES), F32)
    args, specs, alias = (slot, acc, mats), [SMEM, VMEM, VMEM], {}
    if store is not None:
        alias = {len(args) + i: i for i in range(2)}
        args += tuple(map(in_hbm, store))
        specs += [HBM, HBM]
    return pl.pallas_call(
        functools.partial(emit_kernel, k, mats.shape[0], specials),
        in_specs=specs,
        out_specs=[HBM, HBM],
        out_shape=[one, one],
        input_output_aliases=alias,
        scratch_shapes=[
            pltpu.VMEM((mats.shape[0], 2, 2 * RADIX, LANES), F32),
            pltpu.SemaphoreType.DMA((mats.shape[0], 2)),
        ],
        compiler_params=params(8),
        cost_estimate=pl.CostEstimate(flops=10**9, bytes_accessed=2**20, transcendentals=0),
        name="emit",
    )(*args)


def table_kernel(n, count, specials, limbs, least, order, pos, spot, plan, rounds, comp, a_ref, b_ref, end_ref):
    items = count * specials
    shape = (items, LANES)
    row_i = lax.broadcasted_iota(jnp.int32, shape, 0)
    row = row_i.astype(F32)
    lane = lax.broadcasted_iota(jnp.int32, shape, 1).astype(F32)
    kind, turn = lax.rem(row_i, specials), lax.div(row_i, specials)
    ready = jnp.maximum(2 * turn - 1, 0)
    weight = 3.0 * turn.astype(F32)
    p = spot[0]
    before, after = lax.rem(p + n - 1, n), lax.rem(p + 1, n)
    line = lax.broadcasted_iota(jnp.int32, (1, LANES), 1)
    org = jnp.zeros(shape, F32)
    for s in range(specials):
        owner = pos[lax.div(order[DIGITS * specials + s], limbs)]
        org = jnp.where(kind == s, owner.astype(F32), org)
    a_ref[...] = jnp.zeros(shape, F32)
    b_ref[...] = jnp.zeros(shape, F32)
    end_ref[...] = jnp.zeros(shape, F32)
    big = float(items * (2 * n + 3 * count))

    def choose(front, spread, t):
        open_ = jnp.logical_and(spread < n - 1, ready <= t)
        cand = jnp.logical_and(open_, front == lane)
        key = jnp.where(cand, (2.0 * spread + weight) * items + row, big)
        best = jnp.min(key, axis=0, keepdims=True)
        hit = jnp.where(jnp.logical_and(cand, key == best), 1.0, 0.0)
        item = jnp.sum(hit * (row - items), axis=0, keepdims=True) + items
        return item, jnp.sum(hit, axis=1, keepdims=True)

    def note(t, r, item, where):
        t = jnp.asarray(t, jnp.int32)
        mine = jnp.sum(jnp.where(line == where, item, 0.0), axis=1, keepdims=True)
        at = pl.ds(lax.div(PLAN * t + r, LANES), 1)
        here = line == lax.rem(PLAN * t + r, LANES)
        plan[at, :] = jnp.where(here, jnp.broadcast_to(mine, (1, LANES)).astype(jnp.int32), plan[at, :])

    none = jnp.full((1, LANES), float(items), F32)
    plan[...] = jnp.full(plan.shape, items, jnp.int32)
    note(0, 2, none, p)
    note(0, 3, none, p)

    def step(t, carry):
        a, b = a_ref[...], b_ref[...]
        front = org + a
        item, right = choose(jnp.where(front >= n, front - n, front), a + b, t)
        note(t, 0, item, p)
        note(t + 1, 2, item, before)
        a = a + right
        front = org - b
        item, left = choose(jnp.where(front < 0, front + n, front), a + b, t)
        note(t, 1, item, p)
        note(t + 1, 3, item, after)
        b = b + left
        a_ref[...] = a
        b_ref[...] = b
        end_ref[...] = jnp.where(right + left > 0, (t + 1).astype(F32), end_ref[...])
        return carry

    def missing():
        return jnp.sum(n - 1 - a_ref[...] - b_ref[...]).astype(jnp.int32)

    def more(c):
        step(c[0], 0)
        return c[0] + 1, missing()

    lax.fori_loop(0, least, step, 0)
    t, _ = lax.while_loop(lambda c: c[1] > 0, more, (jnp.int32(least), missing()))
    rounds[0] = t
    note(t, 0, none, p)
    note(t, 1, none, p)
    for k in range(count):
        comp[k] = jnp.max(end_ref[pl.ds(k * specials, specials), :]).astype(jnp.int32)


def table_call(n, count, specials, limbs, least, order, pos, spot):
    items = count * specials
    most = items * (n - 1) + 2 * count
    return pl.pallas_call(
        functools.partial(table_kernel, n, count, specials, limbs, least),
        in_specs=[SMEM] * 3,
        out_specs=[pl.BlockSpec(memory_space=pltpu.VMEM), SMEM, SMEM],
        out_shape=[
            jax.ShapeDtypeStruct((-(-PLAN * (most + 1) // (8 * LANES)) * 8, LANES), jnp.int32),
            jax.ShapeDtypeStruct((1,), jnp.int32),
            jax.ShapeDtypeStruct((count,), jnp.int32),
        ],
        scratch_shapes=[pltpu.VMEM((items, LANES), F32)] * 3,
        compiler_params=params(8),
        name="table",
    )(order, in_hbm(pos), spot)


def round_of(tile, t):
    got = [tile[lax.div(f, LANES), lax.rem(f, LANES)] for f in (jnp.asarray(PLAN * t + r, jnp.int32) for r in range(PLAN))]
    return got[:2], got[2:]


def pack_kernel(items, t, first, last, *refs):
    refs = list(refs)
    if t is None:
        t = refs.pop(0)[0]
    table, store = refs.pop(0), refs.pop(0)
    ins = () if first else (refs.pop(0), refs.pop(0))
    refs.pop(0)
    outs = () if last else (refs.pop(0), refs.pop(0))
    tile, keep, send, tsem = refs
    plan = pltpu.make_async_copy(table, tile, tsem)
    plan.start()
    plan.wait()
    go, came = round_of(tile, t)
    for i in range(len(ins)):
        @pl.when(came[i] < items)
        def _():
            pltpu.make_async_copy(ins[i], store.at[came[i]], keep.at[i]).start()

    old = []
    for j in range(len(outs)):
        fresh = [jnp.logical_and(go[j] == came[i], came[i] < items) for i in range(len(ins))]
        held = go[j] < items
        for f in fresh:
            held = jnp.logical_and(held, jnp.logical_not(f))
        old.append(held)

        @pl.when(held)
        def _():
            pltpu.make_async_copy(store.at[go[j]], outs[j], send.at[j]).start()

        for i in range(len(ins)):
            @pl.when(fresh[i])
            def _():
                outs[j][...] = ins[i][...]

    for i in range(len(ins)):
        @pl.when(came[i] < items)
        def _():
            pltpu.make_async_copy(ins[i], store.at[came[i]], keep.at[i]).wait()
    for j in range(len(outs)):
        @pl.when(old[j])
        def _():
            pltpu.make_async_copy(store.at[go[j]], outs[j], send.at[j]).wait()


def pack_call(table, t, store, ins=None, last=False):
    first = ins is None
    store = in_hbm(store)
    items = store.shape[0]
    item = jax.ShapeDtypeStruct(store.shape[1:], store.dtype)
    static = isinstance(t, int)
    args = (() if static else (t.reshape(1),)) + (table, store) + (() if first else tuple(ins))
    at = 1 if static else 2
    outs = [jax.ShapeDtypeStruct(store.shape, store.dtype)] + ([] if last else [item, item])
    size = math.prod(item.shape) * 4
    res = pl.pallas_call(
        functools.partial(pack_kernel, items, t if static else None, first, last),
        in_specs=([] if static else [SMEM]) + [ANY, HBM] + [VMEM] * (0 if first else 2),
        out_specs=[HBM] + [VMEM] * (len(outs) - 1),
        out_shape=outs,
        input_output_aliases={at: 0},
        scratch_shapes=[
            pltpu.SMEM(table.shape, jnp.int32),
            pltpu.SemaphoreType.DMA((2,)),
            pltpu.SemaphoreType.DMA((2,)),
            pltpu.SemaphoreType.DMA,
        ],
        compiler_params=params(2),
        cost_estimate=pl.CostEstimate(flops=0, bytes_accessed=8 * size, transcendentals=0),
        name="pack",
    )(*args)
    return res[0], list(res[1:])


def lower_kernel(low, high, guess, specials, limbs, *refs):
    tables, (diag, mats, *refs) = refs[:6], refs[6:]
    small, smem, refs = refs[-7:-1], refs[-1], refs[:-7]
    part, store, refs = refs[:2], refs[2:4], refs[4:]
    last = high is None
    scalars = [pltpu.make_async_copy(a, b, smem.at[i]) for i, (a, b) in enumerate(zip(tables, small))]
    order, digit, where, scale, conv, comp = small

    def fetch(k):
        return [
            pltpu.make_async_copy(store[c].at[pl.ds(k * specials, specials)], got.at[c], sem.at[c]) for c in range(2)
        ] + [pltpu.make_async_copy(diag.at[k], dg, sem.at[2])]

    if last:
        t, plan, *refs = refs
        ins, store, keep, send, refs = (refs[0:2], refs[2:4]), refs[4:6], refs[6:8], refs[8:10], refs[10:]
        total, got, dg, xs, sem, tile = refs
        total = [total.at[0], total.at[1]]
        copy = pltpu.make_async_copy(plan, tile, sem.at[7])
        copy.start()
    else:
        total, (got, dg, xs, sem) = refs[:2], refs[4:]
    scalars += [pltpu.make_async_copy(part[c], total[c], smem.at[len(small) + c]) for c in range(2)]
    for copy in fetch(guess) + scalars:
        copy.start()
    for copy in scalars + fetch(guess):
        copy.wait()
    count = diag.shape[0]
    first = where[0] * limbs

    if last:
        pltpu.make_async_copy(plan, tile, sem.at[7]).wait()
        _, came = round_of(tile, t[0])

        def arrive(act):
            for c in range(2):
                for i in range(2):
                    @pl.when(came[i] < store[c].shape[0])
                    def _():
                        act(pltpu.make_async_copy(ins[c][i], store[c].at[came[i]], sem.at[3 + 2 * c + i]))

        arrive(lambda copy: copy.start())
        for i in range(2):
            place = came[i] - guess * specials

            @pl.when(jnp.logical_and(place >= 0, place < specials))
            def _():
                for c in range(2):
                    got[c, place] = ins[c][i][...]

    def turn(i, carry):
        if last:
            @pl.when(i == 1)
            def _():
                arrive(lambda copy: copy.wait())

        k = lax.rem(guess + i, count)
        ripe = comp[k] > low
        if not last:
            ripe = jnp.logical_and(ripe, comp[k] <= high)

        @pl.when(ripe)
        def _():
            @pl.when(i > 0)
            def _():
                for copy in fetch(k):
                    copy.start()
                for copy in fetch(k):
                    copy.wait()

            def limb(m, carry):
                q = first + m

                @pl.when(digit[q] != DIGITS)
                def _():
                    h = (mats[m, 0], mats[m, 1])
                    w = [conv[q, order[DIGITS * specials + s]] for s in range(specials)]
                    size = scale[q]
                    step = 64
                    for c in range(2):
                        for i in range(2):
                            for r in range(0, RADIX, step):
                                x = w[0] * got[c, 0, pl.ds(i * RADIX + r, step), :]
                                for s in range(1, specials):
                                    x = x + w[s] * got[c, s, pl.ds(i * RADIX + r, step), :]
                                hi, lo = split(x)
                                xs[c, 0, pl.ds(r, step), pl.ds(i * LANES, LANES)] = hi
                                xs[c, 1, pl.ds(r, step), pl.ds(i * LANES, LANES)] = lo
                    for c in range(2):
                        y = mm(h, split(mm((xs[c, 0], xs[c, 1]), h)))
                        for i in range(2):
                            at = pl.ds(i * limbs + m, RADIX, stride=2 * limbs)
                            total[c][at, :] = total[c][at, :] - dg[at, :] * size * y[:, i * LANES : (i + 1) * LANES]

                return carry

            lax.fori_loop(0, limbs, limb, 0)

        return carry

    lax.fori_loop(0, count, turn, 0)
    if last:
        half = total[0].shape[0] // 2
        mine = where[1]
        for c in range(2):
            keep[c][...] = total[c][pl.ds(pl.multiple_of(mine * half, half), half), :]
            send[c][...] = total[c][pl.ds(pl.multiple_of((1 - mine) * half, half), half), :]


def lower_call(low, high, guess, order, digit, where, scale, conv, comp, diag, mats, specials, part, store, end=()):
    limbs = mats.shape[0]
    store = [in_hbm(s) for s in store]
    rows = part[0].shape[0]
    half = jax.ShapeDtypeStruct((rows // 2, LANES), F32)
    last = high is None
    part = part if last else [in_hbm(p) for p in part]
    shape = lambda a: jax.ShapeDtypeStruct(a.shape, a.dtype)
    scratch = [
        pltpu.VMEM((2, specials, 2 * RADIX, LANES), F32),
        pltpu.VMEM((rows, LANES), F32),
        pltpu.VMEM((2, 2, RADIX, RADIX), BF16),
        pltpu.SemaphoreType.DMA((8,)),
    ]
    if last:
        scratch = [pltpu.VMEM((2, rows, LANES), F32)] + scratch + [pltpu.SMEM(end[1].shape, jnp.int32)]
    tables = (order, in_hbm(digit), where, scale, in_hbm(conv), comp)
    scratch += [pltpu.SMEM(a.shape, a.dtype) for a in tables] + [pltpu.SemaphoreType.DMA((len(tables) + 2,))]
    return pl.pallas_call(
        functools.partial(lower_kernel, low, high, guess, specials, limbs),
        in_specs=[ANY] * 6 + [HBM, VMEM, ANY, ANY, HBM, HBM] + ([SMEM, ANY] + [VMEM] * 4 if last else []),
        out_specs=[HBM, HBM] + [VMEM] * 4 if last else [VMEM, VMEM, HBM, HBM],
        out_shape=[shape(s) for s in store] + [half] * 4 if last else [shape(p) for p in (*part, *store)],
        input_output_aliases={10: 0, 11: 1} if last else {10: 2, 11: 3},
        scratch_shapes=scratch,
        compiler_params=params(12),
        cost_estimate=pl.CostEstimate(flops=10**9, bytes_accessed=8 * 2**20, transcendentals=0),
        name="lower",
    )(*tables, in_hbm(diag), mats, *part, *store, *end)


def interleave(x):
    *lead, limbs, coeffs = x.shape
    x = x.reshape(*lead, limbs, coeffs // LANES, LANES)
    return jnp.swapaxes(x, -3, -2).reshape(*lead, coeffs // LANES * limbs, LANES)


def per_device(order_of, cipher, rotation_keys, diagonals, shifts, twiddles, moduli, digit_of, conversion):
    n = len(order_of)
    limbs = cipher.shape[0]
    ext = digit_of.shape[0]
    specials = ext // (DIGITS + 1)
    count = rotation_keys.shape[1]
    items = count * specials
    pos_of = np.argsort(np.array(order_of)).astype(np.int32)
    cw = [(order_of[i], order_of[(i + 1) % n]) for i in range(n)]
    ccw = [(b, a) for a, b in cw]
    me, rot = lax.axis_index("limb"), lax.axis_index("rot")
    where = jnp.stack([me, rot]).astype(jnp.int32)
    pos = jnp.asarray(pos_of)
    my_pos = pos[me]
    swap = lambda x: lax.ppermute(x, "rot", [(0, 1), (1, 0)])

    grid = np.arange(RADIX)
    angle = (grid[:, None] * grid[None, :] % RADIX) * (2.0 * math.pi / RADIX)
    base = ((np.cos(angle) + np.sin(angle)) / math.sqrt(RADIX)).astype(np.float32)
    base_hi = base.astype(BF16)
    base_lo = (base - base_hi.astype(np.float32)).astype(BF16)

    rows_c = interleave(cipher)
    keys = interleave(rotation_keys).reshape(count, DIGITS * 2, -1, LANES)
    diag = interleave(diagonals).reshape(count, -1, LANES)

    cut = limbs // 2
    given = (limbs, twiddles, where, jnp.asarray(base_hi), jnp.asarray(base_lo), rows_c)
    coef, mats = [None, None], None
    coef[0], mats = coef_call(0, cut, *given)
    coef[1], mats = coef_call(cut, limbs, *given, (mats,))

    ids = jnp.arange(ext, dtype=jnp.int32)
    before = (digit_of[None, :] < digit_of[:, None]) | (
        (digit_of[None, :] == digit_of[:, None]) & (ids[None, :] < ids[:, None])
    )
    place = jnp.sum(before.astype(jnp.int32), axis=1)
    order = jnp.sum(jnp.where(place[None, :] == ids[:, None], ids[None, :], 0), axis=1)
    slot = lax.dynamic_slice_in_dim(jnp.maximum(place - DIGITS * specials, -1), me * limbs, limbs, 0)
    special = digit_of == DIGITS
    mod = moduli.astype(F32)
    scale = jnp.sum(jnp.where(special[None, :], mod[:, None] / mod[None, :], 0.0), axis=1) / specials
    my_special = lax.dynamic_slice_in_dim(special, me * limbs, limbs, 0)
    my_gain = jnp.where(my_special, 1.0, lax.dynamic_slice_in_dim(scale, me * limbs, limbs, 0))
    rows8 = lambda v: jnp.broadcast_to(jnp.tile(v, 8 // limbs)[:, None], (8, LANES))
    gain = rows8(my_gain)
    fixed = items * n // (2 * n)
    plan, rounds, comp = table_call(n, count, specials, limbs, fixed, order, pos, my_pos.reshape(1))

    spans = [(0, cut), (cut, limbs)]
    blocks, lens, steps = list(coef), list(spans), [0, 0]
    right, left = list(coef), list(coef)
    hop = lambda x, ring: lax.ppermute(x, "limb", ring)
    both = (n - 1) // 2
    for r in range(1, both + 1):
        for i in range(2):
            right[i] = hop(right[i], cw)
            left[i] = hop(left[i], ccw)
        blocks += right + left
        lens += spans * 2
        steps += [-r, -r, r, r]
        if r == 2:
            right[1], left[1], order, slot, gain, scale, plan, rounds, comp = lax.optimization_barrier(
                (right[1], left[1], order, slot, gain, scale, plan, rounds, comp)
            )
    if n % 2 == 0:
        blocks += [hop(right[0], cw), hop(left[1], ccw)]
        lens += spans
        steps += [n // 2, n // 2]
    srcs = jnp.asarray(
        np.array([[order_of[(pos_of[d] + s) % n] for s in steps] for d in range(n)], np.int32)
    )[me]

    pad = 64
    mixed = mix_call(n, limbs, tuple(lens), order, digit_of, where, srcs, conversion, blocks)
    raised = raise_call(digit_of, where, mixed, swap(mixed), mats, rows_c, pad)

    def accumulate(k, after=None):
        return accum_call(k, tie(shifts, after), raised, keys, diag, gain, limbs, pad, part)

    def lower(low, high, guess, end=()):
        return lower_call(
            low, high, guess, order, digit_of, where, scale, conversion, comp, diag, mats, specials, part, stores, end
        )

    def tie(x, after):
        return x if after is None else lax.optimization_barrier((x, after))[0]

    def travel(sends):
        return [lax.ppermute(sends[0], "limb", cw), lax.ppermute(sends[1], "limb", ccw)]

    tasks = {max(2 * k - 3, 0): k for k in range(1, count)}, {max(2 * k - 2, 0): k for k in range(1, count)}
    gates = {fixed - 5: 0, fixed - 3: 1, fixed - 1: 2}
    part, stores, ins, low = None, None, [None, None], -1
    *part, acc = accumulate(0)
    stores = list(emit_call(0, slot, acc, mats, specials, items, stores))
    for t in range(fixed):
        for c in range(2):
            stores[c], sends = pack_call(plan, t, stores[c], ins[c])
            ins[c] = travel(sends)
        if t in tasks[0]:
            *part, acc = accumulate(tasks[0][t], sends[0])
            stores[0], acc = lax.optimization_barrier((stores[0], acc))
        if t in tasks[1]:
            stores = list(emit_call(tasks[1][t], slot, tie(acc, sends[0]), mats, specials, items, stores))
        if t in gates:
            *part, stores[0], stores[1] = lower(low, t, min(gates[t], count - 1))
            low = t

    def more(state):
        return state[0] < rounds[0]

    def one(state):
        t, stores, ins = state
        stores, ins = list(stores), list(ins)
        for c in range(2):
            stores[c], sends = pack_call(plan, t, stores[c], ins[c])
            ins[c] = travel(sends)
        return t + 1, stores, ins

    t, stores, ins = lax.while_loop(more, one, (jnp.int32(fixed), stores, ins))
    _, _, *halves = lower(low, None, count - 1, (t.reshape(1), plan, *ins[0], *ins[1]))
    total = jnp.stack([keep + swap(send) for keep, send in zip(halves[:2], halves[2:])])
    total = jnp.swapaxes(total.reshape(2, -1, limbs, LANES), 1, 2)
    return total.reshape(2, limbs, -1)


def solution(mesh):
    in_specs = (
        P(("parts", "limb"), None),
        P("rot", None, None, None, "limb", None),
        P("rot", None, "limb", None),
        P("rot", None),
        P(),
        P(),
        P(),
        P(),
    )
    out_specs = P(None, ("parts", "limb"), "rot")

    def step(*args):
        return per_device(ring_order(mesh), *args)

    return jax.shard_map(step, mesh=mesh, in_specs=in_specs, out_specs=out_specs, check_vma=False)
```
